32 devices in a mesh: dp: 4 (over y, x), expert: 8 (over z, core).
Axes of the slice: x: 2, y: 2, z: 4, core: 2. Of those that a mesh axis runs over, the one named last changes fastest.
Arguments:
- tokens: bfloat16 [4096, 1536], P(('dp', 'expert')), may hold values from -6 to 6
- grad_out: bfloat16 [4096, 1536], P(('dp', 'expert')), may hold values from -6 to 6
- expert_ids: int32 [4096, 4], P(('dp', 'expert')), may hold values from 0 to 7, all different within a row; in each aligned block of 128 rows (0 to 127, 128 to 255, ...) at most 96 rows name the same one
- gate_q: int32 [4096, 4], P(('dp', 'expert')), may hold values from 1 to 65535
- w_up: bfloat16 [8, 1536, 768], P('expert', 'dp'), may hold values from -0.15625 to 0.15625
- w_down: bfloat16 [8, 768, 1536], P('expert', None, 'dp'), may hold values from -0.21875 to 0.21875
Outputs:
- dw_up: bfloat16 [8, 1536, 768], P('expert', 'dp')
- dw_down: bfloat16 [8, 768, 1536], P('expert', None, 'dp')
The draws below stay inside these ranges and needn't reach their ends.
Inputs may be any that keep to these rules, and one draw needn't show every extreme that they name: `expert_ids`: within the rows of one device no expert is named by more than 96 rows, a bound that some block reaches; the 4 ids of a row differ.
All inputs are finite; a program needn't handle non-finite values.
Results may differ from the reference program's by a relative error of at most 0.0064.
Values may be sent and summed in bfloat16 or wider, within the bound.
No kernel may reach another device: no remote copies, remote signals or barrier semaphores. Data moves between devices by JAX's collectives and lax.ppermute only.
A program may use at most 64 MiB of HBM per device.

```python
import math
import jax
import jax.numpy as jnp
import numpy as np
from jax import lax

D = 1536
FF = 768
TOP = 4
TOK_DEV = 128
EXPERTS = 8
CAP = 96
TOKENS = 4096
N_DP = 4


def touch_ends(result, own_key, low, high):
    longest = result.shape.index(max(result.shape))
    spots = []
    for shift in (0, 1):
        where = [jax.random.randint(jax.random.fold_in(own_key, axis), (), 0, length) for axis, length in enumerate(result.shape)]
        where[longest] = (where[longest] + shift) % result.shape[longest]
        spots.append(tuple(where))
    return result.at[spots[0]].set(low).at[spots[1]].set(high)


def levels(own_key, extent, cuts, smallest, top_value):
    level, own = 1.0, jax.random.fold_in(own_key, 6)
    for dim, shards_of in cuts:
        steps = jnp.exp(jax.random.uniform(jax.random.fold_in(own, dim), (shards_of,), jnp.float32, smallest / len(cuts), top_value / len(cuts)))
        level = level * jnp.repeat(steps, extent[dim] // shards_of).reshape([-1 if axis == dim else 1 for axis in range(len(extent))])
    return level


def deal_out(stream_key, own, number, rows, number_of, top, most, slope):
    ranking = jax.random.permutation(stream_key, number_of)
    packed, common = load_shares(number_of, rows * top, most, slope, True), load_shares(number_of, rows * top, most, slope, False)
    places = jnp.arange(number_of)

    def named(tallies, rotation):
        used = int((tallies > 0).sum())
        fixed = max(1, used // 4)
        passed = fixed + (places - fixed + rotation * (used - fixed)) % max(1, number_of - fixed)
        return jnp.zeros((number_of,), jnp.int32).at[ranking[jnp.where(places < fixed, places, passed)]].set(jnp.asarray(tallies, jnp.int32))

    tallies = jnp.where(number % 4 == 0, named(packed, number // 4), named(common, number - number // 4 - 1))
    mixed = jax.random.permutation(jax.random.fold_in(own, 3), number_of)
    source_of, receiver = mixed[0:number_of // 2 * 2:2], mixed[1:number_of // 2 * 2:2]
    room = jnp.minimum(tallies[source_of] - 1, most - tallies[receiver]) // 2
    room = jnp.where((source_of == ranking[0]) | (receiver == ranking[0]) | (tallies[receiver] == 0), 0, jnp.maximum(room, 0))
    passed = jax.random.randint(jax.random.fold_in(own, 4), (number_of // 2,), 0, 1 << 20) % (room + 1)
    tallies = tallies.at[source_of].add(-passed).at[receiver].add(passed)
    labels = jnp.searchsorted(jnp.cumsum(tallies), jnp.arange(rows * top), side="right").astype(jnp.int32)
    grid = labels.reshape(top, rows).T
    grid = grid[jax.random.permutation(jax.random.fold_in(own, 1), rows)]
    rotation = jax.random.randint(jax.random.fold_in(own, 2), (rows, 1), 0, top)
    return jnp.take_along_axis(grid, (jnp.arange(top)[None, :] + rotation) % top, axis=1)


def load_shares(number_of, total, limit, slope, full):
    loads = [(1 << 20) // math.isqrt(standing ** slope) + 1 for standing in range(1, number_of + 1)]
    largest = limit if full else min(limit, max(-(-total // number_of), total * loads[0] // sum(loads)))
    least = 1 if total - largest >= number_of - 1 else 0
    given, surplus = [largest] + [least] * (number_of - 1), total - largest - least * (number_of - 1)
    while surplus > 0:
        candidates = [i for i in range(1, number_of) if given[i] < largest] or [i for i in range(1, number_of) if given[i] < limit]
        whole, remaining = sum([loads[i] for i in candidates]), surplus
        for i in candidates:
            more = min(limit - given[i], max(1, remaining * loads[i] // whole), surplus)
            given[i] = given[i] + more
            surplus = surplus - more
    return np.array(given)


def normal_values(own_key, extent, spread, limit, cuts=(), held_as=jnp.bfloat16):
    gain = levels(own_key, extent, cuts, -0.22, 0.18) if cuts else 1.0
    array = jax.random.normal(own_key, extent, jnp.float32) * spread * gain
    return jnp.minimum(jnp.maximum(array, -limit), limit).astype(held_as)


def setup_inputs(seed: int = 0) -> dict:
    key_list = jax.random.split(jax.random.key(seed), 7)
    tokens = normal_values(key_list[0], (TOKENS, D), 1.0, 6.0, ((0, 32),))
    grad_out = normal_values(key_list[1], (TOKENS, D), 1.0, 6.0, ((0, 32),))
    expert_ids_keys = jax.random.split(jax.random.fold_in(key_list[2], 1), TOKENS // TOK_DEV)
    expert_ids_turns = jax.random.permutation(jax.random.fold_in(key_list[2], 3), TOKENS // TOK_DEV)
    expert_ids = jax.vmap(lambda own, number: deal_out(jax.random.fold_in(key_list[2], 2), own, number, TOK_DEV, EXPERTS, TOP, CAP, 2))(expert_ids_keys, expert_ids_turns).reshape((TOKENS, TOP))
    gate_q = touch_ends(jax.random.randint(key_list[3], (TOKENS, TOP), 1, 65536), jax.random.fold_in(key_list[3], 1), 1, 65535).astype(jnp.int32)
    w_up = normal_values(key_list[4], (EXPERTS, D, FF), D ** -0.5, 0.15625, ((0, 8), (1, 4)))
    w_down = normal_values(key_list[5], (EXPERTS, FF, D), FF ** -0.5, 0.21875, ((0, 8), (2, 4)))
    return {"tokens": tokens, "grad_out": grad_out, "expert_ids": expert_ids, "gate_q": gate_q, "w_up": w_up, "w_down": w_down}


def silu_slope(values):
    sigmoid_part = jax.nn.sigmoid(values)
    return sigmoid_part * (1.0 + values * (1.0 - sigmoid_part))


def reference(tokens, grad_out, expert_ids, gate_q, w_up, w_down):
    first_dims = (((0,), (0,)), ((), ()))
    slot_expert = expert_ids.reshape(-1).astype(jnp.int32)
    slot_total = slot_expert.shape[0]
    group_rows = tokens.shape[0] // N_DP
    slot_group = ((jnp.arange(slot_total, dtype=jnp.int32) // TOP) // group_rows).astype(jnp.int32)
    slot_key = (slot_expert * N_DP + slot_group).astype(jnp.int32)
    slot_order = jnp.argsort(slot_key, stable=True).astype(jnp.int32)
    key_counts = jnp.bincount(slot_key, length=EXPERTS * N_DP).astype(jnp.int32)
    key_starts = (jnp.cumsum(key_counts) - key_counts).astype(jnp.int32)
    gate_values = gate_q.reshape(-1).astype(jnp.float32) * (1.0 / 65536.0)
    block_size = 512

    def per_expert(carry, expert):
        up_matrix = w_up[expert]
        down_matrix = w_down[expert]
        up_total = jnp.zeros((D, FF), jnp.float32)
        down_total = jnp.zeros((FF, D), jnp.float32)
        for group in range(N_DP):
            key_index = expert * N_DP + group

            def block_step(step_index, parts):
                up_part, down_part = parts
                local = step_index * block_size + jnp.arange(block_size, dtype=jnp.int32)
                valid = local < key_counts[key_index]
                positions = jnp.clip(key_starts[key_index] + local, 0, slot_total - 1).astype(jnp.int32)
                slot_index = slot_order[positions]
                token_index = (slot_index // TOP).astype(jnp.int32)
                gate_row = jnp.where(valid, gate_values[slot_index], 0.0)
                token_rows = tokens[token_index]
                projected = jnp.dot(token_rows, up_matrix, preferred_element_type=jnp.float32)
                activated = jax.nn.silu(projected).astype(jnp.bfloat16)
                slot_grad = (gate_row[:, None] * grad_out[token_index].astype(jnp.float32)).astype(jnp.bfloat16)
                act_grad = jnp.dot(slot_grad, down_matrix.T, preferred_element_type=jnp.float32)
                projected_grad = (act_grad * silu_slope(projected)).astype(jnp.bfloat16)
                up_part = up_part + lax.dot_general(token_rows, projected_grad, first_dims, preferred_element_type=jnp.float32)
                down_part = down_part + lax.dot_general(activated, slot_grad, first_dims, preferred_element_type=jnp.float32)
                return up_part, down_part

            step_count = (key_counts[key_index] + block_size - 1) // block_size
            start_parts = (jnp.zeros((D, FF), jnp.float32), jnp.zeros((FF, D), jnp.float32))
            up_part, down_part = lax.fori_loop(0, step_count, block_step, start_parts)
            up_total = up_total + lax.optimization_barrier(up_part.astype(jnp.bfloat16)).astype(jnp.float32)
            down_total = down_total + lax.optimization_barrier(down_part.astype(jnp.bfloat16)).astype(jnp.float32)
        return carry, (up_total.astype(jnp.bfloat16), down_total.astype(jnp.bfloat16))

    _, (dw_up, dw_down) = lax.scan(per_expert, jnp.zeros((), jnp.float32), jnp.arange(EXPERTS, dtype=jnp.int32))
    return dw_up, dw_down
```

```python
import jax
import jax.numpy as jnp
from jax import lax
from jax.sharding import PartitionSpec as P

F32 = jnp.float32
BF16 = jnp.bfloat16
FIRST = (((0,), (0,)), ((), ()))
LAST = (((1,), (1,)), ((), ()))


def silu_slope(values):
    sigmoid_part = jax.nn.sigmoid(values)
    return sigmoid_part * (1.0 + values * (1.0 - sigmoid_part))


def summed_up(recv_rows, projected_grad):
    partial_value = lax.dot_general(recv_rows, projected_grad, FIRST, preferred_element_type=F32).astype(BF16)
    pieces = lax.all_to_all(partial_value[None], "dp", split_axis=1, concat_axis=0, tiled=True)
    return jnp.sum(pieces.astype(F32), axis=0, keepdims=True).astype(BF16)


def summed_down(activated, grad_rows):
    partial_value = lax.dot_general(activated, grad_rows, FIRST, preferred_element_type=F32).astype(BF16)
    pieces = lax.all_to_all(partial_value[None], "dp", split_axis=2, concat_axis=0, tiled=True)
    return jnp.sum(pieces.astype(F32), axis=0, keepdims=True).astype(BF16)


def sparse_shards(tokens, grad_out, expert_ids, gate_q, w_up, w_down, capacity):
    devices = lax.axis_size("expert")
    top_count = expert_ids.shape[1]
    model_width = tokens.shape[1]
    slot_expert = expert_ids.reshape(-1)
    onehot_table = (slot_expert[:, None] == jnp.arange(devices, dtype=jnp.int32)[None, :]).astype(jnp.int32)
    earlier = jnp.cumsum(onehot_table, axis=0) - onehot_table
    slot_rank = jnp.sum(earlier * onehot_table, axis=1)
    slot_target = slot_expert * capacity + slot_rank
    gate_values = gate_q.reshape(-1).astype(F32) * (1.0 / 65536.0)
    token_rows = jnp.repeat(tokens, top_count, axis=0)
    slot_grads = (gate_values[:, None] * jnp.repeat(grad_out, top_count, axis=0).astype(F32)).astype(BF16)
    empty_rows = jnp.zeros((devices * capacity, model_width), BF16)
    send_tokens = empty_rows.at[slot_target].set(token_rows).reshape(devices, capacity, model_width)
    grad_slots = empty_rows.at[slot_target].set(slot_grads).reshape(devices, capacity, model_width)
    up_whole = lax.all_gather(w_up, "dp", axis=1, tiled=True)[0]
    down_whole = lax.all_gather(w_down, "dp", axis=2, tiled=True)[0]
    recv_tokens = lax.all_to_all(send_tokens, "expert", split_axis=0, concat_axis=0, tiled=True)
    recv_rows = recv_tokens.reshape(-1, model_width)
    projected = jnp.dot(recv_rows, up_whole, preferred_element_type=F32)
    recv_grads = lax.all_to_all(grad_slots, "expert", split_axis=0, concat_axis=0, tiled=True)
    activated = jax.nn.silu(projected).astype(BF16)
    grad_rows = recv_grads.reshape(-1, model_width)
    act_grad = lax.dot_general(grad_rows, down_whole, LAST, preferred_element_type=F32)
    projected_grad = (act_grad * silu_slope(projected)).astype(BF16)
    return summed_up(recv_rows, projected_grad), summed_down(activated, grad_rows)


def xor_perm(count, bits):
    return [(i, i ^ bits) for i in range(count)]


def dense_shards(tokens, grad_out, expert_ids, gate_q, w_up, w_down):
    devices = lax.axis_size("expert")
    width = tokens.shape[1]
    w_up, w_down = w_up[0], w_down[0]
    block = w_up.shape[0]
    hidden = w_up.shape[1]
    dp_index = lax.axis_index("dp")
    ex_index = lax.axis_index("expert")
    experts = jnp.arange(devices, dtype=jnp.int32)
    named = expert_ids[:, :, None] == experts[None, None, :]
    gate_table = jnp.sum(jnp.where(named, gate_q[:, :, None], 0), axis=1)
    lanes = 128
    gates = jnp.concatenate([gate_table >> 8, gate_table & 255], axis=1).astype(BF16)
    gates = jnp.pad(gates, ((0, 0), (0, lanes - 2 * devices)))
    own = jnp.concatenate([tokens, grad_out, gates], axis=1)

    def ex(value, perm):
        return lax.ppermute(value, "expert", perm)

    def dp(value, bits):
        return lax.ppermute(value, "dp", xor_perm(4, bits))

    swap = xor_perm(devices, 1)
    up_ring = [(i, (i + 2) % devices) for i in range(devices)]
    down_ring = [(i, (i - 2) % devices) for i in range(devices)]
    up_mid = [(i, i + 2) for i in range(2, devices - 2)]
    down_mid = [(i, i - 2) for i in range(2, devices - 2)]
    slot1 = ex(own, up_ring)
    slot3 = ex(own, down_ring)
    up_x = dp(w_up, 1)
    down_y = dp(w_down, 2)
    up_y = dp(w_up, 2)
    down_x = dp(w_down, 1)
    up_d = dp(up_x, 2)
    down_d = dp(down_y, 1)
    own_b = ex(own, swap)
    slot2u = ex(slot1, up_mid)
    slot2d = ex(slot3, down_mid)
    slot1_b = ex(slot1, swap)
    slot3_b = ex(slot3, swap)
    slot2 = jnp.where(ex_index >= devices // 2, slot2u, slot2d)
    slot2_b = ex(slot2, swap)

    up_all = jnp.zeros((4 * block, hidden), BF16)
    down_all = jnp.zeros((hidden, 4 * block), BF16)
    for bits, up_part, down_part in ((0, w_up, w_down), (1, up_x, down_x), (2, up_y, down_y), (3, up_d, down_d)):
        where = (dp_index ^ bits) * block
        up_all = lax.dynamic_update_slice(up_all, up_part, (where, 0))
        down_all = lax.dynamic_update_slice(down_all, down_part, (0, where))

    def rows_of(payload):
        x = payload[:, :width]
        g = payload[:, width : 2 * width]
        pick = (experts == ex_index).astype(F32)
        high = jnp.sum(payload[:, 2 * width : 2 * width + devices].astype(F32) * pick, axis=1)
        low = jnp.sum(payload[:, 2 * width + devices : 2 * width + 2 * devices].astype(F32) * pick, axis=1)
        gate = (high * 256.0 + low) * (1.0 / 65536.0)
        g = (gate[:, None] * g.astype(F32)).astype(BF16)
        pre = jnp.dot(x, up_all, preferred_element_type=F32)
        act = jax.nn.silu(pre).astype(BF16)
        act_grad = lax.dot_general(g, down_all, LAST, preferred_element_type=F32)
        pre_grad = (act_grad * silu_slope(pre)).astype(BF16)
        return x, pre_grad, act, g

    groups = []
    for parts in ((own, own_b), (slot1, slot1_b, slot3, slot3_b), (slot2, slot2_b)):
        groups.append(rows_of(jnp.concatenate(parts, axis=0)))

    def up_block(bits):
        where = (dp_index ^ bits) * block
        total = None
        for x, pre_grad, act, g in groups:
            cols = lax.dynamic_slice(x, (0, where), (x.shape[0], block))
            part = lax.dot_general(cols, pre_grad, FIRST, preferred_element_type=F32)
            total = part if total is None else total + part
        return total

    def down_block(bits):
        where = (dp_index ^ bits) * block
        total = None
        for x, pre_grad, act, g in groups:
            cols = lax.dynamic_slice(g, (0, where), (g.shape[0], block))
            part = lax.dot_general(act, cols, FIRST, preferred_element_type=F32)
            total = part if total is None else total + part
        return total

    up_far = dp(up_block(3).astype(BF16), 2)
    down_far = dp(down_block(3).astype(BF16), 1)
    up_near = dp(up_block(2).astype(BF16), 2)
    down_near = dp(down_block(1).astype(BF16), 1)
    up_fwd = dp((up_block(1) + up_far.astype(F32)).astype(BF16), 1)
    down_fwd = dp((down_block(2) + down_far.astype(F32)).astype(BF16), 2)
    dw_up = (up_block(0) + up_near.astype(F32) + up_fwd.astype(F32)).astype(BF16)
    dw_down = (down_block(0) + down_near.astype(F32) + down_fwd.astype(F32)).astype(BF16)
    return dw_up[None], dw_down[None]


def shards(tokens, grad_out, expert_ids, gate_q, w_up, w_down):
    devices = lax.axis_size("expert")
    token_count, top_count = expert_ids.shape
    capacity = max(2, token_count * top_count * 3 // (2 * devices))
    if 2 * capacity >= token_count and devices == 8 and lax.axis_size("dp") == 4:
        return dense_shards(tokens, grad_out, expert_ids, gate_q, w_up, w_down)
    return sparse_shards(tokens, grad_out, expert_ids, gate_q, w_up, w_down, capacity)


def solution(mesh):
    in_specs = (
        P(("dp", "expert"), None),
        P(("dp", "expert"), None),
        P(("dp", "expert"), None),
        P(("dp", "expert"), None),
        P("expert", "dp", None),
        P("expert", None, "dp"),
    )
    out_specs = (P("expert", "dp", None), P("expert", None, "dp"))
    return jax.shard_map(shards, mesh=mesh, in_specs=in_specs, out_specs=out_specs, check_vma=False)
```

```python
import jax
import jax.numpy as jnp
from jax import lax
from jax.sharding import PartitionSpec as P


F32 = jnp.float32
BF16 = jnp.bfloat16
FIRST = (((0,), (0,)), ((), ()))
LAST = (((1,), (1,)), ((), ()))


def silu_slope(values):
    sigmoid_part = jax.nn.sigmoid(values)
    return sigmoid_part * (1.0 + values * (1.0 - sigmoid_part))


def summed_up(recv_rows, projected_grad):
    partial_value = lax.dot_general(recv_rows, projected_grad, FIRST, preferred_element_type=F32).astype(BF16)
    pieces = lax.all_to_all(partial_value[None], "dp", split_axis=1, concat_axis=0, tiled=True)
    return jnp.sum(pieces.astype(F32), axis=0, keepdims=True).astype(BF16)


def summed_down(activated, grad_rows):
    partial_value = lax.dot_general(activated, grad_rows, FIRST, preferred_element_type=F32).astype(BF16)
    pieces = lax.all_to_all(partial_value[None], "dp", split_axis=2, concat_axis=0, tiled=True)
    return jnp.sum(pieces.astype(F32), axis=0, keepdims=True).astype(BF16)


def sparse_shards(tokens, grad_out, expert_ids, gate_q, w_up, w_down, capacity):
    devices = lax.axis_size("expert")
    top_count = expert_ids.shape[1]
    model_width = tokens.shape[1]
    slot_expert = expert_ids.reshape(-1)
    onehot_table = (slot_expert[:, None] == jnp.arange(devices, dtype=jnp.int32)[None, :]).astype(jnp.int32)
    earlier = jnp.cumsum(onehot_table, axis=0) - onehot_table
    slot_rank = jnp.sum(earlier * onehot_table, axis=1)
    slot_target = slot_expert * capacity + slot_rank
    gate_values = gate_q.reshape(-1).astype(F32) * (1.0 / 65536.0)
    token_rows = jnp.repeat(tokens, top_count, axis=0)
    slot_grads = (gate_values[:, None] * jnp.repeat(grad_out, top_count, axis=0).astype(F32)).astype(BF16)
    empty_rows = jnp.zeros((devices * capacity, model_width), BF16)
    send_tokens = empty_rows.at[slot_target].set(token_rows).reshape(devices, capacity, model_width)
    grad_slots = empty_rows.at[slot_target].set(slot_grads).reshape(devices, capacity, model_width)
    up_whole = lax.all_gather(w_up, "dp", axis=1, tiled=True)[0]
    down_whole = lax.all_gather(w_down, "dp", axis=2, tiled=True)[0]
    recv_tokens = lax.all_to_all(send_tokens, "expert", split_axis=0, concat_axis=0, tiled=True)
    recv_rows = recv_tokens.reshape(-1, model_width)
    projected = jnp.dot(recv_rows, up_whole, preferred_element_type=F32)
    recv_grads = lax.all_to_all(grad_slots, "expert", split_axis=0, concat_axis=0, tiled=True)
    activated = jax.nn.silu(projected).astype(BF16)
    grad_rows = recv_grads.reshape(-1, model_width)
    act_grad = lax.dot_general(grad_rows, down_whole, LAST, preferred_element_type=F32)
    projected_grad = (act_grad * silu_slope(projected)).astype(BF16)
    return summed_up(recv_rows, projected_grad), summed_down(activated, grad_rows)


def xor_perm(count, bits):
    return [(i, i ^ bits) for i in range(count)]


def dense_shards(tokens, grad_out, expert_ids, gate_q, w_up, w_down):
    return dense_body(tokens, grad_out, expert_ids, gate_q, w_up[0], w_down[0])


def dense_body(tokens, grad_out, expert_ids, gate_q, w_up, w_down):
    devices = lax.axis_size("expert")
    block, hidden = w_up.shape
    dp_index = lax.axis_index("dp")
    ex_index = lax.axis_index("expert")
    upper = ex_index >= devices // 2

    def ex(value, perm):
        return lax.ppermute(value, "expert", perm)

    def dp(value, bits):
        return lax.ppermute(value, "dp", xor_perm(4, bits))

    swap = xor_perm(devices, 1)

    def ring(hops):
        return [(i, (i + 2 * hops) % devices) for i in range(devices)]

    up_mid = [(i, i + 2) for i in range(2, devices - 2)]
    down_mid = [(i, i - 2) for i in range(2, devices - 2)]

    t1 = ex(tokens, ring(1))
    t3 = ex(tokens, ring(-1))
    up_x = dp(w_up, 1)
    down_y = dp(w_down, 2)
    g1 = ex(grad_out, ring(1))
    g3 = ex(grad_out, ring(-1))
    up_y = dp(w_up, 2)
    down_x = dp(w_down, 1)

    experts = jnp.arange(devices, dtype=jnp.int32)
    named = expert_ids[:, :, None] == experts[None, None, :]
    gate_table = jnp.sum(jnp.where(named, gate_q[:, :, None], 0), axis=1).astype(F32) * (1.0 / 65536.0)
    c0 = jnp.concatenate([gate_table, ex(gate_table, swap)], axis=0)
    c1 = ex(c0, ring(1))
    c2 = ex(c0, ring(2))
    c3 = ex(c0, ring(3))
    t0b = ex(tokens, swap)
    g0b = ex(grad_out, swap)

    up_d = dp(up_x, 2)
    down_d = dp(down_y, 1)
    t2u = ex(t1, up_mid)
    t2d = ex(t3, down_mid)
    t1b = ex(t1, swap)
    t3b = ex(t3, swap)
    g2u = ex(g1, up_mid)
    g2d = ex(g3, down_mid)
    g1b = ex(g1, swap)
    g3b = ex(g3, swap)

    up_all = jnp.zeros((4 * block, hidden), BF16)
    down_all = jnp.zeros((hidden, 4 * block), BF16)
    for bits, up_part, down_part in ((0, w_up, w_down), (1, up_x, down_x), (2, up_y, down_y), (3, up_d, down_d)):
        where = (dp_index ^ bits) * block
        up_all = lax.dynamic_update_slice(up_all, up_part, (where, 0))
        down_all = lax.dynamic_update_slice(down_all, down_part, (0, where))

    pick = (experts == ex_index).astype(F32)

    def gate_of(*tables):
        table = jnp.concatenate(tables, axis=0)
        return jnp.sum(table * pick, axis=1)

    def scaled(gate, g):
        return (gate[:, None] * g.astype(F32)).astype(BF16)

    def backward(pre, g):
        act_grad = lax.dot_general(g, down_all, LAST, preferred_element_type=F32)
        return (act_grad * silu_slope(pre)).astype(BF16)

    def outer(left, right):
        return lax.dot_general(left, right, FIRST, preferred_element_type=F32)

    x_a = jnp.concatenate([tokens, t0b], axis=0)
    x_b = jnp.concatenate([t1, t1b, t3, t3b], axis=0)
    pre_a = jnp.dot(x_a, up_all, preferred_element_type=F32)
    pre_b = jnp.dot(x_b, up_all, preferred_element_type=F32)
    act_a = jax.nn.silu(pre_a).astype(BF16)
    act_b = jax.nn.silu(pre_b).astype(BF16)
    gate_a = gate_of(c0)
    gate_b = gate_of(c1, c3)
    gate_c = gate_of(c2)
    g_a = scaled(gate_a, jnp.concatenate([grad_out, g0b], axis=0))
    g_b = scaled(gate_b, jnp.concatenate([g1, g1b, g3, g3b], axis=0))
    back_a = backward(pre_a, g_a)
    back_b = backward(pre_b, g_b)
    up_acc = outer(x_a, back_a) + outer(x_b, back_b)
    down_acc = outer(act_a, g_a) + outer(act_b, g_b)
    t2 = jnp.where(upper, t2u, t2d)
    t2b = ex(t2, swap)
    x_c = jnp.concatenate([t2, t2b], axis=0)
    pre_c = jnp.dot(x_c, up_all, preferred_element_type=F32)
    act_c = jax.nn.silu(pre_c).astype(BF16)
    up_acc, down_acc, act_c, pre_c, g2u, g2d = lax.optimization_barrier((up_acc, down_acc, act_c, pre_c, g2u, g2d))
    g2 = jnp.where(upper, g2u, g2d)
    g2b = ex(g2, swap)
    g_c = scaled(gate_c, jnp.concatenate([g2, g2b], axis=0))
    back_c = backward(pre_c, g_c)

    def up_block(bits):
        where = (dp_index ^ bits) * block
        cols = lax.dynamic_slice(x_c, (0, where), (x_c.shape[0], block))
        return outer(cols, back_c) + lax.dynamic_slice(up_acc, (where, 0), (block, hidden))

    def down_block(bits):
        where = (dp_index ^ bits) * block
        cols = lax.dynamic_slice(g_c, (0, where), (g_c.shape[0], block))
        return outer(act_c, cols) + lax.dynamic_slice(down_acc, (0, where), (hidden, block))

    up_far = dp(up_block(3).astype(BF16), 2)
    down_far = dp(down_block(3).astype(BF16), 1)
    up_near = dp(up_block(2).astype(BF16), 2)
    down_near = dp(down_block(1).astype(BF16), 1)
    up_side, down_side = up_block(1), down_block(2)
    up_own, down_own = up_block(0), down_block(0)
    up_side, down_side, up_own, down_own = lax.optimization_barrier((up_side, down_side, up_own, down_own))
    up_fwd = dp((up_side + up_far.astype(F32)).astype(BF16), 1)
    down_fwd = dp((down_side + down_far.astype(F32)).astype(BF16), 2)
    dw_up = (up_own + up_near.astype(F32) + up_fwd.astype(F32)).astype(BF16)
    dw_down = (down_own + down_near.astype(F32) + down_fwd.astype(F32)).astype(BF16)
    return dw_up[None], dw_down[None]


def shards(tokens, grad_out, expert_ids, gate_q, w_up, w_down):
    devices = lax.axis_size("expert")
    token_count, top_count = expert_ids.shape
    capacity = max(2, token_count * top_count * 3 // (2 * devices))
    if 2 * capacity >= token_count and devices == 8 and lax.axis_size("dp") == 4:
        return dense_shards(tokens, grad_out, expert_ids, gate_q, w_up, w_down)
    return sparse_shards(tokens, grad_out, expert_ids, gate_q, w_up, w_down, capacity)


def solution(mesh):
    in_specs = (
        P(("dp", "expert"), None),
        P(("dp", "expert"), None),
        P(("dp", "expert"), None),
        P(("dp", "expert"), None),
        P("expert", "dp", None),
        P("expert", None, "dp"),
    )
    out_specs = (P("expert", "dp", None), P("expert", None, "dp"))
    return jax.shard_map(shards, mesh=mesh, in_specs=in_specs, out_specs=out_specs, check_vma=False)
```

```python
import jax
import jax.numpy as jnp
from jax import lax
from jax.sharding import PartitionSpec as P


F32 = jnp.float32
BF16 = jnp.bfloat16
FIRST = (((0,), (0,)), ((), ()))
LAST = (((1,), (1,)), ((), ()))


def silu_slope(values):
    sigmoid_part = jax.nn.sigmoid(values)
    return sigmoid_part * (1.0 + values * (1.0 - sigmoid_part))


def summed_up(recv_rows, projected_grad):
    partial_value = lax.dot_general(recv_rows, projected_grad, FIRST, preferred_element_type=F32).astype(BF16)
    pieces = lax.all_to_all(partial_value[None], "dp", split_axis=1, concat_axis=0, tiled=True)
    return jnp.sum(pieces.astype(F32), axis=0, keepdims=True).astype(BF16)


def summed_down(activated, grad_rows):
    partial_value = lax.dot_general(activated, grad_rows, FIRST, preferred_element_type=F32).astype(BF16)
    pieces = lax.all_to_all(partial_value[None], "dp", split_axis=2, concat_axis=0, tiled=True)
    return jnp.sum(pieces.astype(F32), axis=0, keepdims=True).astype(BF16)


def sparse_shards(tokens, grad_out, expert_ids, gate_q, w_up, w_down, capacity):
    devices = lax.axis_size("expert")
    top_count = expert_ids.shape[1]
    model_width = tokens.shape[1]
    slot_expert = expert_ids.reshape(-1)
    onehot_table = (slot_expert[:, None] == jnp.arange(devices, dtype=jnp.int32)[None, :]).astype(jnp.int32)
    earlier = jnp.cumsum(onehot_table, axis=0) - onehot_table
    slot_rank = jnp.sum(earlier * onehot_table, axis=1)
    slot_target = slot_expert * capacity + slot_rank
    gate_values = gate_q.reshape(-1).astype(F32) * (1.0 / 65536.0)
    token_rows = jnp.repeat(tokens, top_count, axis=0)
    slot_grads = (gate_values[:, None] * jnp.repeat(grad_out, top_count, axis=0).astype(F32)).astype(BF16)
    empty_rows = jnp.zeros((devices * capacity, model_width), BF16)
    send_tokens = empty_rows.at[slot_target].set(token_rows).reshape(devices, capacity, model_width)
    grad_slots = empty_rows.at[slot_target].set(slot_grads).reshape(devices, capacity, model_width)
    up_whole = lax.all_gather(w_up, "dp", axis=1, tiled=True)[0]
    down_whole = lax.all_gather(w_down, "dp", axis=2, tiled=True)[0]
    recv_tokens = lax.all_to_all(send_tokens, "expert", split_axis=0, concat_axis=0, tiled=True)
    recv_rows = recv_tokens.reshape(-1, model_width)
    projected = jnp.dot(recv_rows, up_whole, preferred_element_type=F32)
    recv_grads = lax.all_to_all(grad_slots, "expert", split_axis=0, concat_axis=0, tiled=True)
    activated = jax.nn.silu(projected).astype(BF16)
    grad_rows = recv_grads.reshape(-1, model_width)
    act_grad = lax.dot_general(grad_rows, down_whole, LAST, preferred_element_type=F32)
    projected_grad = (act_grad * silu_slope(projected)).astype(BF16)
    return summed_up(recv_rows, projected_grad), summed_down(activated, grad_rows)


def xor_perm(count, bits):
    return [(i, i ^ bits) for i in range(count)]


def dense_shards(tokens, grad_out, expert_ids, gate_q, w_up, w_down):
    return dense_body(tokens, grad_out, expert_ids, gate_q, w_up[0], w_down[0])


def dense_body(tokens, grad_out, expert_ids, gate_q, w_up, w_down):
    devices = lax.axis_size("expert")
    block, _ = w_up.shape
    dp_index = lax.axis_index("dp")
    ex_index = lax.axis_index("expert")
    upper = ex_index >= devices // 2

    def ex(value, perm):
        return lax.ppermute(value, "expert", perm)

    def dp(value, bits):
        return lax.ppermute(value, "dp", xor_perm(4, bits))

    swap = xor_perm(devices, 1)

    def ring(hops):
        return [(i, (i + 2 * hops) % devices) for i in range(devices)]

    up_mid = [(i, i + 2) for i in range(2, devices - 2)]
    down_mid = [(i, i - 2) for i in range(2, devices - 2)]

    t1 = ex(tokens, ring(1))
    t3 = ex(tokens, ring(-1))
    up_x = dp(w_up, 1)
    down_y = dp(w_down, 2)
    g1 = ex(grad_out, ring(1))
    g3 = ex(grad_out, ring(-1))
    up_y = dp(w_up, 2)
    down_x = dp(w_down, 1)

    experts = jnp.arange(devices, dtype=jnp.int32)
    named = expert_ids[:, :, None] == experts[None, None, :]
    gate_table = jnp.sum(jnp.where(named, gate_q[:, :, None], 0), axis=1).astype(F32) * (1.0 / 65536.0)
    c0 = jnp.concatenate([gate_table, ex(gate_table, swap)], axis=0)
    c1 = ex(c0, ring(1))
    c2 = ex(c0, ring(2))
    c3 = ex(c0, ring(3))
    t0b = ex(tokens, swap)
    g0b = ex(grad_out, swap)

    up_d = dp(up_x, 2)
    down_d = dp(down_y, 1)
    t2u = ex(t1, up_mid)
    t2d = ex(t3, down_mid)
    t1b = ex(t1, swap)
    t3b = ex(t3, swap)
    g2u = ex(g1, up_mid)
    g2d = ex(g3, down_mid)
    g1b = ex(g1, swap)
    g3b = ex(g3, swap)

    pick = (experts == ex_index).astype(F32)
    ups = (w_up, up_x, up_y, up_d)
    downs = (w_down, down_x, down_y, down_d)

    def gate_of(*tables):
        table = jnp.concatenate(tables, axis=0)
        return jnp.sum(table * pick, axis=1)

    def scaled(gate, g):
        return (gate[:, None] * g.astype(F32)).astype(BF16)

    def columns(rows, bits):
        return lax.dynamic_slice(rows, (0, (dp_index ^ bits) * block), (rows.shape[0], block))

    def forward_part(x, bits, total):
        part = jnp.dot(columns(x, bits), ups[bits], preferred_element_type=F32)
        return part if total is None else total + part

    def backward_part(g, bits, total):
        part = lax.dot_general(columns(g, bits), downs[bits], LAST, preferred_element_type=F32)
        return part if total is None else total + part

    def outer(left, right):
        return lax.dot_general(left, right, FIRST, preferred_element_type=F32)

    x_ab = jnp.concatenate([tokens, t0b, t1, t1b, t3, t3b], axis=0)
    pre = None
    for bits in (0, 1, 2, 3):
        pre = forward_part(x_ab, bits, pre)
    g_ab = scaled(gate_of(c0, c1, c3), jnp.concatenate([grad_out, g0b, g1, g1b, g3, g3b], axis=0))
    act_grad = None
    for bits in (0, 1, 2, 3):
        act_grad = backward_part(g_ab, bits, act_grad)
    act_ab = jax.nn.silu(pre).astype(BF16)
    back_ab = (act_grad * silu_slope(pre)).astype(BF16)
    up_acc = [outer(columns(x_ab, bits), back_ab) for bits in range(4)]
    down_acc = [outer(act_ab, columns(g_ab, bits)) for bits in range(4)]
    t2 = jnp.where(upper, t2u, t2d)
    t2b = ex(t2, swap)
    x_c = jnp.concatenate([t2, t2b], axis=0)
    pre_c = None
    for bits in (0, 1, 2, 3):
        pre_c = forward_part(x_c, bits, pre_c)
    act_c = jax.nn.silu(pre_c).astype(BF16)
    slope_c = silu_slope(pre_c)
    gate_c = gate_of(c2)
    up_acc, down_acc, act_c, slope_c, gate_c, g2u, g2d = lax.optimization_barrier(
        (up_acc, down_acc, act_c, slope_c, gate_c, g2u, g2d)
    )
    g2 = jnp.where(upper, g2u, g2d)
    g2b = ex(g2, swap)
    g_c = scaled(gate_c, jnp.concatenate([g2, g2b], axis=0))
    act_grad_c = None
    for bits in (0, 1, 2, 3):
        act_grad_c = backward_part(g_c, bits, act_grad_c)
    back_c = (act_grad_c * slope_c).astype(BF16)

    def up_block(bits):
        return outer(columns(x_c, bits), back_c) + up_acc[bits]

    def down_block(bits):
        return outer(act_c, columns(g_c, bits)) + down_acc[bits]

    down_far = dp(down_block(3).astype(BF16), 1)
    up_far = dp(up_block(3).astype(BF16), 2)
    up_near = dp(up_block(2).astype(BF16), 2)
    down_near = dp(down_block(1).astype(BF16), 1)
    up_side, down_side = up_block(1), down_block(2)
    up_own, down_own = up_block(0), down_block(0)
    up_side, down_side, up_own, down_own = lax.optimization_barrier((up_side, down_side, up_own, down_own))
    up_fwd = dp((up_side + up_far.astype(F32)).astype(BF16), 1)
    down_fwd = dp((down_side + down_far.astype(F32)).astype(BF16), 2)
    dw_up = (up_own + up_near.astype(F32) + up_fwd.astype(F32)).astype(BF16)
    dw_down = (down_own + down_near.astype(F32) + down_fwd.astype(F32)).astype(BF16)
    return dw_up[None], dw_down[None]


def shards(tokens, grad_out, expert_ids, gate_q, w_up, w_down):
    devices = lax.axis_size("expert")
    token_count, top_count = expert_ids.shape
    capacity = max(2, token_count * top_count * 3 // (2 * devices))
    if 2 * capacity >= token_count and devices == 8 and lax.axis_size("dp") == 4:
        return dense_shards(tokens, grad_out, expert_ids, gate_q, w_up, w_down)
    return sparse_shards(tokens, grad_out, expert_ids, gate_q, w_up, w_down, capacity)


def solution(mesh):
    in_specs = (
        P(("dp", "expert"), None),
        P(("dp", "expert"), None),
        P(("dp", "expert"), None),
        P(("dp", "expert"), None),
        P("expert", "dp", None),
        P("expert", None, "dp"),
    )
    out_specs = (P("expert", "dp", None), P("expert", None, "dp"))
    return jax.shard_map(shards, mesh=mesh, in_specs=in_specs, out_specs=out_specs, check_vma=False)
```

```python
import functools

import jax
import jax.numpy as jnp
from jax import lax
from jax.experimental import pallas as pl
from jax.experimental.pallas import tpu as pltpu
from jax.sharding import PartitionSpec as P


F32 = jnp.float32
BF16 = jnp.bfloat16
FIRST = (((0,), (0,)), ((), ()))
LAST = (((1,), (1,)), ((), ()))


def silu_slope(values):
    sigmoid_part = jax.nn.sigmoid(values)
    return sigmoid_part * (1.0 + values * (1.0 - sigmoid_part))


def summed_up(recv_rows, projected_grad):
    partial_value = lax.dot_general(recv_rows, projected_grad, FIRST, preferred_element_type=F32).astype(BF16)
    pieces = lax.all_to_all(partial_value[None], "dp", split_axis=1, concat_axis=0, tiled=True)
    return jnp.sum(pieces.astype(F32), axis=0, keepdims=True).astype(BF16)


def summed_down(activated, grad_rows):
    partial_value = lax.dot_general(activated, grad_rows, FIRST, preferred_element_type=F32).astype(BF16)
    pieces = lax.all_to_all(partial_value[None], "dp", split_axis=2, concat_axis=0, tiled=True)
    return jnp.sum(pieces.astype(F32), axis=0, keepdims=True).astype(BF16)


def sparse_shards(tokens, grad_out, expert_ids, gate_q, w_up, w_down, capacity):
    devices = lax.axis_size("expert")
    top_count = expert_ids.shape[1]
    model_width = tokens.shape[1]
    slot_expert = expert_ids.reshape(-1)
    onehot_table = (slot_expert[:, None] == jnp.arange(devices, dtype=jnp.int32)[None, :]).astype(jnp.int32)
    earlier = jnp.cumsum(onehot_table, axis=0) - onehot_table
    slot_rank = jnp.sum(earlier * onehot_table, axis=1)
    slot_target = slot_expert * capacity + slot_rank
    gate_values = gate_q.reshape(-1).astype(F32) * (1.0 / 65536.0)
    token_rows = jnp.repeat(tokens, top_count, axis=0)
    slot_grads = (gate_values[:, None] * jnp.repeat(grad_out, top_count, axis=0).astype(F32)).astype(BF16)
    empty_rows = jnp.zeros((devices * capacity, model_width), BF16)
    send_tokens = empty_rows.at[slot_target].set(token_rows).reshape(devices, capacity, model_width)
    grad_slots = empty_rows.at[slot_target].set(slot_grads).reshape(devices, capacity, model_width)
    up_whole = lax.all_gather(w_up, "dp", axis=1, tiled=True)[0]
    down_whole = lax.all_gather(w_down, "dp", axis=2, tiled=True)[0]
    recv_tokens = lax.all_to_all(send_tokens, "expert", split_axis=0, concat_axis=0, tiled=True)
    recv_rows = recv_tokens.reshape(-1, model_width)
    projected = jnp.dot(recv_rows, up_whole, preferred_element_type=F32)
    recv_grads = lax.all_to_all(grad_slots, "expert", split_axis=0, concat_axis=0, tiled=True)
    activated = jax.nn.silu(projected).astype(BF16)
    grad_rows = recv_grads.reshape(-1, model_width)
    act_grad = lax.dot_general(grad_rows, down_whole, LAST, preferred_element_type=F32)
    projected_grad = (act_grad * silu_slope(projected)).astype(BF16)
    return summed_up(recv_rows, projected_grad), summed_down(activated, grad_rows)


def xor_perm(count, bits):
    return [(i, i ^ bits) for i in range(count)]


MIB = 1 << 20


def pick_gate(table_ref, part, expert):
    table = table_ref[:, part * SHARD : (part + 1) * SHARD]
    mine = lax.broadcasted_iota(jnp.int32, table.shape, 0) == expert
    row = jnp.sum(jnp.where(mine, table, 0.0), axis=0, keepdims=True)
    return jnp.transpose(jnp.broadcast_to(row, (SHARD, SHARD)))


SHARD = 128


def scale_rows(gate, rows):
    wide = jnp.concatenate([gate] * (rows.shape[1] // gate.shape[1]), axis=1)
    return (wide * rows.astype(F32)).astype(BF16)


def dot_rows(left, right):
    return jnp.dot(left, right, preferred_element_type=F32)


def dot_last(left, right):
    return lax.dot_general(left, right, LAST, preferred_element_type=F32)


def dot_first(left, right):
    return lax.dot_general(left, right, FIRST, preferred_element_type=F32)


def most_kernel(block, *refs):
    count = 6
    xs, gs, tables = refs[0:count], refs[count : 2 * count], refs[12:15]
    ups, downs = refs[15:19], refs[19:23]
    up_out, down_out = refs[23:27], refs[27:31]
    x, g, up, down, act, back, up_stage, down_stage, x_sem, g_sem, w_sem, o_sem = refs[31:]
    me = lax.axis_index("dp")
    expert = lax.axis_index("expert")
    x_copies, g_copies, w_copies = [], [], []
    for i in range(4):
        w_copies.append(pltpu.make_async_copy(ups[i], up.at[pl.ds(i * block, block), :], w_sem.at[i]))
    for i in range(4):
        w_copies.append(pltpu.make_async_copy(downs[i], down.at[:, pl.ds(i * block, block)], w_sem.at[4 + i]))
    for i in range(count):
        for bits in range(4):
            where = pl.multiple_of((me ^ bits) * block, block)
            rows, cols = pl.ds(i * SHARD, SHARD), pl.ds(bits * block, block)
            x_copies.append(pltpu.make_async_copy(xs[i].at[:, pl.ds(where, block)], x.at[rows, cols], x_sem.at[i, bits]))
            g_copies.append(pltpu.make_async_copy(gs[i].at[:, pl.ds(where, block)], g.at[rows, cols], g_sem.at[i, bits]))
    for c in x_copies[:8] + w_copies[:4] + g_copies[:8] + w_copies[4:]:
        c.start()
    for c in x_copies[8:] + g_copies[8:]:
        c.start()
    for c in w_copies[:4]:
        c.wait()
    for pair in range(count // 2):
        rows = slice(pair * 2 * SHARD, (pair + 1) * 2 * SHARD)
        for c in x_copies[pair * 8 : pair * 8 + 8]:
            c.wait()
        pre = dot_rows(x[rows, :], up[...])
        sig = jax.nn.sigmoid(pre)
        act[rows, :] = (pre * sig).astype(BF16)
        slope = sig * (1.0 + pre * (1.0 - sig))
        for c in g_copies[pair * 8 : pair * 8 + 8]:
            c.wait()
        for half in range(2):
            own = slice((pair * 2 + half) * SHARD, (pair * 2 + half + 1) * SHARD)
            g[own, :] = scale_rows(pick_gate(tables[pair], half, expert), g[own, :])
        if pair == 0:
            for c in w_copies[4:]:
                c.wait()
        back[rows, :] = (dot_last(g[rows, :], down[...]) * slope).astype(BF16)
    outs = []
    for n, bits in enumerate((3, 2, 1, 0)):
        slot = n % 2
        if n >= 2:
            outs[2 * (n - 2)].wait()
            outs[2 * (n - 2) + 1].wait()
        cols = slice(bits * block, (bits + 1) * block)
        up_stage[slot] = dot_first(x[:, cols], back[...])
        outs.append(pltpu.make_async_copy(up_stage.at[slot], up_out[bits], o_sem.at[bits]))
        outs[-1].start()
        down_stage[slot] = dot_first(act[...], g[:, cols])
        outs.append(pltpu.make_async_copy(down_stage.at[slot], down_out[bits], o_sem.at[4 + bits]))
        outs[-1].start()
    for c in outs[4:]:
        c.wait()


def last_forward_kernel(block, *refs):
    shards, ups = refs[0:4], refs[4:8]
    x_out, act_out, slope_out = refs[8:11]
    parts, up, sems = refs[11:]
    me = lax.axis_index("dp")
    copies = []
    for i in range(4):
        for bits in range(4):
            where = pl.multiple_of((me ^ bits) * block, block)
            copies.append(
                pltpu.make_async_copy(
                    shards[i].at[:, pl.ds(where, block)], parts.at[i, :, pl.ds(bits * block, block)], sems.at[i, bits]
                )
            )
    for i in range(4):
        copies.append(pltpu.make_async_copy(ups[i], up.at[pl.ds(i * block, block), :], sems.at[4, i]))
    for c in copies:
        c.start()
    for c in copies:
        c.wait()
    x_out[:SHARD, :] = parts[0] + parts[1]
    x_out[SHARD:, :] = parts[2] + parts[3]
    pre = dot_rows(x_out[...], up[...])
    sig = jax.nn.sigmoid(pre)
    act_out[...] = (pre * sig).astype(BF16)
    slope_out[...] = sig * (1.0 + pre * (1.0 - sig))


def last_backward_kernel(block, *refs):
    shards, downs = refs[0:4], refs[4:8]
    table, x_ref, act, slope, up_acc, down_acc = refs[8:14]
    up_far, down_far, back, g = refs[14:18]
    parts, down, up_part, down_part, x_part, sems = refs[18:]
    me = lax.axis_index("dp")
    expert = lax.axis_index("expert")
    copies = []
    for i in range(4):
        for bits in range(4):
            where = pl.multiple_of((me ^ bits) * block, block)
            copies.append(
                pltpu.make_async_copy(
                    shards[i].at[:, pl.ds(where, block)], parts.at[i, :, pl.ds(bits * block, block)], sems.at[i, bits]
                )
            )
    down_copy = pltpu.make_async_copy(down_acc, down_part, sems.at[5, 0])
    up_copy = pltpu.make_async_copy(up_acc, up_part, sems.at[5, 1])
    x_copy = pltpu.make_async_copy(x_ref.at[:, pl.ds(3 * block, block)], x_part, sems.at[5, 2])
    w_copies = []
    for i in range(4):
        w_copies.append(pltpu.make_async_copy(downs[i], down.at[:, pl.ds(i * block, block)], sems.at[4, i]))
    for c in copies + [down_copy] + w_copies + [x_copy, up_copy]:
        c.start()
    for c in copies:
        c.wait()
    for half in range(2):
        own = slice(half * SHARD, (half + 1) * SHARD)
        g[own, :] = scale_rows(pick_gate(table, half, expert), parts[2 * half] + parts[2 * half + 1])
    down_copy.wait()
    far = slice(3 * block, 4 * block)
    down_far[...] = (dot_first(act[...], g[:, far]) + down_part[...]).astype(BF16)
    for c in w_copies:
        c.wait()
    back[...] = (dot_last(g[...], down[...]) * slope[...]).astype(BF16)
    x_copy.wait()
    up_copy.wait()
    up_far[...] = (dot_first(x_part[...], back[...]) + up_part[...]).astype(BF16)


ANY = pl.BlockSpec(memory_space=pl.ANY)
VMEM = pl.BlockSpec(memory_space=pltpu.VMEM)


def most_of(xs, gs, tables, ups, downs):
    block, hidden = ups[0].shape
    rows, width = 6 * SHARD, 4 * block
    out = [jax.ShapeDtypeStruct((block, hidden), F32)] * 4 + [jax.ShapeDtypeStruct((hidden, block), F32)] * 4
    got = pl.pallas_call(
        functools.partial(most_kernel, block),
        out_shape=out,
        in_specs=[ANY] * 12 + [VMEM] * 3 + [ANY] * 8,
        out_specs=[ANY] * 8,
        scratch_shapes=[
            pltpu.VMEM((rows, width), BF16),
            pltpu.VMEM((rows, width), BF16),
            pltpu.VMEM((width, hidden), BF16),
            pltpu.VMEM((hidden, width), BF16),
            pltpu.VMEM((rows, hidden), BF16),
            pltpu.VMEM((rows, hidden), BF16),
            pltpu.VMEM((2, block, hidden), F32),
            pltpu.VMEM((2, hidden, block), F32),
            pltpu.SemaphoreType.DMA((6, 4)),
            pltpu.SemaphoreType.DMA((6, 4)),
            pltpu.SemaphoreType.DMA((8,)),
            pltpu.SemaphoreType.DMA((8,)),
        ],
        compiler_params=pltpu.CompilerParams(vmem_limit_bytes=32 * MIB),
        cost_estimate=pl.CostEstimate(flops=8 * rows * width * hidden, bytes_accessed=20 * MIB, transcendentals=rows * hidden),
        name="most",
    )(*xs, *gs, *tables, *ups, *downs)
    return got[:4], got[4:]


def last_forward(shards, ups):
    block, hidden = ups[0].shape
    rows, width = 2 * SHARD, 4 * block
    return pl.pallas_call(
        functools.partial(last_forward_kernel, block),
        out_shape=[
            jax.ShapeDtypeStruct((rows, width), BF16),
            jax.ShapeDtypeStruct((rows, hidden), BF16),
            jax.ShapeDtypeStruct((rows, hidden), F32),
        ],
        in_specs=[ANY] * 8,
        out_specs=[VMEM] * 3,
        scratch_shapes=[
            pltpu.VMEM((4, SHARD, width), BF16),
            pltpu.VMEM((width, hidden), BF16),
            pltpu.SemaphoreType.DMA((5, 4)),
        ],
        compiler_params=pltpu.CompilerParams(vmem_limit_bytes=16 * MIB),
        cost_estimate=pl.CostEstimate(flops=2 * rows * width * hidden, bytes_accessed=5 * MIB, transcendentals=rows * hidden),
        name="last_forward",
    )(*shards, *ups)


def last_backward(shards, downs, table, x, act, slope, up_acc, down_acc):
    hidden, block = downs[0].shape
    rows, width = 2 * SHARD, 4 * block
    return pl.pallas_call(
        functools.partial(last_backward_kernel, block),
        out_shape=[
            jax.ShapeDtypeStruct((block, hidden), BF16),
            jax.ShapeDtypeStruct((hidden, block), BF16),
            jax.ShapeDtypeStruct((rows, hidden), BF16),
            jax.ShapeDtypeStruct((rows, width), BF16),
        ],
        in_specs=[ANY] * 8 + [VMEM, ANY, VMEM, VMEM, ANY, ANY],
        out_specs=[VMEM] * 4,
        scratch_shapes=[
            pltpu.VMEM((4, SHARD, width), BF16),
            pltpu.VMEM((hidden, width), BF16),
            pltpu.VMEM((block, hidden), F32),
            pltpu.VMEM((hidden, block), F32),
            pltpu.VMEM((rows, block), BF16),
            pltpu.SemaphoreType.DMA((6, 4)),
        ],
        compiler_params=pltpu.CompilerParams(vmem_limit_bytes=20 * MIB),
        cost_estimate=pl.CostEstimate(flops=4 * rows * width * hidden, bytes_accessed=8 * MIB, transcendentals=0),
        name="last_backward",
    )(*shards, *downs, table, x, act, slope, up_acc, down_acc)


def dense_shards(tokens, grad_out, expert_ids, gate_q, w_up, w_down):
    return dense_body(tokens, grad_out, expert_ids, gate_q, w_up[0], w_down[0])


def dense_body(tokens, grad_out, expert_ids, gate_q, w_up, w_down):
    devices = lax.axis_size("expert")
    block, _ = w_up.shape

    def ex(value, perm):
        return lax.ppermute(value, "expert", perm)

    def dp(value, bits):
        return lax.ppermute(value, "dp", xor_perm(4, bits))

    swap = xor_perm(devices, 1)

    def ring(hops):
        return [(i, (i + 2 * hops) % devices) for i in range(devices)]

    up_mid = [(i, i + 2) for i in range(2, devices - 2)]
    down_mid = [(i, i - 2) for i in range(2, devices - 2)]

    t1 = ex(tokens, ring(1))
    t3 = ex(tokens, ring(-1))
    up_x = dp(w_up, 1)
    down_y = dp(w_down, 2)
    g1 = ex(grad_out, ring(1))
    g3 = ex(grad_out, ring(-1))
    up_y = dp(w_up, 2)
    down_x = dp(w_down, 1)

    experts = jnp.arange(devices, dtype=jnp.int32)
    named = expert_ids.T[None, :, :] == experts[:, None, None]
    gate_table = jnp.sum(jnp.where(named, gate_q.T[None, :, :], 0), axis=1).astype(F32) * (1.0 / 65536.0)
    c0 = jnp.concatenate([gate_table, ex(gate_table, swap)], axis=1)
    c1 = ex(c0, ring(1))
    c2 = ex(c0, ring(2))
    c3 = ex(c0, ring(3))
    t0b = ex(tokens, swap)
    g0b = ex(grad_out, swap)

    up_d = dp(up_x, 2)
    down_d = dp(down_y, 1)
    t2u = ex(t1, up_mid)
    t2d = ex(t3, down_mid)
    t1b = ex(t1, swap)
    t3b = ex(t3, swap)
    g2u = ex(g1, up_mid)
    g2d = ex(g3, down_mid)
    g1b = ex(g1, swap)
    g3b = ex(g3, swap)
    t2ub = ex(t2u, swap)
    t2db = ex(t2d, swap)
    g2ub = ex(g2u, swap)
    g2db = ex(g2d, swap)

    ups = (w_up, up_x, up_y, up_d)
    downs = (w_down, down_x, down_y, down_d)
    up_acc, down_acc = most_of((tokens, t0b, t1, t1b, t3, t3b), (grad_out, g0b, g1, g1b, g3, g3b), (c0, c1, c3), ups, downs)
    x_c, act_c, slope_c = last_forward((t2u, t2d, t2ub, t2db), ups)
    up_first, down_first, back_c, g_c = last_backward(
        (g2u, g2d, g2ub, g2db), downs, c2, x_c, act_c, slope_c, up_acc[3], down_acc[3]
    )

    def columns(rows, bits):
        return rows[:, bits * block : (bits + 1) * block]

    def up_block(bits):
        return dot_first(columns(x_c, bits), back_c) + up_acc[bits]

    def down_block(bits):
        return dot_first(act_c, columns(g_c, bits)) + down_acc[bits]

    down_far = dp(down_first, 1)
    up_far = dp(up_first, 2)
    up_near = dp(up_block(2).astype(BF16), 2)
    down_near = dp(down_block(1).astype(BF16), 1)
    up_side, down_side = up_block(1), down_block(2)
    up_own, down_own = up_block(0), down_block(0)
    up_side, down_side, up_own, down_own = lax.optimization_barrier((up_side, down_side, up_own, down_own))
    up_fwd = dp((up_side + up_far.astype(F32)).astype(BF16), 1)
    down_fwd = dp((down_side + down_far.astype(F32)).astype(BF16), 2)
    dw_up = (up_own + up_near.astype(F32) + up_fwd.astype(F32)).astype(BF16)
    dw_down = (down_own + down_near.astype(F32) + down_fwd.astype(F32)).astype(BF16)
    return dw_up[None], dw_down[None]


def shards(tokens, grad_out, expert_ids, gate_q, w_up, w_down):
    devices = lax.axis_size("expert")
    token_count, top_count = expert_ids.shape
    capacity = max(2, token_count * top_count * 3 // (2 * devices))
    if 2 * capacity >= token_count and devices == 8 and lax.axis_size("dp") == 4 and token_count == SHARD:
        return dense_shards(tokens, grad_out, expert_ids, gate_q, w_up, w_down)
    return sparse_shards(tokens, grad_out, expert_ids, gate_q, w_up, w_down, capacity)


def solution(mesh):
    in_specs = (
        P(("dp", "expert"), None),
        P(("dp", "expert"), None),
        P(("dp", "expert"), None),
        P(("dp", "expert"), None),
        P("expert", "dp", None),
        P("expert", None, "dp"),
    )
    out_specs = (P("expert", "dp", None), P("expert", None, "dp"))
    return jax.shard_map(shards, mesh=mesh, in_specs=in_specs, out_specs=out_specs, check_vma=False)
```

```python
import functools

import jax
import jax.numpy as jnp
from jax import lax
from jax.experimental import pallas as pl
from jax.experimental.pallas import tpu as pltpu
from jax.sharding import PartitionSpec as P


F32 = jnp.float32
BF16 = jnp.bfloat16
FIRST = (((0,), (0,)), ((), ()))
LAST = (((1,), (1,)), ((), ()))


def silu_slope(values):
    sigmoid_part = jax.nn.sigmoid(values)
    return sigmoid_part * (1.0 + values * (1.0 - sigmoid_part))


def summed_up(recv_rows, projected_grad):
    partial_value = lax.dot_general(recv_rows, projected_grad, FIRST, preferred_element_type=F32).astype(BF16)
    pieces = lax.all_to_all(partial_value[None], "dp", split_axis=1, concat_axis=0, tiled=True)
    return jnp.sum(pieces.astype(F32), axis=0, keepdims=True).astype(BF16)


def summed_down(activated, grad_rows):
    partial_value = lax.dot_general(activated, grad_rows, FIRST, preferred_element_type=F32).astype(BF16)
    pieces = lax.all_to_all(partial_value[None], "dp", split_axis=2, concat_axis=0, tiled=True)
    return jnp.sum(pieces.astype(F32), axis=0, keepdims=True).astype(BF16)


def sparse_shards(tokens, grad_out, expert_ids, gate_q, w_up, w_down, capacity):
    devices = lax.axis_size("expert")
    top_count = expert_ids.shape[1]
    model_width = tokens.shape[1]
    slot_expert = expert_ids.reshape(-1)
    onehot_table = (slot_expert[:, None] == jnp.arange(devices, dtype=jnp.int32)[None, :]).astype(jnp.int32)
    earlier = jnp.cumsum(onehot_table, axis=0) - onehot_table
    slot_rank = jnp.sum(earlier * onehot_table, axis=1)
    slot_target = slot_expert * capacity + slot_rank
    gate_values = gate_q.reshape(-1).astype(F32) * (1.0 / 65536.0)
    token_rows = jnp.repeat(tokens, top_count, axis=0)
    slot_grads = (gate_values[:, None] * jnp.repeat(grad_out, top_count, axis=0).astype(F32)).astype(BF16)
    empty_rows = jnp.zeros((devices * capacity, model_width), BF16)
    send_tokens = empty_rows.at[slot_target].set(token_rows).reshape(devices, capacity, model_width)
    grad_slots = empty_rows.at[slot_target].set(slot_grads).reshape(devices, capacity, model_width)
    up_whole = lax.all_gather(w_up, "dp", axis=1, tiled=True)[0]
    down_whole = lax.all_gather(w_down, "dp", axis=2, tiled=True)[0]
    recv_tokens = lax.all_to_all(send_tokens, "expert", split_axis=0, concat_axis=0, tiled=True)
    recv_rows = recv_tokens.reshape(-1, model_width)
    projected = jnp.dot(recv_rows, up_whole, preferred_element_type=F32)
    recv_grads = lax.all_to_all(grad_slots, "expert", split_axis=0, concat_axis=0, tiled=True)
    activated = jax.nn.silu(projected).astype(BF16)
    grad_rows = recv_grads.reshape(-1, model_width)
    act_grad = lax.dot_general(grad_rows, down_whole, LAST, preferred_element_type=F32)
    projected_grad = (act_grad * silu_slope(projected)).astype(BF16)
    return summed_up(recv_rows, projected_grad), summed_down(activated, grad_rows)


def xor_perm(count, bits):
    return [(i, i ^ bits) for i in range(count)]


MIB = 1 << 20


def pick_gate(table_ref, part, expert):
    table = table_ref[:, part * SHARD : (part + 1) * SHARD]
    mine = lax.broadcasted_iota(jnp.int32, table.shape, 0) == expert
    row = jnp.sum(jnp.where(mine, table, 0.0), axis=0, keepdims=True)
    return jnp.transpose(jnp.broadcast_to(row, (SHARD, SHARD)))


SHARD = 128


def scale_rows(gate, rows):
    wide = jnp.concatenate([gate] * (rows.shape[1] // gate.shape[1]), axis=1)
    return (wide * rows.astype(F32)).astype(BF16)


def dot_rows(left, right):
    return jnp.dot(left, right, preferred_element_type=F32)


def dot_last(left, right):
    return lax.dot_general(left, right, LAST, preferred_element_type=F32)


def owner_columns(block, bits):
    return pl.ds(pl.multiple_of((lax.axis_index("dp") ^ bits) * block, block), block)


def early_forward_kernel(block, shards, *refs):
    xs, ups = refs[0:shards], refs[shards : shards + 3]
    x_last, x_turned, part = refs[shards + 3 : shards + 6]
    x = refs[shards + 6]
    for pair in range(shards // 2):
        rows = slice(pair * 2 * SHARD, (pair + 1) * 2 * SHARD)
        for half in range(2):
            for bits in range(4):
                x[half * SHARD : (half + 1) * SHARD, bits * block : (bits + 1) * block] = xs[pair * 2 + half][
                    :, owner_columns(block, bits)
                ]
        total = dot_rows(x[:, :block], ups[0][...])
        for bits in (1, 2):
            total = total + dot_rows(x[:, bits * block : (bits + 1) * block], ups[bits][...])
        part[rows, :] = total
        x_last[rows, :] = x[:, 3 * block :]
        x_turned[:, rows] = jnp.transpose(x[...])


def early_backward_kernel(block, shards, *refs):
    gs, tables, downs = refs[0:shards], refs[shards : shards + shards // 2], refs[shards + shards // 2 : shards + shards // 2 + 3]
    g, part = refs[shards + shards // 2 + 3 :]
    expert = lax.axis_index("expert")
    for pair in range(shards // 2):
        rows = slice(pair * 2 * SHARD, (pair + 1) * 2 * SHARD)
        for half in range(2):
            own = slice((pair * 2 + half) * SHARD, (pair * 2 + half + 1) * SHARD)
            gate = pick_gate(tables[pair], half, expert)
            for bits in range(4):
                g[own, bits * block : (bits + 1) * block] = scale_rows(gate, gs[pair * 2 + half][:, owner_columns(block, bits)])
        total = dot_last(g[rows, :block], downs[0][...])
        for bits in (1, 2):
            total = total + dot_last(g[rows, bits * block : (bits + 1) * block], downs[bits][...])
        part[rows, :] = total


def most_kernel(block, *refs):
    x_last, x_turned, g, pre_part, grad_part, up, down = refs[0:7]
    up_out, down_out = refs[7:11], refs[11:15]
    act_turned, back = refs[15:]
    for pair in range(g.shape[0] // (2 * SHARD)):
        rows = slice(pair * 2 * SHARD, (pair + 1) * 2 * SHARD)
        pre = pre_part[rows, :] + dot_rows(x_last[rows, :], up[...])
        grad = grad_part[rows, :] + dot_last(g[rows, 3 * block :], down[...])
        sig = jax.nn.sigmoid(pre)
        act_turned[:, rows] = jnp.transpose((pre * sig).astype(BF16))
        back[rows, :] = (grad * (sig * (1.0 + pre * (1.0 - sig)))).astype(BF16)
    for bits in range(4):
        cols = slice(bits * block, (bits + 1) * block)
        up_out[bits][...] = dot_rows(x_turned[cols, :], back[...])
        down_out[bits][...] = dot_rows(act_turned[...], g[:, cols])


def last_forward_kernel(block, *refs):
    shards, ups = refs[0:4], refs[4:8]
    x_turned, act_turned, slope, x = refs[8:]
    for half in range(2):
        for bits in range(4):
            cols = owner_columns(block, bits)
            x[half * SHARD : (half + 1) * SHARD, bits * block : (bits + 1) * block] = (
                shards[2 * half][:, cols] + shards[2 * half + 1][:, cols]
            )
    pre = dot_rows(x[:, :block], ups[0][...])
    for bits in (1, 2, 3):
        pre = pre + dot_rows(x[:, bits * block : (bits + 1) * block], ups[bits][...])
    x_turned[...] = jnp.transpose(x[...])
    sig = jax.nn.sigmoid(pre)
    act_turned[...] = jnp.transpose((pre * sig).astype(BF16))
    slope[...] = sig * (1.0 + pre * (1.0 - sig))


def last_backward_kernel(block, *refs):
    shards, downs = refs[0:4], refs[4:8]
    table, x_turned, act_turned, slope, up_acc, down_acc = refs[8:14]
    up_far, down_far, back, g = refs[14:18]
    expert = lax.axis_index("expert")
    for half in range(2):
        gate = pick_gate(table, half, expert)
        for bits in range(4):
            cols = owner_columns(block, bits)
            g[half * SHARD : (half + 1) * SHARD, bits * block : (bits + 1) * block] = scale_rows(
                gate, shards[2 * half][:, cols] + shards[2 * half + 1][:, cols]
            )
    far = slice(3 * block, 4 * block)
    grad = dot_last(g[:, :block], downs[0][...])
    for bits in (1, 2, 3):
        grad = grad + dot_last(g[:, bits * block : (bits + 1) * block], downs[bits][...])
    back[...] = (grad * slope[...]).astype(BF16)
    down_far[...] = (dot_rows(act_turned[...], g[:, far]) + down_acc[...]).astype(BF16)
    up_far[...] = (dot_rows(x_turned[far, :], back[...]) + up_acc[...]).astype(BF16)


VMEM = pl.BlockSpec(memory_space=pltpu.VMEM)


def local_call(kernel, outs, args, scratch=(), flops=0):
    moved = sum(v.size * v.dtype.itemsize for v in (*args, *outs))
    return pl.pallas_call(
        kernel,
        out_shape=outs,
        in_specs=[VMEM] * len(args),
        out_specs=[VMEM] * len(outs),
        scratch_shapes=list(scratch),
        compiler_params=pltpu.CompilerParams(vmem_limit_bytes=GRANT * MIB),
        cost_estimate=pl.CostEstimate(flops=flops, bytes_accessed=moved, transcendentals=0),
    )(*args)


GRANT = 24


def shape(rows, cols, dtype):
    return jax.ShapeDtypeStruct((rows, cols), dtype)


def early_forward(xs, ups):
    block, hidden = ups[0].shape
    rows, width = len(xs) * SHARD, 4 * block
    return local_call(
        functools.partial(early_forward_kernel, block, len(xs)),
        [shape(rows, block, BF16), shape(width, rows, BF16), shape(rows, hidden, F32)],
        (*xs, *ups[:3]),
        [pltpu.VMEM((2 * SHARD, width), BF16)],
        flops=6 * rows * block * hidden,
    )


def early_backward(gs, tables, downs):
    hidden, block = downs[0].shape
    rows, width = len(gs) * SHARD, 4 * block
    return local_call(
        functools.partial(early_backward_kernel, block, len(gs)),
        [shape(rows, width, BF16), shape(rows, hidden, F32)],
        (*gs, *tables, *downs[:3]),
        flops=6 * rows * block * hidden,
    )


def most_of(x_last, x_turned, g, pre_part, grad_part, up, down):
    block, hidden = up.shape
    rows = g.shape[0]
    got = local_call(
        functools.partial(most_kernel, block),
        [shape(block, hidden, F32)] * 4 + [shape(hidden, block, F32)] * 4,
        (x_last, x_turned, g, pre_part, grad_part, up, down),
        [pltpu.VMEM((hidden, rows), BF16), pltpu.VMEM((rows, hidden), BF16)],
        flops=20 * rows * block * hidden,
    )
    return got[:4], got[4:]


def last_forward(shards, ups):
    block, hidden = ups[0].shape
    rows, width = 2 * SHARD, 4 * block
    return local_call(
        functools.partial(last_forward_kernel, block),
        [shape(width, rows, BF16), shape(hidden, rows, BF16), shape(rows, hidden, F32)],
        (*shards, *ups),
        [pltpu.VMEM((rows, width), BF16)],
        flops=2 * rows * width * hidden,
    )


def last_backward(shards, downs, table, x, act, slope, up_acc, down_acc):
    hidden, block = downs[0].shape
    rows, width = 2 * SHARD, 4 * block
    return local_call(
        functools.partial(last_backward_kernel, block),
        [shape(block, hidden, BF16), shape(hidden, block, BF16), shape(rows, hidden, BF16), shape(rows, width, BF16)],
        (*shards, *downs, table, x, act, slope, up_acc, down_acc),
        flops=4 * rows * width * hidden,
    )


def dense_shards(tokens, grad_out, expert_ids, gate_q, w_up, w_down):
    return dense_body(tokens, grad_out, expert_ids, gate_q, w_up[0], w_down[0])


def dense_body(tokens, grad_out, expert_ids, gate_q, w_up, w_down):
    devices = lax.axis_size("expert")
    block, _ = w_up.shape

    def ex(value, perm):
        return lax.ppermute(value, "expert", perm)

    def dp(value, bits):
        return lax.ppermute(value, "dp", xor_perm(4, bits))

    swap = xor_perm(devices, 1)

    def ring(hops):
        return [(i, (i + 2 * hops) % devices) for i in range(devices)]

    up_mid = [(i, i + 2) for i in range(2, devices - 2)]
    down_mid = [(i, i - 2) for i in range(2, devices - 2)]

    t1 = ex(tokens, ring(1))
    t3 = ex(tokens, ring(-1))
    up_x = dp(w_up, 1)
    down_y = dp(w_down, 2)
    g1 = ex(grad_out, ring(1))
    g3 = ex(grad_out, ring(-1))
    up_y = dp(w_up, 2)
    down_x = dp(w_down, 1)

    experts = jnp.arange(devices, dtype=jnp.int32)
    named = expert_ids.T[None, :, :] == experts[:, None, None]
    gate_table = jnp.sum(jnp.where(named, gate_q.T[None, :, :], 0), axis=1).astype(F32) * (1.0 / 65536.0)
    c0 = jnp.concatenate([gate_table, ex(gate_table, swap)], axis=1)
    c1 = ex(c0, ring(1))
    c2 = ex(c0, ring(2))
    c3 = ex(c0, ring(3))
    t0b = ex(tokens, swap)
    g0b = ex(grad_out, swap)

    up_d = dp(up_x, 2)
    down_d = dp(down_y, 1)
    t2u = ex(t1, up_mid)
    t2d = ex(t3, down_mid)
    t1b = ex(t1, swap)
    t3b = ex(t3, swap)
    g2u = ex(g1, up_mid)
    g2d = ex(g3, down_mid)
    g1b = ex(g1, swap)
    g3b = ex(g3, swap)
    t2ub = ex(t2u, swap)
    t2db = ex(t2d, swap)
    g2ub = ex(g2u, swap)
    g2db = ex(g2d, swap)

    ups = (w_up, up_x, up_y, up_d)
    downs = (w_down, down_x, down_y, down_d)
    x_last, x_turned, pre_part = early_forward((tokens, t0b, t1, t1b, t3, t3b), ups)
    g_ab, grad_part = early_backward((grad_out, g0b, g1, g1b, g3, g3b), (c0, c1, c3), downs)
    up_acc, down_acc = most_of(x_last, x_turned, g_ab, pre_part, grad_part, up_d, down_d)
    x_c, act_c, slope_c = last_forward((t2u, t2d, t2ub, t2db), ups)
    up_first, down_first, back_c, g_c = last_backward(
        (g2u, g2d, g2ub, g2db), downs, c2, x_c, act_c, slope_c, up_acc[3], down_acc[3]
    )

    def up_block(bits):
        return dot_rows(x_c[bits * block : (bits + 1) * block, :], back_c) + up_acc[bits]

    def down_block(bits):
        return dot_rows(act_c, g_c[:, bits * block : (bits + 1) * block]) + down_acc[bits]

    down_far = dp(down_first, 1)
    up_far = dp(up_first, 2)
    up_second, down_second = up_block(2).astype(BF16), down_block(1).astype(BF16)
    up_near = dp(up_second, 2)
    down_near = dp(down_second, 1)
    up_side, down_side = up_block(1), down_block(2)
    up_own, down_own = up_block(0), down_block(0)
    up_side, down_side, up_own, down_own = lax.optimization_barrier((up_side, down_side, up_own, down_own))
    up_fwd = dp((up_side + up_far.astype(F32)).astype(BF16), 1)
    down_fwd = dp((down_side + down_far.astype(F32)).astype(BF16), 2)
    dw_up = (up_own + up_near.astype(F32) + up_fwd.astype(F32)).astype(BF16)
    dw_down = (down_own + down_near.astype(F32) + down_fwd.astype(F32)).astype(BF16)
    return dw_up[None], dw_down[None]


def shards(tokens, grad_out, expert_ids, gate_q, w_up, w_down):
    devices = lax.axis_size("expert")
    token_count, top_count = expert_ids.shape
    capacity = max(2, token_count * top_count * 3 // (2 * devices))
    if 2 * capacity >= token_count and devices == 8 and lax.axis_size("dp") == 4 and token_count == SHARD:
        return dense_shards(tokens, grad_out, expert_ids, gate_q, w_up, w_down)
    return sparse_shards(tokens, grad_out, expert_ids, gate_q, w_up, w_down, capacity)


def solution(mesh):
    in_specs = (
        P(("dp", "expert"), None),
        P(("dp", "expert"), None),
        P(("dp", "expert"), None),
        P(("dp", "expert"), None),
        P("expert", "dp", None),
        P("expert", None, "dp"),
    )
    out_specs = (P("expert", "dp", None), P("expert", None, "dp"))
    return jax.shard_map(shards, mesh=mesh, in_specs=in_specs, out_specs=out_specs, check_vma=False)
```

```python
import functools

import jax
import jax.numpy as jnp
from jax import lax
from jax.experimental import pallas as pl
from jax.experimental.pallas import tpu as pltpu
from jax.sharding import PartitionSpec as P


F32 = jnp.float32
BF16 = jnp.bfloat16
FIRST = (((0,), (0,)), ((), ()))
LAST = (((1,), (1,)), ((), ()))


def silu_slope(values):
    sigmoid_part = jax.nn.sigmoid(values)
    return sigmoid_part * (1.0 + values * (1.0 - sigmoid_part))


def summed_up(recv_rows, projected_grad):
    partial_value = lax.dot_general(recv_rows, projected_grad, FIRST, preferred_element_type=F32).astype(BF16)
    pieces = lax.all_to_all(partial_value[None], "dp", split_axis=1, concat_axis=0, tiled=True)
    return jnp.sum(pieces.astype(F32), axis=0, keepdims=True).astype(BF16)


def summed_down(activated, grad_rows):
    partial_value = lax.dot_general(activated, grad_rows, FIRST, preferred_element_type=F32).astype(BF16)
    pieces = lax.all_to_all(partial_value[None], "dp", split_axis=2, concat_axis=0, tiled=True)
    return jnp.sum(pieces.astype(F32), axis=0, keepdims=True).astype(BF16)


def sparse_shards(tokens, grad_out, expert_ids, gate_q, w_up, w_down, capacity):
    devices = lax.axis_size("expert")
    top_count = expert_ids.shape[1]
    model_width = tokens.shape[1]
    slot_expert = expert_ids.reshape(-1)
    onehot_table = (slot_expert[:, None] == jnp.arange(devices, dtype=jnp.int32)[None, :]).astype(jnp.int32)
    earlier = jnp.cumsum(onehot_table, axis=0) - onehot_table
    slot_rank = jnp.sum(earlier * onehot_table, axis=1)
    slot_target = slot_expert * capacity + slot_rank
    gate_values = gate_q.reshape(-1).astype(F32) * (1.0 / 65536.0)
    token_rows = jnp.repeat(tokens, top_count, axis=0)
    slot_grads = (gate_values[:, None] * jnp.repeat(grad_out, top_count, axis=0).astype(F32)).astype(BF16)
    empty_rows = jnp.zeros((devices * capacity, model_width), BF16)
    send_tokens = empty_rows.at[slot_target].set(token_rows).reshape(devices, capacity, model_width)
    grad_slots = empty_rows.at[slot_target].set(slot_grads).reshape(devices, capacity, model_width)
    up_whole = lax.all_gather(w_up, "dp", axis=1, tiled=True)[0]
    down_whole = lax.all_gather(w_down, "dp", axis=2, tiled=True)[0]
    recv_tokens = lax.all_to_all(send_tokens, "expert", split_axis=0, concat_axis=0, tiled=True)
    recv_rows = recv_tokens.reshape(-1, model_width)
    projected = jnp.dot(recv_rows, up_whole, preferred_element_type=F32)
    recv_grads = lax.all_to_all(grad_slots, "expert", split_axis=0, concat_axis=0, tiled=True)
    activated = jax.nn.silu(projected).astype(BF16)
    grad_rows = recv_grads.reshape(-1, model_width)
    act_grad = lax.dot_general(grad_rows, down_whole, LAST, preferred_element_type=F32)
    projected_grad = (act_grad * silu_slope(projected)).astype(BF16)
    return summed_up(recv_rows, projected_grad), summed_down(activated, grad_rows)


def xor_perm(count, bits):
    return [(i, i ^ bits) for i in range(count)]


MIB = 1 << 20


def pick_gate(table_ref, part, expert):
    table = table_ref[:, part * SHARD : (part + 1) * SHARD]
    mine = lax.broadcasted_iota(jnp.int32, table.shape, 0) == expert
    row = jnp.sum(jnp.where(mine, table, 0.0), axis=0, keepdims=True)
    return jnp.transpose(jnp.broadcast_to(row, (SHARD, SHARD)))


SHARD = 128


def scale_rows(gate, rows):
    wide = jnp.concatenate([gate] * (rows.shape[1] // gate.shape[1]), axis=1)
    return (wide * rows.astype(F32)).astype(BF16)


def dot_rows(left, right):
    return jnp.dot(left, right, preferred_element_type=F32)


def dot_last(left, right):
    return lax.dot_general(left, right, LAST, preferred_element_type=F32)


def owner_columns(block, bits):
    return pl.ds(pl.multiple_of((lax.axis_index("dp") ^ bits) * block, block), block)


SENT = (3, 1, 2)


def prepare_kernel(block, grad, tokens, up, down, sent, kept, tokens_copy, up_copy, down_copy):
    for place, bits in enumerate(SENT):
        sent[:, place * block : (place + 1) * block] = grad[:, owner_columns(block, bits)]
    kept[...] = grad[:, owner_columns(block, 0)]
    tokens_copy[...] = tokens[...]
    up_copy[...] = up[...]
    down_copy[...] = down[...]


def early_forward_kernel(block, shards, *refs):
    xs, ups = refs[0:shards], refs[shards : shards + 2]
    x_tail, x_turned, part = refs[shards + 2 : shards + 5]
    x = refs[shards + 5]
    for pair in range(shards // 2):
        rows = slice(pair * 2 * SHARD, (pair + 1) * 2 * SHARD)
        for half in range(2):
            for bits in range(4):
                x[half * SHARD : (half + 1) * SHARD, bits * block : (bits + 1) * block] = xs[pair * 2 + half][
                    :, owner_columns(block, bits)
                ]
        part[rows, :] = dot_rows(x[:, :block], ups[0][...]) + dot_rows(x[:, block : 2 * block], ups[1][...])
        x_tail[rows, :] = x[:, 2 * block :]
        x_turned[:, rows] = jnp.transpose(x[...])


def activate(pre):
    sig = jax.nn.sigmoid(pre)
    return (pre * sig).astype(BF16), sig * (1.0 + pre * (1.0 - sig))


def most_down_kernel(block, shards, *refs):
    gs, tables = refs[0:shards], refs[shards : shards + shards // 2]
    x_tail, part, up_y, up_d = refs[shards + shards // 2 : shards + shards // 2 + 4]
    g, act_turned, slope, *sums = refs[shards + shards // 2 + 4 :]
    expert = lax.axis_index("expert")
    for pair in range(shards // 2):
        rows = slice(pair * 2 * SHARD, (pair + 1) * 2 * SHARD)
        for half in range(2):
            own = slice((pair * 2 + half) * SHARD, (pair * 2 + half + 1) * SHARD)
            g[own, :] = scale_rows(pick_gate(tables[pair], half, expert), gs[pair * 2 + half][...])
        pre = part[rows, :] + dot_rows(x_tail[rows, :block], up_y[...]) + dot_rows(x_tail[rows, block:], up_d[...])
        act, slope[rows, :] = activate(pre)
        act_turned[:, rows] = jnp.transpose(act)
    for place in range(3):
        sums[place][...] = dot_rows(act_turned[...], g[:, place * block : (place + 1) * block])


def last_forward_kernel(block, *refs):
    shards, ups = refs[0:4], refs[4:8]
    x_turned, act_turned, slope, x = refs[8:]
    for half in range(2):
        for bits in range(4):
            cols = owner_columns(block, bits)
            x[half * SHARD : (half + 1) * SHARD, bits * block : (bits + 1) * block] = (
                shards[2 * half][:, cols] + shards[2 * half + 1][:, cols]
            )
    pre = dot_rows(x[:, :block], ups[0][...])
    for bits in (1, 2, 3):
        pre = pre + dot_rows(x[:, bits * block : (bits + 1) * block], ups[bits][...])
    x_turned[...] = jnp.transpose(x[...])
    act, slope[...] = activate(pre)
    act_turned[...] = jnp.transpose(act)


def last_down_kernel(block, *refs):
    shards, table, act_turned, sums = refs[0:4], refs[4], refs[5], refs[6:9]
    g, far_a, far_b, near_a, near_b, side_a, side_b = refs[9:]
    expert = lax.axis_index("expert")
    for half in range(2):
        gate = pick_gate(table, half, expert)
        g[half * SHARD : (half + 1) * SHARD, :] = scale_rows(gate, shards[2 * half][...] + shards[2 * half + 1][...])
    middle = act_turned.shape[0] // 2
    total = dot_rows(act_turned[...], g[:, :block]) + sums[0][...]
    far_a[...] = total[:middle].astype(BF16)
    far_b[...] = total[middle:].astype(BF16)
    total = dot_rows(act_turned[...], g[:, block : 2 * block]) + sums[1][...]
    near_a[...] = total[:middle].astype(BF16)
    side_b[...] = total[middle:]
    total = dot_rows(act_turned[...], g[:, 2 * block :]) + sums[2][...]
    side_a[...] = total[:middle]
    near_b[...] = total[middle:].astype(BF16)


def early_backward_kernel(block, g, *refs):
    downs, part = refs[0:3], refs[3]
    for pair in range(g.shape[0] // (2 * SHARD)):
        rows = slice(pair * 2 * SHARD, (pair + 1) * 2 * SHARD)
        total = dot_last(g[rows, :block], downs[0][...])
        for place in (1, 2):
            total = total + dot_last(g[rows, place * block : (place + 1) * block], downs[place][...])
        part[rows, :] = total


def most_up_kernel(block, shards, *refs):
    gs, tables = refs[0:shards], refs[shards : shards + shards // 2]
    part, slope, x_turned, act_turned, down = refs[shards + shards // 2 : shards + shards // 2 + 5]
    sums, down_own = refs[shards + shards // 2 + 5 : shards + shards // 2 + 9], refs[shards + shards // 2 + 9]
    g, back = refs[shards + shards // 2 + 10 :]
    expert = lax.axis_index("expert")
    for pair in range(shards // 2):
        rows = slice(pair * 2 * SHARD, (pair + 1) * 2 * SHARD)
        for half in range(2):
            own = slice((pair * 2 + half) * SHARD, (pair * 2 + half + 1) * SHARD)
            g[own, :] = scale_rows(pick_gate(tables[pair], half, expert), gs[pair * 2 + half][...])
        back[rows, :] = ((part[rows, :] + dot_last(g[rows, :], down[...])) * slope[rows, :]).astype(BF16)
    for bits in range(4):
        sums[bits][...] = dot_rows(x_turned[bits * block : (bits + 1) * block, :], back[...])
    down_own[...] = dot_rows(act_turned[...], g[...])


def last_up_kernel(block, *refs):
    shards, table, g, slope, x_turned, act_turned = refs[0:2], refs[2], refs[3], refs[4], refs[5], refs[6]
    downs, sums, down_sum = refs[7:11], refs[11:15], refs[15]
    far_a, far_b, near_a, near_b, side_a, side_b, up_own, down_own = refs[16:24]
    kept, back = refs[24:]
    expert = lax.axis_index("expert")
    for half in range(2):
        gate = pick_gate(table, half, expert)
        kept[half * SHARD : (half + 1) * SHARD, :] = scale_rows(gate, shards[half][...])
    grad = dot_last(kept[...], downs[0][...])
    for place, bits in enumerate(SENT):
        grad = grad + dot_last(g[:, place * block : (place + 1) * block], downs[bits][...])
    back[...] = (grad * slope[...]).astype(BF16)
    middle = block // 2
    total = dot_rows(x_turned[3 * block :, :], back[...]) + sums[3][...]
    far_a[...] = total[:middle].astype(BF16)
    far_b[...] = total[middle:].astype(BF16)
    total = dot_rows(x_turned[block : 2 * block, :], back[...]) + sums[1][...]
    near_a[...] = total[:middle].astype(BF16)
    side_b[...] = total[middle:]
    total = dot_rows(x_turned[2 * block : 3 * block, :], back[...]) + sums[2][...]
    side_a[...] = total[:middle]
    near_b[...] = total[middle:].astype(BF16)
    up_own[...] = dot_rows(x_turned[:block, :], back[...]) + sums[0][...]
    down_own[...] = dot_rows(act_turned[...], kept[...]) + down_sum[...]


def finish_kernel(own, near_a, near_b, far_a, far_b, out):
    middle = own.shape[0] // 2
    out[:middle, :] = (own[:middle, :] + near_a[...].astype(F32) + far_a[...].astype(F32)).astype(BF16)
    out[middle:, :] = (own[middle:, :] + near_b[...].astype(F32) + far_b[...].astype(F32)).astype(BF16)


VMEM = pl.BlockSpec(memory_space=pltpu.VMEM)


def local_call(kernel, outs, args, scratch=(), flops=0):
    moved = sum(v.size * v.dtype.itemsize for v in (*args, *outs))
    return pl.pallas_call(
        kernel,
        out_shape=outs,
        in_specs=[VMEM] * len(args),
        out_specs=[VMEM] * len(outs),
        scratch_shapes=list(scratch),
        compiler_params=pltpu.CompilerParams(vmem_limit_bytes=GRANT * MIB),
        cost_estimate=pl.CostEstimate(flops=flops, bytes_accessed=moved, transcendentals=0),
    )(*args)


GRANT = 24


def shape(rows, cols, dtype):
    return jax.ShapeDtypeStruct((rows, cols), dtype)


def prepare(grad, tokens, up, down):
    rows, width = grad.shape
    block = width // 4
    outs = [shape(rows, 3 * block, BF16), shape(rows, block, BF16)] + [shape(*v.shape, BF16) for v in (tokens, up, down)]
    return local_call(functools.partial(prepare_kernel, block), outs, (grad, tokens, up, down))


def early_forward(xs, ups):
    block, hidden = ups[0].shape
    rows, width = len(xs) * SHARD, 4 * block
    return local_call(
        functools.partial(early_forward_kernel, block, len(xs)),
        [shape(rows, 2 * block, BF16), shape(width, rows, BF16), shape(rows, hidden, F32)],
        (*xs, *ups[:2]),
        [pltpu.VMEM((2 * SHARD, width), BF16)],
        flops=4 * rows * block * hidden,
    )


def most_down(gs, tables, x_tail, part, up_y, up_d):
    block, hidden = up_y.shape
    rows = len(gs) * SHARD
    return local_call(
        functools.partial(most_down_kernel, block, len(gs)),
        [shape(rows, 3 * block, BF16), shape(hidden, rows, BF16), shape(rows, hidden, F32)] + [shape(hidden, block, F32)] * 3,
        (*gs, *tables, x_tail, part, up_y, up_d),
        flops=10 * rows * block * hidden,
    )


def last_forward(shards, ups):
    block, hidden = ups[0].shape
    rows, width = 2 * SHARD, 4 * block
    return local_call(
        functools.partial(last_forward_kernel, block),
        [shape(width, rows, BF16), shape(hidden, rows, BF16), shape(rows, hidden, F32)],
        (*shards, *ups),
        [pltpu.VMEM((rows, width), BF16)],
        flops=2 * rows * width * hidden,
    )


def exchanged(rows, cols):
    return [shape(rows // 2, cols, BF16)] * 4 + [shape(rows // 2, cols, F32)] * 2


def last_down(shards, table, act_turned, sums):
    hidden, block = sums[0].shape
    return local_call(
        functools.partial(last_down_kernel, block),
        [shape(2 * SHARD, 3 * block, BF16)] + exchanged(hidden, block),
        (*shards, table, act_turned, *sums),
        flops=12 * SHARD * block * hidden,
    )


def early_backward(g, downs):
    hidden, block = downs[0].shape
    rows = g.shape[0]
    return local_call(
        functools.partial(early_backward_kernel, block),
        [shape(rows, hidden, F32)],
        (g, *(downs[bits] for bits in SENT)),
        flops=6 * rows * block * hidden,
    )[0]


def most_up(gs, tables, part, slope, x_turned, act_turned, down):
    hidden, block = down.shape
    rows = len(gs) * SHARD
    got = local_call(
        functools.partial(most_up_kernel, block, len(gs)),
        [shape(block, hidden, F32)] * 4 + [shape(hidden, block, F32)],
        (*gs, *tables, part, slope, x_turned, act_turned, down),
        [pltpu.VMEM((rows, block), BF16), pltpu.VMEM((rows, hidden), BF16)],
        flops=12 * rows * block * hidden,
    )
    return got[:4], got[4]


def last_up(shards, table, g, slope, x_turned, act_turned, downs, sums, down_sum):
    hidden, block = downs[0].shape
    rows = 2 * SHARD
    return local_call(
        functools.partial(last_up_kernel, block),
        exchanged(block, hidden) + [shape(block, hidden, F32), shape(hidden, block, F32)],
        (*shards, table, g, slope, x_turned, act_turned, *downs, *sums, down_sum),
        [pltpu.VMEM((rows, block), BF16), pltpu.VMEM((rows, hidden), BF16)],
        flops=18 * rows * block * hidden,
    )


def finish(own, near_a, near_b, far_a, far_b):
    return local_call(finish_kernel, [shape(*own.shape, BF16)], (own, near_a, near_b, far_a, far_b))[0]


def dense_shards(tokens, grad_out, expert_ids, gate_q, w_up, w_down):
    return dense_body(tokens, grad_out, expert_ids, gate_q, w_up[0], w_down[0])


def dense_body(tokens, grad_out, expert_ids, gate_q, w_up, w_down):
    devices = lax.axis_size("expert")

    def ex(value, perm):
        return lax.ppermute(value, "expert", perm)

    def dp(value, bits):
        return lax.ppermute(value, "dp", xor_perm(4, bits))

    swap = xor_perm(devices, 1)

    def ring(hops):
        return [(i, (i + 2 * hops) % devices) for i in range(devices)]

    up_mid = [(i, i + 2) for i in range(2, devices - 2)]
    down_mid = [(i, i - 2) for i in range(2, devices - 2)]

    ga, gb, tokens_here, up_here, down_here = prepare(grad_out, tokens, w_up, w_down)

    t1 = ex(tokens, ring(1))
    t3 = ex(tokens, ring(-1))
    up_x = dp(w_up, 1)
    down_y = dp(w_down, 2)
    ga1 = ex(ga, ring(1))
    ga3 = ex(ga, ring(-1))
    up_y = dp(w_up, 2)
    down_x = dp(w_down, 1)

    experts = jnp.arange(devices, dtype=jnp.int32)
    named = expert_ids.T[None, :, :] == experts[:, None, None]
    gate_table = jnp.sum(jnp.where(named, gate_q.T[None, :, :], 0), axis=1).astype(F32) * (1.0 / 65536.0)
    c0 = jnp.concatenate([gate_table, ex(gate_table, swap)], axis=1)
    c1 = ex(c0, ring(1))
    c2 = ex(c0, ring(2))
    c3 = ex(c0, ring(3))
    t0b = ex(tokens, swap)
    ga0b = ex(ga, swap)
    gb0b = ex(gb, swap)

    up_d = dp(up_x, 2)
    down_d = dp(down_y, 1)
    t2u = ex(t1, up_mid)
    t2d = ex(t3, down_mid)
    t1b = ex(t1, swap)
    t3b = ex(t3, swap)
    ga2u = ex(ga1, up_mid)
    ga2d = ex(ga3, down_mid)
    ga1b = ex(ga1, swap)
    ga3b = ex(ga3, swap)
    gb1 = ex(gb, ring(1))
    gb3 = ex(gb, ring(-1))
    gb2 = ex(gb, ring(2))
    t2ub = ex(t2u, swap)
    t2db = ex(t2d, swap)
    ga2ub = ex(ga2u, swap)
    ga2db = ex(ga2d, swap)
    gb1b = ex(gb1, swap)
    gb3b = ex(gb3, swap)
    gb2b = ex(gb2, swap)

    ups = (up_here, up_x, up_y, up_d)
    downs = (down_here, down_x, down_y, down_d)
    tables = (c0, c1, c3)
    x_tail, x_turned, pre_part = early_forward((tokens_here, t0b, t1, t1b, t3, t3b), ups)
    g_ab, act_ab, slope_ab, *down_sums = most_down((ga, ga0b, ga1, ga1b, ga3, ga3b), tables, x_tail, pre_part, up_y, up_d)
    x_c, act_c, slope_c = last_forward((t2u, t2d, t2ub, t2db), ups)
    g_c, *down_parts = last_down((ga2u, ga2d, ga2ub, ga2db), c2, act_c, down_sums)
    grad_part = early_backward(g_ab, downs)
    up_sums, down_sum = most_up((gb, gb0b, gb1, gb1b, gb3, gb3b), tables, grad_part, slope_ab, x_turned, act_ab, down_here)
    *up_parts, up_own, down_own = last_up((gb2, gb2b), c2, g_c, slope_c, x_c, act_c, downs, up_sums, down_sum)

    def exchange(far_a, far_b, near_a, near_b, side_a, side_b):
        far_a = dp(far_a, 1)
        far_b = dp(far_b, 2)
        near_a = dp(near_a, 1)
        near_b = dp(near_b, 2)
        side_a = (side_a + far_a.astype(F32)).astype(BF16)
        side_b = (side_b + far_b.astype(F32)).astype(BF16)
        return near_a, near_b, dp(side_a, 2), dp(side_b, 1)

    down_got = exchange(*down_parts)
    up_got = exchange(*up_parts)
    dw_down = finish(down_own, *down_got)
    dw_up = finish(up_own, *up_got)
    return dw_up[None], dw_down[None]


def shards(tokens, grad_out, expert_ids, gate_q, w_up, w_down):
    devices = lax.axis_size("expert")
    token_count, top_count = expert_ids.shape
    capacity = max(2, token_count * top_count * 3 // (2 * devices))
    if 2 * capacity >= token_count and devices == 8 and lax.axis_size("dp") == 4 and token_count == SHARD:
        return dense_shards(tokens, grad_out, expert_ids, gate_q, w_up, w_down)
    return sparse_shards(tokens, grad_out, expert_ids, gate_q, w_up, w_down, capacity)


def solution(mesh):
    in_specs = (
        P(("dp", "expert"), None),
        P(("dp", "expert"), None),
        P(("dp", "expert"), None),
        P(("dp", "expert"), None),
        P("expert", "dp", None),
        P("expert", None, "dp"),
    )
    out_specs = (P("expert", "dp", None), P("expert", None, "dp"))
    return jax.shard_map(shards, mesh=mesh, in_specs=in_specs, out_specs=out_specs, check_vma=False)
```

```python
import functools

import jax
import jax.numpy as jnp
from jax import lax
from jax.experimental import pallas as pl
from jax.experimental.pallas import tpu as pltpu
from jax.sharding import PartitionSpec as P


F32 = jnp.float32
BF16 = jnp.bfloat16
FIRST = (((0,), (0,)), ((), ()))
LAST = (((1,), (1,)), ((), ()))


def silu_slope(values):
    sigmoid_part = jax.nn.sigmoid(values)
    return sigmoid_part * (1.0 + values * (1.0 - sigmoid_part))


def summed_up(recv_rows, projected_grad):
    partial_value = lax.dot_general(recv_rows, projected_grad, FIRST, preferred_element_type=F32).astype(BF16)
    pieces = lax.all_to_all(partial_value[None], "dp", split_axis=1, concat_axis=0, tiled=True)
    return jnp.sum(pieces.astype(F32), axis=0, keepdims=True).astype(BF16)


def summed_down(activated, grad_rows):
    partial_value = lax.dot_general(activated, grad_rows, FIRST, preferred_element_type=F32).astype(BF16)
    pieces = lax.all_to_all(partial_value[None], "dp", split_axis=2, concat_axis=0, tiled=True)
    return jnp.sum(pieces.astype(F32), axis=0, keepdims=True).astype(BF16)


def sparse_shards(tokens, grad_out, expert_ids, gate_q, w_up, w_down, capacity):
    devices = lax.axis_size("expert")
    top_count = expert_ids.shape[1]
    model_width = tokens.shape[1]
    slot_expert = expert_ids.reshape(-1)
    onehot_table = (slot_expert[:, None] == jnp.arange(devices, dtype=jnp.int32)[None, :]).astype(jnp.int32)
    earlier = jnp.cumsum(onehot_table, axis=0) - onehot_table
    slot_rank = jnp.sum(earlier * onehot_table, axis=1)
    slot_target = slot_expert * capacity + slot_rank
    gate_values = gate_q.reshape(-1).astype(F32) * (1.0 / 65536.0)
    token_rows = jnp.repeat(tokens, top_count, axis=0)
    slot_grads = (gate_values[:, None] * jnp.repeat(grad_out, top_count, axis=0).astype(F32)).astype(BF16)
    empty_rows = jnp.zeros((devices * capacity, model_width), BF16)
    send_tokens = empty_rows.at[slot_target].set(token_rows).reshape(devices, capacity, model_width)
    grad_slots = empty_rows.at[slot_target].set(slot_grads).reshape(devices, capacity, model_width)
    up_whole = lax.all_gather(w_up, "dp", axis=1, tiled=True)[0]
    down_whole = lax.all_gather(w_down, "dp", axis=2, tiled=True)[0]
    recv_tokens = lax.all_to_all(send_tokens, "expert", split_axis=0, concat_axis=0, tiled=True)
    recv_rows = recv_tokens.reshape(-1, model_width)
    projected = jnp.dot(recv_rows, up_whole, preferred_element_type=F32)
    recv_grads = lax.all_to_all(grad_slots, "expert", split_axis=0, concat_axis=0, tiled=True)
    activated = jax.nn.silu(projected).astype(BF16)
    grad_rows = recv_grads.reshape(-1, model_width)
    act_grad = lax.dot_general(grad_rows, down_whole, LAST, preferred_element_type=F32)
    projected_grad = (act_grad * silu_slope(projected)).astype(BF16)
    return summed_up(recv_rows, projected_grad), summed_down(activated, grad_rows)


def xor_perm(count, bits):
    return [(i, i ^ bits) for i in range(count)]


MIB = 1 << 20


def pick_gate(table_ref, part, expert):
    table = table_ref[:, part * SHARD : (part + 1) * SHARD]
    mine = lax.broadcasted_iota(jnp.int32, table.shape, 0) == expert
    row = jnp.sum(jnp.where(mine, table, 0.0), axis=0, keepdims=True)
    return jnp.transpose(jnp.broadcast_to(row, (SHARD, SHARD)))


SHARD = 128


def scale_rows(gate, rows):
    wide = jnp.concatenate([gate] * (rows.shape[1] // gate.shape[1]), axis=1)
    return (wide * rows.astype(F32)).astype(BF16)


def dot_rows(left, right):
    return jnp.dot(left, right, preferred_element_type=F32)


def dot_last(left, right):
    return lax.dot_general(left, right, LAST, preferred_element_type=F32)


def owner_columns(block, bits):
    return pl.ds(pl.multiple_of((lax.axis_index("dp") ^ bits) * block, block), block)


SENT = (3, 1, 2)


def prepare_kernel(block, grad, tokens, up, down, sent, kept, tokens_copy, up_copy, down_copy):
    for place, bits in enumerate(SENT):
        sent[:, place * block : (place + 1) * block] = grad[:, owner_columns(block, bits)]
    kept[...] = grad[:, owner_columns(block, 0)]
    tokens_copy[...] = tokens[...]
    up_copy[...] = up[...]
    down_copy[...] = down[...]


def early_forward_kernel(block, shards, *refs):
    xs, ups = refs[0:shards], refs[shards : shards + 2]
    x_tail, x_turned, part = refs[shards + 2 : shards + 5]
    x = refs[shards + 5]
    for pair in range(shards // 2):
        rows = slice(pair * 2 * SHARD, (pair + 1) * 2 * SHARD)
        for half in range(2):
            for bits in range(4):
                x[half * SHARD : (half + 1) * SHARD, bits * block : (bits + 1) * block] = xs[pair * 2 + half][
                    :, owner_columns(block, bits)
                ]
        part[rows, :] = dot_rows(x[:, :block], ups[0][...]) + dot_rows(x[:, block : 2 * block], ups[1][...])
        x_tail[rows, :] = x[:, 2 * block :]
        x_turned[:, rows] = jnp.transpose(x[...])


def activate(pre):
    sig = jax.nn.sigmoid(pre)
    return (pre * sig).astype(BF16), sig * (1.0 + pre * (1.0 - sig))


def most_down_kernel(block, shards, *refs):
    gs, tables = refs[0:shards], refs[shards : shards + shards // 2]
    x_tail, part, up_y, up_d = refs[shards + shards // 2 : shards + shards // 2 + 4]
    g, act_turned, slope, *sums = refs[shards + shards // 2 + 4 :]
    expert = lax.axis_index("expert")
    for pair in range(shards // 2):
        rows = slice(pair * 2 * SHARD, (pair + 1) * 2 * SHARD)
        for half in range(2):
            own = slice((pair * 2 + half) * SHARD, (pair * 2 + half + 1) * SHARD)
            g[own, :] = scale_rows(pick_gate(tables[pair], half, expert), gs[pair * 2 + half][...])
        pre = part[rows, :] + dot_rows(x_tail[rows, :block], up_y[...]) + dot_rows(x_tail[rows, block:], up_d[...])
        act, slope[rows, :] = activate(pre)
        act_turned[:, rows] = jnp.transpose(act)
    for place in range(3):
        sums[place][...] = dot_rows(act_turned[...], g[:, place * block : (place + 1) * block])


def last_forward_kernel(block, *refs):
    shards, ups = refs[0:4], refs[4:8]
    x_turned, act_turned, slope, x = refs[8:]
    for half in range(2):
        for bits in range(4):
            cols = owner_columns(block, bits)
            x[half * SHARD : (half + 1) * SHARD, bits * block : (bits + 1) * block] = (
                shards[2 * half][:, cols] + shards[2 * half + 1][:, cols]
            )
    pre = dot_rows(x[:, :block], ups[0][...])
    for bits in (1, 2, 3):
        pre = pre + dot_rows(x[:, bits * block : (bits + 1) * block], ups[bits][...])
    x_turned[...] = jnp.transpose(x[...])
    act, slope[...] = activate(pre)
    act_turned[...] = jnp.transpose(act)


def last_down_kernel(block, *refs):
    shards, table, act_turned, sums = refs[0:4], refs[4], refs[5], refs[6:9]
    g, far_a, far_b, near_a, near_b, side_a, side_b = refs[9:]
    expert = lax.axis_index("expert")
    for half in range(2):
        gate = pick_gate(table, half, expert)
        g[half * SHARD : (half + 1) * SHARD, :] = scale_rows(gate, shards[2 * half][...] + shards[2 * half + 1][...])
    middle = act_turned.shape[0] // 2
    total = dot_rows(act_turned[...], g[:, :block]) + sums[0][...]
    far_a[...] = total[:middle].astype(BF16)
    far_b[...] = total[middle:].astype(BF16)
    total = dot_rows(act_turned[...], g[:, block : 2 * block]) + sums[1][...]
    near_a[...] = total[:middle].astype(BF16)
    side_b[...] = total[middle:]
    total = dot_rows(act_turned[...], g[:, 2 * block :]) + sums[2][...]
    side_a[...] = total[:middle]
    near_b[...] = total[middle:].astype(BF16)


def early_backward_kernel(block, g, *refs):
    downs, part = refs[0:3], refs[3]
    for pair in range(g.shape[0] // (2 * SHARD)):
        rows = slice(pair * 2 * SHARD, (pair + 1) * 2 * SHARD)
        total = dot_last(g[rows, :block], downs[0][...])
        for place in (1, 2):
            total = total + dot_last(g[rows, place * block : (place + 1) * block], downs[place][...])
        part[rows, :] = total


def most_up_kernel(block, shards, *refs):
    gs, tables = refs[0:shards], refs[shards : shards + shards // 2]
    part, slope, x_turned, act_turned, down = refs[shards + shards // 2 : shards + shards // 2 + 5]
    sums, down_own = refs[shards + shards // 2 + 5 : shards + shards // 2 + 9], refs[shards + shards // 2 + 9]
    g, back = refs[shards + shards // 2 + 10 :]
    expert = lax.axis_index("expert")
    for pair in range(shards // 2):
        rows = slice(pair * 2 * SHARD, (pair + 1) * 2 * SHARD)
        for half in range(2):
            own = slice((pair * 2 + half) * SHARD, (pair * 2 + half + 1) * SHARD)
            g[own, :] = scale_rows(pick_gate(tables[pair], half, expert), gs[pair * 2 + half][...])
        back[rows, :] = ((part[rows, :] + dot_last(g[rows, :], down[...])) * slope[rows, :]).astype(BF16)
    for bits in range(4):
        sums[bits][...] = dot_rows(x_turned[bits * block : (bits + 1) * block, :], back[...])
    down_own[...] = dot_rows(act_turned[...], g[...])


def last_up_kernel(block, *refs):
    shards, table, g, slope, x_turned, act_turned = refs[0:2], refs[2], refs[3], refs[4], refs[5], refs[6]
    downs, sums, down_sum = refs[7:11], refs[11:15], refs[15]
    far_a, far_b, near_a, near_b, side_a, side_b, up_own, down_own = refs[16:24]
    kept, back = refs[24:]
    expert = lax.axis_index("expert")
    for half in range(2):
        gate = pick_gate(table, half, expert)
        kept[half * SHARD : (half + 1) * SHARD, :] = scale_rows(gate, shards[half][...])
    grad = dot_last(kept[...], downs[0][...])
    for place, bits in enumerate(SENT):
        grad = grad + dot_last(g[:, place * block : (place + 1) * block], downs[bits][...])
    back[...] = (grad * slope[...]).astype(BF16)
    middle = block // 2
    total = dot_rows(x_turned[3 * block :, :], back[...]) + sums[3][...]
    far_a[...] = total[:middle].astype(BF16)
    far_b[...] = total[middle:].astype(BF16)
    total = dot_rows(x_turned[block : 2 * block, :], back[...]) + sums[1][...]
    near_a[...] = total[:middle].astype(BF16)
    side_b[...] = total[middle:]
    total = dot_rows(x_turned[2 * block : 3 * block, :], back[...]) + sums[2][...]
    side_a[...] = total[:middle]
    near_b[...] = total[middle:].astype(BF16)
    up_own[...] = dot_rows(x_turned[:block, :], back[...]) + sums[0][...]
    down_own[...] = dot_rows(act_turned[...], kept[...]) + down_sum[...]


def finish_kernel(parts, near_sum, far_a, far_b, out, stage, sems):
    rows = near_sum.shape[0]
    step = rows // parts
    copies = []
    for i in range(parts):
        here = slice(i * step, (i + 1) * step)
        far, base = (far_a, 0) if i * 2 < parts else (far_b, rows // 2)
        got = far[i * step - base : (i + 1) * step - base, :]
        stage[here, :] = (near_sum[here, :] + got.astype(F32)).astype(BF16)
        copies.append(pltpu.make_async_copy(stage.at[pl.ds(i * step, step), :], out.at[pl.ds(i * step, step), :], sems.at[i]))
        copies[-1].start()
    for c in copies:
        c.wait()


def near_kernel(own, near_a, near_b, out):
    middle = own.shape[0] // 2
    out[:middle, :] = own[:middle, :] + near_a[...].astype(F32)
    out[middle:, :] = own[middle:, :] + near_b[...].astype(F32)


VMEM = pl.BlockSpec(memory_space=pltpu.VMEM)


def local_call(kernel, outs, args, scratch=(), flops=0):
    moved = sum(v.size * v.dtype.itemsize for v in (*args, *outs))
    return pl.pallas_call(
        kernel,
        out_shape=outs,
        in_specs=[VMEM] * len(args),
        out_specs=[VMEM] * len(outs),
        scratch_shapes=list(scratch),
        compiler_params=pltpu.CompilerParams(vmem_limit_bytes=GRANT * MIB),
        cost_estimate=pl.CostEstimate(flops=flops, bytes_accessed=moved, transcendentals=0),
    )(*args)


GRANT = 24


def shape(rows, cols, dtype):
    return jax.ShapeDtypeStruct((rows, cols), dtype)


def prepare(grad, tokens, up, down):
    rows, width = grad.shape
    block = width // 4
    outs = [shape(rows, 3 * block, BF16), shape(rows, block, BF16)] + [shape(*v.shape, BF16) for v in (tokens, up, down)]
    return local_call(functools.partial(prepare_kernel, block), outs, (grad, tokens, up, down))


def early_forward(xs, ups):
    block, hidden = ups[0].shape
    rows, width = len(xs) * SHARD, 4 * block
    return local_call(
        functools.partial(early_forward_kernel, block, len(xs)),
        [shape(rows, 2 * block, BF16), shape(width, rows, BF16), shape(rows, hidden, F32)],
        (*xs, *ups[:2]),
        [pltpu.VMEM((2 * SHARD, width), BF16)],
        flops=4 * rows * block * hidden,
    )


def most_down(gs, tables, x_tail, part, up_y, up_d):
    block, hidden = up_y.shape
    rows = len(gs) * SHARD
    return local_call(
        functools.partial(most_down_kernel, block, len(gs)),
        [shape(rows, 3 * block, BF16), shape(hidden, rows, BF16), shape(rows, hidden, F32)] + [shape(hidden, block, F32)] * 3,
        (*gs, *tables, x_tail, part, up_y, up_d),
        flops=10 * rows * block * hidden,
    )


def last_forward(shards, ups):
    block, hidden = ups[0].shape
    rows, width = 2 * SHARD, 4 * block
    return local_call(
        functools.partial(last_forward_kernel, block),
        [shape(width, rows, BF16), shape(hidden, rows, BF16), shape(rows, hidden, F32)],
        (*shards, *ups),
        [pltpu.VMEM((rows, width), BF16)],
        flops=2 * rows * width * hidden,
    )


def exchanged(rows, cols):
    return [shape(rows // 2, cols, BF16)] * 4 + [shape(rows // 2, cols, F32)] * 2


def last_down(shards, table, act_turned, sums):
    hidden, block = sums[0].shape
    return local_call(
        functools.partial(last_down_kernel, block),
        [shape(2 * SHARD, 3 * block, BF16)] + exchanged(hidden, block),
        (*shards, table, act_turned, *sums),
        flops=12 * SHARD * block * hidden,
    )


def early_backward(g, downs):
    hidden, block = downs[0].shape
    rows = g.shape[0]
    return local_call(
        functools.partial(early_backward_kernel, block),
        [shape(rows, hidden, F32)],
        (g, *(downs[bits] for bits in SENT)),
        flops=6 * rows * block * hidden,
    )[0]


def most_up(gs, tables, part, slope, x_turned, act_turned, down):
    hidden, block = down.shape
    rows = len(gs) * SHARD
    got = local_call(
        functools.partial(most_up_kernel, block, len(gs)),
        [shape(block, hidden, F32)] * 4 + [shape(hidden, block, F32)],
        (*gs, *tables, part, slope, x_turned, act_turned, down),
        [pltpu.VMEM((rows, block), BF16), pltpu.VMEM((rows, hidden), BF16)],
        flops=12 * rows * block * hidden,
    )
    return got[:4], got[4]


def last_up(shards, table, g, slope, x_turned, act_turned, downs, sums, down_sum):
    hidden, block = downs[0].shape
    rows = 2 * SHARD
    return local_call(
        functools.partial(last_up_kernel, block),
        exchanged(block, hidden) + [shape(block, hidden, F32), shape(hidden, block, F32)],
        (*shards, table, g, slope, x_turned, act_turned, *downs, *sums, down_sum),
        [pltpu.VMEM((rows, block), BF16), pltpu.VMEM((rows, hidden), BF16)],
        flops=18 * rows * block * hidden,
    )


def with_near(own, near_a, near_b):
    return local_call(near_kernel, [shape(*own.shape, F32)], (own, near_a, near_b))[0]


def finish(near_sum, far_a, far_b):
    parts = 4
    return pl.pallas_call(
        functools.partial(finish_kernel, parts),
        out_shape=shape(*near_sum.shape, BF16),
        in_specs=[VMEM] * 3,
        out_specs=pl.BlockSpec(memory_space=pl.ANY),
        scratch_shapes=[pltpu.VMEM(near_sum.shape, BF16), pltpu.SemaphoreType.DMA((parts,))],
        compiler_params=pltpu.CompilerParams(vmem_limit_bytes=GRANT * MIB),
        cost_estimate=pl.CostEstimate(flops=near_sum.size, bytes_accessed=10 * near_sum.size, transcendentals=0),
    )(near_sum, far_a, far_b)


def dense_shards(tokens, grad_out, expert_ids, gate_q, w_up, w_down):
    return dense_body(tokens, grad_out, expert_ids, gate_q, w_up[0], w_down[0])


def dense_body(tokens, grad_out, expert_ids, gate_q, w_up, w_down):
    devices = lax.axis_size("expert")

    def ex(value, perm):
        return lax.ppermute(value, "expert", perm)

    def dp(value, bits):
        return lax.ppermute(value, "dp", xor_perm(4, bits))

    swap = xor_perm(devices, 1)

    def ring(hops):
        return [(i, (i + 2 * hops) % devices) for i in range(devices)]

    up_mid = [(i, i + 2) for i in range(2, devices - 2)]
    down_mid = [(i, i - 2) for i in range(2, devices - 2)]

    ga, gb, tokens_here, up_here, down_here = prepare(grad_out, tokens, w_up, w_down)

    t1 = ex(tokens, ring(1))
    t3 = ex(tokens, ring(-1))
    up_x = dp(w_up, 1)
    down_y = dp(w_down, 2)
    ga1 = ex(ga, ring(1))
    ga3 = ex(ga, ring(-1))
    up_y = dp(w_up, 2)
    down_x = dp(w_down, 1)

    experts = jnp.arange(devices, dtype=jnp.int32)
    named = expert_ids.T[None, :, :] == experts[:, None, None]
    gate_table = jnp.sum(jnp.where(named, gate_q.T[None, :, :], 0), axis=1).astype(F32) * (1.0 / 65536.0)
    c0 = jnp.concatenate([gate_table, ex(gate_table, swap)], axis=1)
    c1 = ex(c0, ring(1))
    c2 = ex(c0, ring(2))
    c3 = ex(c0, ring(3))
    t0b = ex(tokens, swap)
    ga0b = ex(ga, swap)
    gb0b = ex(gb, swap)

    up_d = dp(up_x, 2)
    down_d = dp(down_y, 1)
    t2u = ex(t1, up_mid)
    t2d = ex(t3, down_mid)
    t1b = ex(t1, swap)
    t3b = ex(t3, swap)
    ga2u = ex(ga1, up_mid)
    ga2d = ex(ga3, down_mid)
    ga1b = ex(ga1, swap)
    ga3b = ex(ga3, swap)
    gb1 = ex(gb, ring(1))
    gb3 = ex(gb, ring(-1))
    gb2 = ex(gb, ring(2))
    t2ub = ex(t2u, swap)
    t2db = ex(t2d, swap)
    ga2ub = ex(ga2u, swap)
    ga2db = ex(ga2d, swap)
    gb1b = ex(gb1, swap)
    gb3b = ex(gb3, swap)
    gb2b = ex(gb2, swap)

    ups = (up_here, up_x, up_y, up_d)
    downs = (down_here, down_x, down_y, down_d)
    tables = (c0, c1, c3)
    x_tail, x_turned, pre_part = early_forward((tokens_here, t0b, t1, t1b, t3, t3b), ups)
    g_ab, act_ab, slope_ab, *down_sums = most_down((ga, ga0b, ga1, ga1b, ga3, ga3b), tables, x_tail, pre_part, up_y, up_d)
    x_c, act_c, slope_c = last_forward((t2u, t2d, t2ub, t2db), ups)
    g_c, *down_parts = last_down((ga2u, ga2d, ga2ub, ga2db), c2, act_c, down_sums)
    grad_part = early_backward(g_ab, downs)
    up_sums, down_sum = most_up((gb, gb0b, gb1, gb1b, gb3, gb3b), tables, grad_part, slope_ab, x_turned, act_ab, down_here)
    *up_parts, up_own, down_own = last_up((gb2, gb2b), c2, g_c, slope_c, x_c, act_c, downs, up_sums, down_sum)

    def exchange(far_a, far_b, near_a, near_b, side_a, side_b):
        far_a = dp(far_a, 1)
        far_b = dp(far_b, 2)
        near_a = dp(near_a, 1)
        near_b = dp(near_b, 2)
        side_a = (side_a + far_a.astype(F32)).astype(BF16)
        side_b = (side_b + far_b.astype(F32)).astype(BF16)
        return near_a, near_b, dp(side_a, 2), dp(side_b, 1)

    down_got = exchange(*down_parts)
    up_got = exchange(*up_parts)
    down_sum = with_near(down_own, *down_got[:2])
    dw_down = finish(down_sum, *down_got[2:])
    up_sum = with_near(up_own, *up_got[:2])
    dw_up = finish(up_sum, *up_got[2:])
    return dw_up[None], dw_down[None]


def shards(tokens, grad_out, expert_ids, gate_q, w_up, w_down):
    devices = lax.axis_size("expert")
    token_count, top_count = expert_ids.shape
    capacity = max(2, token_count * top_count * 3 // (2 * devices))
    if 2 * capacity >= token_count and devices == 8 and lax.axis_size("dp") == 4 and token_count == SHARD:
        return dense_shards(tokens, grad_out, expert_ids, gate_q, w_up, w_down)
    return sparse_shards(tokens, grad_out, expert_ids, gate_q, w_up, w_down, capacity)


def solution(mesh):
    in_specs = (
        P(("dp", "expert"), None),
        P(("dp", "expert"), None),
        P(("dp", "expert"), None),
        P(("dp", "expert"), None),
        P("expert", "dp", None),
        P("expert", None, "dp"),
    )
    out_specs = (P("expert", "dp", None), P("expert", None, "dp"))
    return jax.shard_map(shards, mesh=mesh, in_specs=in_specs, out_specs=out_specs, check_vma=False)
```

```python
import functools

import jax
import jax.numpy as jnp
from jax import lax
from jax.experimental import pallas as pl
from jax.experimental.pallas import tpu as pltpu
from jax.sharding import PartitionSpec as P


F32 = jnp.float32
BF16 = jnp.bfloat16
FIRST = (((0,), (0,)), ((), ()))
LAST = (((1,), (1,)), ((), ()))


def silu_slope(values):
    sigmoid_part = jax.nn.sigmoid(values)
    return sigmoid_part * (1.0 + values * (1.0 - sigmoid_part))


def summed_up(recv_rows, projected_grad):
    partial_value = lax.dot_general(recv_rows, projected_grad, FIRST, preferred_element_type=F32).astype(BF16)
    pieces = lax.all_to_all(partial_value[None], "dp", split_axis=1, concat_axis=0, tiled=True)
    return jnp.sum(pieces.astype(F32), axis=0, keepdims=True).astype(BF16)


def summed_down(activated, grad_rows):
    partial_value = lax.dot_general(activated, grad_rows, FIRST, preferred_element_type=F32).astype(BF16)
    pieces = lax.all_to_all(partial_value[None], "dp", split_axis=2, concat_axis=0, tiled=True)
    return jnp.sum(pieces.astype(F32), axis=0, keepdims=True).astype(BF16)


def sparse_shards(tokens, grad_out, expert_ids, gate_q, w_up, w_down, capacity):
    devices = lax.axis_size("expert")
    top_count = expert_ids.shape[1]
    model_width = tokens.shape[1]
    slot_expert = expert_ids.reshape(-1)
    onehot_table = (slot_expert[:, None] == jnp.arange(devices, dtype=jnp.int32)[None, :]).astype(jnp.int32)
    earlier = jnp.cumsum(onehot_table, axis=0) - onehot_table
    slot_rank = jnp.sum(earlier * onehot_table, axis=1)
    slot_target = slot_expert * capacity + slot_rank
    gate_values = gate_q.reshape(-1).astype(F32) * (1.0 / 65536.0)
    token_rows = jnp.repeat(tokens, top_count, axis=0)
    slot_grads = (gate_values[:, None] * jnp.repeat(grad_out, top_count, axis=0).astype(F32)).astype(BF16)
    empty_rows = jnp.zeros((devices * capacity, model_width), BF16)
    send_tokens = empty_rows.at[slot_target].set(token_rows).reshape(devices, capacity, model_width)
    grad_slots = empty_rows.at[slot_target].set(slot_grads).reshape(devices, capacity, model_width)
    up_whole = lax.all_gather(w_up, "dp", axis=1, tiled=True)[0]
    down_whole = lax.all_gather(w_down, "dp", axis=2, tiled=True)[0]
    recv_tokens = lax.all_to_all(send_tokens, "expert", split_axis=0, concat_axis=0, tiled=True)
    recv_rows = recv_tokens.reshape(-1, model_width)
    projected = jnp.dot(recv_rows, up_whole, preferred_element_type=F32)
    recv_grads = lax.all_to_all(grad_slots, "expert", split_axis=0, concat_axis=0, tiled=True)
    activated = jax.nn.silu(projected).astype(BF16)
    grad_rows = recv_grads.reshape(-1, model_width)
    act_grad = lax.dot_general(grad_rows, down_whole, LAST, preferred_element_type=F32)
    projected_grad = (act_grad * silu_slope(projected)).astype(BF16)
    return summed_up(recv_rows, projected_grad), summed_down(activated, grad_rows)


def xor_perm(count, bits):
    return [(i, i ^ bits) for i in range(count)]


MIB = 1 << 20


def pick_gate(table_ref, part, expert):
    table = table_ref[:, part * SHARD : (part + 1) * SHARD]
    mine = lax.broadcasted_iota(jnp.int32, table.shape, 0) == expert
    row = jnp.sum(jnp.where(mine, table, 0.0), axis=0, keepdims=True)
    return jnp.transpose(jnp.broadcast_to(row, (SHARD, SHARD)))


SHARD = 128


def scale_rows(gate, rows):
    wide = jnp.concatenate([gate] * (rows.shape[1] // gate.shape[1]), axis=1)
    return (wide * rows.astype(F32)).astype(BF16)


def dot_rows(left, right):
    return jnp.dot(left, right, preferred_element_type=F32)


def dot_last(left, right):
    return lax.dot_general(left, right, LAST, preferred_element_type=F32)


def owner_columns(block, bits):
    return pl.ds(pl.multiple_of((lax.axis_index("dp") ^ bits) * block, block), block)


SENT = (3, 1, 2)


def prepare_kernel(block, grad, tokens, up, down, sent, kept, tokens_copy, up_copy, down_copy):
    for place, bits in enumerate(SENT):
        sent[:, place * block : (place + 1) * block] = grad[:, owner_columns(block, bits)]
    kept[...] = grad[:, owner_columns(block, 0)]
    tokens_copy[...] = tokens[...]
    up_copy[...] = up[...]
    down_copy[...] = down[...]


def early_forward_kernel(block, shards, *refs):
    xs, ups = refs[0:shards], refs[shards : shards + 2]
    x_tail, x_turned, part = refs[shards + 2 : shards + 5]
    x = refs[shards + 5]
    for pair in range(shards // 2):
        rows = slice(pair * 2 * SHARD, (pair + 1) * 2 * SHARD)
        for half in range(2):
            for bits in range(4):
                x[half * SHARD : (half + 1) * SHARD, bits * block : (bits + 1) * block] = xs[pair * 2 + half][
                    :, owner_columns(block, bits)
                ]
        part[rows, :] = dot_rows(x[:, :block], ups[0][...]) + dot_rows(x[:, block : 2 * block], ups[1][...])
        x_tail[rows, :] = x[:, 2 * block :]
        x_turned[:, rows] = jnp.transpose(x[...])


def activate(pre):
    sig = jax.nn.sigmoid(pre)
    return (pre * sig).astype(BF16), sig * (1.0 + pre * (1.0 - sig))


def most_down_kernel(block, shards, *refs):
    gs, tables = refs[0:shards], refs[shards : shards + shards // 2]
    x_tail, part, up_y, up_d = refs[shards + shards // 2 : shards + shards // 2 + 4]
    g, act_turned, slope, *sums = refs[shards + shards // 2 + 4 :]
    expert = lax.axis_index("expert")
    for pair in range(shards // 2):
        rows = slice(pair * 2 * SHARD, (pair + 1) * 2 * SHARD)
        for half in range(2):
            own = slice((pair * 2 + half) * SHARD, (pair * 2 + half + 1) * SHARD)
            g[own, :] = scale_rows(pick_gate(tables[pair], half, expert), gs[pair * 2 + half][...])
        pre = part[rows, :] + dot_rows(x_tail[rows, :block], up_y[...]) + dot_rows(x_tail[rows, block:], up_d[...])
        act, slope[rows, :] = activate(pre)
        act_turned[:, rows] = jnp.transpose(act)
    for place in range(3):
        sums[place][...] = dot_rows(act_turned[...], g[:, place * block : (place + 1) * block])


def last_forward_kernel(block, *refs):
    shards, ups = refs[0:4], refs[4:8]
    x_turned, act_turned, slope, x = refs[8:]
    for half in range(2):
        for bits in range(4):
            cols = owner_columns(block, bits)
            x[half * SHARD : (half + 1) * SHARD, bits * block : (bits + 1) * block] = (
                shards[2 * half][:, cols] + shards[2 * half + 1][:, cols]
            )
    pre = dot_rows(x[:, :block], ups[0][...])
    for bits in (1, 2, 3):
        pre = pre + dot_rows(x[:, bits * block : (bits + 1) * block], ups[bits][...])
    x_turned[...] = jnp.transpose(x[...])
    act, slope[...] = activate(pre)
    act_turned[...] = jnp.transpose(act)


def last_far_kernel(block, *refs):
    shards, table, act_turned, far_sum = refs[0:4], refs[4], refs[5], refs[6]
    g, far_a, far_b = refs[7:]
    expert = lax.axis_index("expert")
    for half in range(2):
        gate = pick_gate(table, half, expert)
        g[half * SHARD : (half + 1) * SHARD, :] = scale_rows(gate, shards[2 * half][...] + shards[2 * half + 1][...])
    middle = act_turned.shape[0] // 2
    total = dot_rows(act_turned[...], g[:, :block]) + far_sum[...]
    far_a[...] = total[:middle].astype(BF16)
    far_b[...] = total[middle:].astype(BF16)


def last_near_kernel(block, *refs):
    g, act_turned, sum_x, sum_y = refs[:4]
    near_a, near_b, side_a, side_b = refs[4:]
    middle = act_turned.shape[0] // 2
    total = dot_rows(act_turned[...], g[:, block : 2 * block]) + sum_x[...]
    near_a[...] = total[:middle].astype(BF16)
    side_b[...] = total[middle:]
    total = dot_rows(act_turned[...], g[:, 2 * block :]) + sum_y[...]
    side_a[...] = total[:middle]
    near_b[...] = total[middle:].astype(BF16)


def early_backward_kernel(block, g, *refs):
    downs, part = refs[0:3], refs[3]
    for pair in range(g.shape[0] // (2 * SHARD)):
        rows = slice(pair * 2 * SHARD, (pair + 1) * 2 * SHARD)
        total = dot_last(g[rows, :block], downs[0][...])
        for place in (1, 2):
            total = total + dot_last(g[rows, place * block : (place + 1) * block], downs[place][...])
        part[rows, :] = total


def most_up_kernel(block, shards, *refs):
    gs, tables = refs[0:shards], refs[shards : shards + shards // 2]
    part, slope, x_turned, act_turned, down = refs[shards + shards // 2 : shards + shards // 2 + 5]
    sums, down_own = refs[shards + shards // 2 + 5 : shards + shards // 2 + 9], refs[shards + shards // 2 + 9]
    g, back = refs[shards + shards // 2 + 10 :]
    expert = lax.axis_index("expert")
    for pair in range(shards // 2):
        rows = slice(pair * 2 * SHARD, (pair + 1) * 2 * SHARD)
        for half in range(2):
            own = slice((pair * 2 + half) * SHARD, (pair * 2 + half + 1) * SHARD)
            g[own, :] = scale_rows(pick_gate(tables[pair], half, expert), gs[pair * 2 + half][...])
        back[rows, :] = ((part[rows, :] + dot_last(g[rows, :], down[...])) * slope[rows, :]).astype(BF16)
    for bits in range(4):
        sums[bits][...] = dot_rows(x_turned[bits * block : (bits + 1) * block, :], back[...])
    down_own[...] = dot_rows(act_turned[...], g[...])


def last_up_kernel(block, *refs):
    shards, table, g, slope, x_turned, act_turned = refs[0:2], refs[2], refs[3], refs[4], refs[5], refs[6]
    downs, sums, down_sum = refs[7:11], refs[11:15], refs[15]
    far_a, far_b, near_a, near_b, side_a, side_b, up_own, down_own = refs[16:24]
    kept, back = refs[24:]
    expert = lax.axis_index("expert")
    for half in range(2):
        gate = pick_gate(table, half, expert)
        kept[half * SHARD : (half + 1) * SHARD, :] = scale_rows(gate, shards[half][...])
    grad = dot_last(kept[...], downs[0][...])
    for place, bits in enumerate(SENT):
        grad = grad + dot_last(g[:, place * block : (place + 1) * block], downs[bits][...])
    back[...] = (grad * slope[...]).astype(BF16)
    middle = block // 2
    total = dot_rows(x_turned[3 * block :, :], back[...]) + sums[3][...]
    far_a[...] = total[:middle].astype(BF16)
    far_b[...] = total[middle:].astype(BF16)
    total = dot_rows(x_turned[block : 2 * block, :], back[...]) + sums[1][...]
    near_a[...] = total[:middle].astype(BF16)
    side_b[...] = total[middle:]
    total = dot_rows(x_turned[2 * block : 3 * block, :], back[...]) + sums[2][...]
    side_a[...] = total[:middle]
    near_b[...] = total[middle:].astype(BF16)
    up_own[...] = dot_rows(x_turned[:block, :], back[...]) + sums[0][...]
    down_own[...] = dot_rows(act_turned[...], kept[...]) + down_sum[...]


def finish_kernel(parts, near_sum, far_a, far_b, out, stage, sems):
    rows = near_sum.shape[0]
    step = rows // parts
    copies = []
    for i in range(parts):
        here = slice(i * step, (i + 1) * step)
        far, base = (far_a, 0) if i * 2 < parts else (far_b, rows // 2)
        got = far[i * step - base : (i + 1) * step - base, :]
        stage[here, :] = (near_sum[here, :] + got.astype(F32)).astype(BF16)
        copies.append(pltpu.make_async_copy(stage.at[pl.ds(i * step, step), :], out.at[pl.ds(i * step, step), :], sems.at[i]))
        copies[-1].start()
    for c in copies:
        c.wait()


def near_kernel(own, near_a, near_b, out):
    middle = own.shape[0] // 2
    out[:middle, :] = own[:middle, :] + near_a[...].astype(F32)
    out[middle:, :] = own[middle:, :] + near_b[...].astype(F32)


VMEM = pl.BlockSpec(memory_space=pltpu.VMEM)


def local_call(kernel, outs, args, scratch=(), flops=0):
    moved = sum(v.size * v.dtype.itemsize for v in (*args, *outs))
    return pl.pallas_call(
        kernel,
        out_shape=outs,
        in_specs=[VMEM] * len(args),
        out_specs=[VMEM] * len(outs),
        scratch_shapes=list(scratch),
        compiler_params=pltpu.CompilerParams(vmem_limit_bytes=GRANT * MIB),
        cost_estimate=pl.CostEstimate(flops=flops, bytes_accessed=moved, transcendentals=0),
    )(*args)


GRANT = 24


def shape(rows, cols, dtype):
    return jax.ShapeDtypeStruct((rows, cols), dtype)


def prepare(grad, tokens, up, down):
    rows, width = grad.shape
    block = width // 4
    outs = [shape(rows, 3 * block, BF16), shape(rows, block, BF16)] + [shape(*v.shape, BF16) for v in (tokens, up, down)]
    return local_call(functools.partial(prepare_kernel, block), outs, (grad, tokens, up, down))


def early_forward(xs, ups):
    block, hidden = ups[0].shape
    rows, width = len(xs) * SHARD, 4 * block
    return local_call(
        functools.partial(early_forward_kernel, block, len(xs)),
        [shape(rows, 2 * block, BF16), shape(width, rows, BF16), shape(rows, hidden, F32)],
        (*xs, *ups[:2]),
        [pltpu.VMEM((2 * SHARD, width), BF16)],
        flops=4 * rows * block * hidden,
    )


def most_down(gs, tables, x_tail, part, up_y, up_d):
    block, hidden = up_y.shape
    rows = len(gs) * SHARD
    return local_call(
        functools.partial(most_down_kernel, block, len(gs)),
        [shape(rows, 3 * block, BF16), shape(hidden, rows, BF16), shape(rows, hidden, F32)] + [shape(hidden, block, F32)] * 3,
        (*gs, *tables, x_tail, part, up_y, up_d),
        flops=10 * rows * block * hidden,
    )


def last_forward(shards, ups):
    block, hidden = ups[0].shape
    rows, width = 2 * SHARD, 4 * block
    return local_call(
        functools.partial(last_forward_kernel, block),
        [shape(width, rows, BF16), shape(hidden, rows, BF16), shape(rows, hidden, F32)],
        (*shards, *ups),
        [pltpu.VMEM((rows, width), BF16)],
        flops=2 * rows * width * hidden,
    )


def exchanged(rows, cols):
    return [shape(rows // 2, cols, BF16)] * 4 + [shape(rows // 2, cols, F32)] * 2


def last_far(shards, table, act_turned, far_sum):
    hidden, block = far_sum.shape
    return local_call(
        functools.partial(last_far_kernel, block),
        [shape(2 * SHARD, 3 * block, BF16)] + exchanged(hidden, block)[:2],
        (*shards, table, act_turned, far_sum),
        flops=4 * SHARD * block * hidden,
    )


def last_near(g, act_turned, sum_x, sum_y):
    hidden, block = sum_x.shape
    return local_call(
        functools.partial(last_near_kernel, block),
        exchanged(hidden, block)[2:],
        (g, act_turned, sum_x, sum_y),
        flops=8 * SHARD * block * hidden,
    )


def early_backward(g, downs):
    hidden, block = downs[0].shape
    rows = g.shape[0]
    return local_call(
        functools.partial(early_backward_kernel, block),
        [shape(rows, hidden, F32)],
        (g, *(downs[bits] for bits in SENT)),
        flops=6 * rows * block * hidden,
    )[0]


def most_up(gs, tables, part, slope, x_turned, act_turned, down):
    hidden, block = down.shape
    rows = len(gs) * SHARD
    got = local_call(
        functools.partial(most_up_kernel, block, len(gs)),
        [shape(block, hidden, F32)] * 4 + [shape(hidden, block, F32)],
        (*gs, *tables, part, slope, x_turned, act_turned, down),
        [pltpu.VMEM((rows, block), BF16), pltpu.VMEM((rows, hidden), BF16)],
        flops=12 * rows * block * hidden,
    )
    return got[:4], got[4]


def last_up(shards, table, g, slope, x_turned, act_turned, downs, sums, down_sum):
    hidden, block = downs[0].shape
    rows = 2 * SHARD
    return local_call(
        functools.partial(last_up_kernel, block),
        exchanged(block, hidden) + [shape(block, hidden, F32), shape(hidden, block, F32)],
        (*shards, table, g, slope, x_turned, act_turned, *downs, *sums, down_sum),
        [pltpu.VMEM((rows, block), BF16), pltpu.VMEM((rows, hidden), BF16)],
        flops=18 * rows * block * hidden,
    )


def with_near(own, near_a, near_b):
    return local_call(near_kernel, [shape(*own.shape, F32)], (own, near_a, near_b))[0]


def finish(near_sum, far_a, far_b):
    parts = 4
    return pl.pallas_call(
        functools.partial(finish_kernel, parts),
        out_shape=shape(*near_sum.shape, BF16),
        in_specs=[VMEM] * 3,
        out_specs=pl.BlockSpec(memory_space=pl.ANY),
        scratch_shapes=[pltpu.VMEM(near_sum.shape, BF16), pltpu.SemaphoreType.DMA((parts,))],
        compiler_params=pltpu.CompilerParams(vmem_limit_bytes=GRANT * MIB),
        cost_estimate=pl.CostEstimate(flops=near_sum.size, bytes_accessed=10 * near_sum.size, transcendentals=0),
    )(near_sum, far_a, far_b)


def dense_shards(tokens, grad_out, expert_ids, gate_q, w_up, w_down):
    return dense_body(tokens, grad_out, expert_ids, gate_q, w_up[0], w_down[0])


def dense_body(tokens, grad_out, expert_ids, gate_q, w_up, w_down):
    devices = lax.axis_size("expert")

    def ex(value, perm):
        return lax.ppermute(value, "expert", perm)

    def dp(value, bits):
        return lax.ppermute(value, "dp", xor_perm(4, bits))

    swap = xor_perm(devices, 1)

    def ring(hops):
        return [(i, (i + 2 * hops) % devices) for i in range(devices)]

    up_mid = [(i, i + 2) for i in range(2, devices - 2)]
    down_mid = [(i, i - 2) for i in range(2, devices - 2)]

    ga, gb, tokens_here, up_here, down_here = prepare(grad_out, tokens, w_up, w_down)

    t1 = ex(tokens, ring(1))
    t3 = ex(tokens, ring(-1))
    up_x = dp(w_up, 1)
    down_y = dp(w_down, 2)
    ga1 = ex(ga, ring(1))
    ga3 = ex(ga, ring(-1))
    up_y = dp(w_up, 2)
    down_x = dp(w_down, 1)

    experts = jnp.arange(devices, dtype=jnp.int32)
    named = expert_ids.T[None, :, :] == experts[:, None, None]
    gate_table = jnp.sum(jnp.where(named, gate_q.T[None, :, :], 0), axis=1).astype(F32) * (1.0 / 65536.0)
    c0 = jnp.concatenate([gate_table, ex(gate_table, swap)], axis=1)
    c1 = ex(c0, ring(1))
    c2 = ex(c0, ring(2))
    c3 = ex(c0, ring(3))
    t0b = ex(tokens, swap)
    ga0b = ex(ga, swap)
    gb0b = ex(gb, swap)

    up_d = dp(up_x, 2)
    down_d = dp(down_y, 1)
    t2u = ex(t1, up_mid)
    t2d = ex(t3, down_mid)
    t1b = ex(t1, swap)
    t3b = ex(t3, swap)
    ga2u = ex(ga1, up_mid)
    ga2d = ex(ga3, down_mid)
    ga1b = ex(ga1, swap)
    ga3b = ex(ga3, swap)
    gb1 = ex(gb, ring(1))
    gb3 = ex(gb, ring(-1))
    gb2 = ex(gb, ring(2))
    t2ub = ex(t2u, swap)
    t2db = ex(t2d, swap)
    ga2ub = ex(ga2u, swap)
    ga2db = ex(ga2d, swap)
    gb1b = ex(gb1, swap)
    gb3b = ex(gb3, swap)
    gb2b = ex(gb2, swap)

    ups = (up_here, up_x, up_y, up_d)
    downs = (down_here, down_x, down_y, down_d)
    tables = (c0, c1, c3)
    x_tail, x_turned, pre_part = early_forward((tokens_here, t0b, t1, t1b, t3, t3b), ups)
    g_ab, act_ab, slope_ab, *down_sums = most_down((ga, ga0b, ga1, ga1b, ga3, ga3b), tables, x_tail, pre_part, up_y, up_d)
    x_c, act_c, slope_c = last_forward((t2u, t2d, t2ub, t2db), ups)
    g_c, *down_far = last_far((ga2u, ga2d, ga2ub, ga2db), c2, act_c, down_sums[0])
    down_parts = (*down_far, *last_near(g_c, act_c, *down_sums[1:]))
    grad_part = early_backward(g_ab, downs)
    up_sums, down_sum = most_up((gb, gb0b, gb1, gb1b, gb3, gb3b), tables, grad_part, slope_ab, x_turned, act_ab, down_here)
    *up_parts, up_own, down_own = last_up((gb2, gb2b), c2, g_c, slope_c, x_c, act_c, downs, up_sums, down_sum)

    def exchange(far_a, far_b, near_a, near_b, side_a, side_b):
        far_a = dp(far_a, 1)
        far_b = dp(far_b, 2)
        near_a = dp(near_a, 1)
        near_b = dp(near_b, 2)
        side_a = (side_a + far_a.astype(F32)).astype(BF16)
        side_b = (side_b + far_b.astype(F32)).astype(BF16)
        return near_a, near_b, dp(side_a, 2), dp(side_b, 1)

    down_got = exchange(*down_parts)
    up_got = exchange(*up_parts)
    down_sum = with_near(down_own, *down_got[:2])
    dw_down = finish(down_sum, *down_got[2:])
    up_sum = with_near(up_own, *up_got[:2])
    dw_up = finish(up_sum, *up_got[2:])
    return dw_up[None], dw_down[None]


def shards(tokens, grad_out, expert_ids, gate_q, w_up, w_down):
    devices = lax.axis_size("expert")
    token_count, top_count = expert_ids.shape
    capacity = max(2, token_count * top_count * 3 // (2 * devices))
    if 2 * capacity >= token_count and devices == 8 and lax.axis_size("dp") == 4 and token_count == SHARD:
        return dense_shards(tokens, grad_out, expert_ids, gate_q, w_up, w_down)
    return sparse_shards(tokens, grad_out, expert_ids, gate_q, w_up, w_down, capacity)


def solution(mesh):
    in_specs = (
        P(("dp", "expert"), None),
        P(("dp", "expert"), None),
        P(("dp", "expert"), None),
        P(("dp", "expert"), None),
        P("expert", "dp", None),
        P("expert", None, "dp"),
    )
    out_specs = (P("expert", "dp", None), P("expert", None, "dp"))
    return jax.shard_map(shards, mesh=mesh, in_specs=in_specs, out_specs=out_specs, check_vma=False)
```

```python
import functools

import jax
import jax.numpy as jnp
from jax import lax
from jax.experimental import pallas as pl
from jax.experimental.pallas import tpu as pltpu
from jax.sharding import PartitionSpec as P


F32 = jnp.float32
BF16 = jnp.bfloat16
FIRST = (((0,), (0,)), ((), ()))
LAST = (((1,), (1,)), ((), ()))


def silu_slope(values):
    sigmoid_part = jax.nn.sigmoid(values)
    return sigmoid_part * (1.0 + values * (1.0 - sigmoid_part))


def summed_up(recv_rows, projected_grad):
    partial_value = lax.dot_general(recv_rows, projected_grad, FIRST, preferred_element_type=F32).astype(BF16)
    pieces = lax.all_to_all(partial_value[None], "dp", split_axis=1, concat_axis=0, tiled=True)
    return jnp.sum(pieces.astype(F32), axis=0, keepdims=True).astype(BF16)


def summed_down(activated, grad_rows):
    partial_value = lax.dot_general(activated, grad_rows, FIRST, preferred_element_type=F32).astype(BF16)
    pieces = lax.all_to_all(partial_value[None], "dp", split_axis=2, concat_axis=0, tiled=True)
    return jnp.sum(pieces.astype(F32), axis=0, keepdims=True).astype(BF16)


def sparse_shards(tokens, grad_out, expert_ids, gate_q, w_up, w_down, capacity):
    devices = lax.axis_size("expert")
    top_count = expert_ids.shape[1]
    model_width = tokens.shape[1]
    slot_expert = expert_ids.reshape(-1)
    onehot_table = (slot_expert[:, None] == jnp.arange(devices, dtype=jnp.int32)[None, :]).astype(jnp.int32)
    earlier = jnp.cumsum(onehot_table, axis=0) - onehot_table
    slot_rank = jnp.sum(earlier * onehot_table, axis=1)
    slot_target = slot_expert * capacity + slot_rank
    gate_values = gate_q.reshape(-1).astype(F32) * (1.0 / 65536.0)
    token_rows = jnp.repeat(tokens, top_count, axis=0)
    slot_grads = (gate_values[:, None] * jnp.repeat(grad_out, top_count, axis=0).astype(F32)).astype(BF16)
    empty_rows = jnp.zeros((devices * capacity, model_width), BF16)
    send_tokens = empty_rows.at[slot_target].set(token_rows).reshape(devices, capacity, model_width)
    grad_slots = empty_rows.at[slot_target].set(slot_grads).reshape(devices, capacity, model_width)
    up_whole = lax.all_gather(w_up, "dp", axis=1, tiled=True)[0]
    down_whole = lax.all_gather(w_down, "dp", axis=2, tiled=True)[0]
    recv_tokens = lax.all_to_all(send_tokens, "expert", split_axis=0, concat_axis=0, tiled=True)
    recv_rows = recv_tokens.reshape(-1, model_width)
    projected = jnp.dot(recv_rows, up_whole, preferred_element_type=F32)
    recv_grads = lax.all_to_all(grad_slots, "expert", split_axis=0, concat_axis=0, tiled=True)
    activated = jax.nn.silu(projected).astype(BF16)
    grad_rows = recv_grads.reshape(-1, model_width)
    act_grad = lax.dot_general(grad_rows, down_whole, LAST, preferred_element_type=F32)
    projected_grad = (act_grad * silu_slope(projected)).astype(BF16)
    return summed_up(recv_rows, projected_grad), summed_down(activated, grad_rows)


def xor_perm(count, bits):
    return [(i, i ^ bits) for i in range(count)]


MIB = 1 << 20


def pick_gate(table_ref, part, expert):
    table = table_ref[:, part * SHARD : (part + 1) * SHARD]
    mine = lax.broadcasted_iota(jnp.int32, table.shape, 0) == expert
    row = jnp.sum(jnp.where(mine, table, 0.0), axis=0, keepdims=True)
    return jnp.transpose(jnp.broadcast_to(row, (SHARD, SHARD)))


SHARD = 128


def scale_rows(gate, rows):
    wide = jnp.concatenate([gate] * (rows.shape[1] // gate.shape[1]), axis=1)
    return (wide * rows.astype(F32)).astype(BF16)


def dot_rows(left, right):
    return jnp.dot(left, right, preferred_element_type=F32)


def dot_last(left, right):
    return lax.dot_general(left, right, LAST, preferred_element_type=F32)


def owner_columns(block, bits):
    return pl.ds(pl.multiple_of((lax.axis_index("dp") ^ bits) * block, block), block)


SENT = (3, 1, 2)


def prepare_kernel(block, grad, tokens, up, down, sent, kept, tokens_copy, up_copy, down_copy):
    for place, bits in enumerate(SENT):
        sent[:, place * block : (place + 1) * block] = grad[:, owner_columns(block, bits)]
    kept[...] = grad[:, owner_columns(block, 0)]
    tokens_copy[...] = tokens[...]
    up_copy[...] = up[...]
    down_copy[...] = down[...]


def early_forward_kernel(block, shards, *refs):
    xs, ups = refs[0:shards], refs[shards : shards + 2]
    x_tail, x_turned, part = refs[shards + 2 : shards + 5]
    x = refs[shards + 5]
    for pair in range(shards // 2):
        rows = slice(pair * 2 * SHARD, (pair + 1) * 2 * SHARD)
        for half in range(2):
            for bits in range(4):
                x[half * SHARD : (half + 1) * SHARD, bits * block : (bits + 1) * block] = xs[pair * 2 + half][
                    :, owner_columns(block, bits)
                ]
        part[rows, :] = dot_rows(x[:, :block], ups[0][...]) + dot_rows(x[:, block : 2 * block], ups[1][...])
        x_tail[rows, :] = x[:, 2 * block :]
        x_turned[:, rows] = jnp.transpose(x[...])


def activate(pre):
    sig = jax.nn.sigmoid(pre)
    return (pre * sig).astype(BF16), sig * (1.0 + pre * (1.0 - sig))


def most_down_kernel(block, shards, *refs):
    gs, tables = refs[0:shards], refs[shards : shards + shards // 2]
    x_tail, part, up_y, up_d = refs[shards + shards // 2 : shards + shards // 2 + 4]
    g, act_turned, slope, *sums = refs[shards + shards // 2 + 4 :]
    expert = lax.axis_index("expert")
    for pair in range(shards // 2):
        rows = slice(pair * 2 * SHARD, (pair + 1) * 2 * SHARD)
        for half in range(2):
            own = slice((pair * 2 + half) * SHARD, (pair * 2 + half + 1) * SHARD)
            g[own, :] = scale_rows(pick_gate(tables[pair], half, expert), gs[pair * 2 + half][...])
        pre = part[rows, :] + dot_rows(x_tail[rows, :block], up_y[...]) + dot_rows(x_tail[rows, block:], up_d[...])
        act, slope[rows, :] = activate(pre)
        act_turned[:, rows] = jnp.transpose(act)
    for place in range(3):
        sums[place][...] = dot_rows(act_turned[...], g[:, place * block : (place + 1) * block])


def merge_kernel(upper, lower, out):
    out[...] = upper[...] + lower[...]


def last_forward_kernel(block, *refs):
    shards, ups = refs[0:2], refs[2:6]
    x_turned, act_turned, slope, x = refs[6:]
    for half in range(2):
        for bits in range(4):
            x[half * SHARD : (half + 1) * SHARD, bits * block : (bits + 1) * block] = shards[half][:, owner_columns(block, bits)]
    pre = dot_rows(x[:, :block], ups[0][...])
    for bits in (1, 2, 3):
        pre = pre + dot_rows(x[:, bits * block : (bits + 1) * block], ups[bits][...])
    x_turned[...] = jnp.transpose(x[...])
    act, slope[...] = activate(pre)
    act_turned[...] = jnp.transpose(act)


def last_far_kernel(block, *refs):
    shards, table, act_turned, far_sum = refs[0:2], refs[2], refs[3], refs[4]
    g, far_a, far_b = refs[5:]
    expert = lax.axis_index("expert")
    for half in range(2):
        g[half * SHARD : (half + 1) * SHARD, :] = scale_rows(pick_gate(table, half, expert), shards[half][...])
    middle = act_turned.shape[0] // 2
    total = dot_rows(act_turned[...], g[:, :block]) + far_sum[...]
    far_a[...] = total[:middle].astype(BF16)
    far_b[...] = total[middle:].astype(BF16)


def last_near_kernel(block, *refs):
    g, act_turned, sum_x, sum_y = refs[:4]
    near_a, near_b, side_a, side_b = refs[4:]
    middle = act_turned.shape[0] // 2
    total = dot_rows(act_turned[...], g[:, block : 2 * block]) + sum_x[...]
    near_a[...] = total[:middle].astype(BF16)
    side_b[...] = total[middle:]
    total = dot_rows(act_turned[...], g[:, 2 * block :]) + sum_y[...]
    side_a[...] = total[:middle]
    near_b[...] = total[middle:].astype(BF16)


def early_backward_kernel(block, g, *refs):
    downs, part = refs[0:3], refs[3]
    for pair in range(g.shape[0] // (2 * SHARD)):
        rows = slice(pair * 2 * SHARD, (pair + 1) * 2 * SHARD)
        total = dot_last(g[rows, :block], downs[0][...])
        for place in (1, 2):
            total = total + dot_last(g[rows, place * block : (place + 1) * block], downs[place][...])
        part[rows, :] = total


def most_up_kernel(block, shards, *refs):
    gs, tables = refs[0:shards], refs[shards : shards + shards // 2]
    part, slope, x_turned, act_turned, down = refs[shards + shards // 2 : shards + shards // 2 + 5]
    sums, down_own = refs[shards + shards // 2 + 5 : shards + shards // 2 + 9], refs[shards + shards // 2 + 9]
    g, back = refs[shards + shards // 2 + 10 :]
    expert = lax.axis_index("expert")
    for pair in range(shards // 2):
        rows = slice(pair * 2 * SHARD, (pair + 1) * 2 * SHARD)
        for half in range(2):
            own = slice((pair * 2 + half) * SHARD, (pair * 2 + half + 1) * SHARD)
            g[own, :] = scale_rows(pick_gate(tables[pair], half, expert), gs[pair * 2 + half][...])
        back[rows, :] = ((part[rows, :] + dot_last(g[rows, :], down[...])) * slope[rows, :]).astype(BF16)
    for bits in range(4):
        sums[bits][...] = dot_rows(x_turned[bits * block : (bits + 1) * block, :], back[...])
    down_own[...] = dot_rows(act_turned[...], g[...])


def last_up_kernel(block, *refs):
    shards, table, g, slope, x_turned, act_turned = refs[0:2], refs[2], refs[3], refs[4], refs[5], refs[6]
    downs, sums, down_sum = refs[7:11], refs[11:15], refs[15]
    far_a, far_b, near_a, near_b, side_a, side_b, up_own, down_own = refs[16:24]
    kept, back = refs[24:]
    expert = lax.axis_index("expert")
    for half in range(2):
        gate = pick_gate(table, half, expert)
        kept[half * SHARD : (half + 1) * SHARD, :] = scale_rows(gate, shards[half][...])
    grad = dot_last(kept[...], downs[0][...])
    for place, bits in enumerate(SENT):
        grad = grad + dot_last(g[:, place * block : (place + 1) * block], downs[bits][...])
    back[...] = (grad * slope[...]).astype(BF16)
    middle = block // 2
    total = dot_rows(x_turned[3 * block :, :], back[...]) + sums[3][...]
    far_a[...] = total[:middle].astype(BF16)
    far_b[...] = total[middle:].astype(BF16)
    total = dot_rows(x_turned[block : 2 * block, :], back[...]) + sums[1][...]
    near_a[...] = total[:middle].astype(BF16)
    side_b[...] = total[middle:]
    total = dot_rows(x_turned[2 * block : 3 * block, :], back[...]) + sums[2][...]
    side_a[...] = total[:middle]
    near_b[...] = total[middle:].astype(BF16)
    up_own[...] = dot_rows(x_turned[:block, :], back[...]) + sums[0][...]
    down_own[...] = dot_rows(act_turned[...], kept[...]) + down_sum[...]


def finish_kernel(parts, near_sum, far_a, far_b, out, stage, sems):
    rows = near_sum.shape[0]
    step = rows // parts
    copies = []
    for i in range(parts):
        here = slice(i * step, (i + 1) * step)
        far, base = (far_a, 0) if i * 2 < parts else (far_b, rows // 2)
        got = far[i * step - base : (i + 1) * step - base, :]
        stage[here, :] = (near_sum[here, :] + got.astype(F32)).astype(BF16)
        copies.append(pltpu.make_async_copy(stage.at[pl.ds(i * step, step), :], out.at[pl.ds(i * step, step), :], sems.at[i]))
        copies[-1].start()
    for c in copies:
        c.wait()


def near_kernel(own, near_a, near_b, out):
    middle = own.shape[0] // 2
    out[:middle, :] = own[:middle, :] + near_a[...].astype(F32)
    out[middle:, :] = own[middle:, :] + near_b[...].astype(F32)


VMEM = pl.BlockSpec(memory_space=pltpu.VMEM)


def local_call(kernel, outs, args, scratch=(), flops=0):
    moved = sum(v.size * v.dtype.itemsize for v in (*args, *outs))
    return pl.pallas_call(
        kernel,
        out_shape=outs,
        in_specs=[VMEM] * len(args),
        out_specs=[VMEM] * len(outs),
        scratch_shapes=list(scratch),
        compiler_params=pltpu.CompilerParams(vmem_limit_bytes=GRANT * MIB),
        cost_estimate=pl.CostEstimate(flops=flops, bytes_accessed=moved, transcendentals=0),
    )(*args)


GRANT = 24


def shape(rows, cols, dtype):
    return jax.ShapeDtypeStruct((rows, cols), dtype)


def prepare(grad, tokens, up, down):
    rows, width = grad.shape
    block = width // 4
    outs = [shape(rows, 3 * block, BF16), shape(rows, block, BF16)] + [shape(*v.shape, BF16) for v in (tokens, up, down)]
    return local_call(functools.partial(prepare_kernel, block), outs, (grad, tokens, up, down))


def early_forward(xs, ups):
    block, hidden = ups[0].shape
    rows, width = len(xs) * SHARD, 4 * block
    return local_call(
        functools.partial(early_forward_kernel, block, len(xs)),
        [shape(rows, 2 * block, BF16), shape(width, rows, BF16), shape(rows, hidden, F32)],
        (*xs, *ups[:2]),
        [pltpu.VMEM((2 * SHARD, width), BF16)],
        flops=4 * rows * block * hidden,
    )


def most_down(gs, tables, x_tail, part, up_y, up_d):
    block, hidden = up_y.shape
    rows = len(gs) * SHARD
    return local_call(
        functools.partial(most_down_kernel, block, len(gs)),
        [shape(rows, 3 * block, BF16), shape(hidden, rows, BF16), shape(rows, hidden, F32)] + [shape(hidden, block, F32)] * 3,
        (*gs, *tables, x_tail, part, up_y, up_d),
        flops=10 * rows * block * hidden,
    )


def merged(upper, lower):
    return local_call(merge_kernel, [shape(*upper.shape, BF16)], (upper, lower))[0]


def last_forward(shards, ups):
    block, hidden = ups[0].shape
    rows, width = 2 * SHARD, 4 * block
    return local_call(
        functools.partial(last_forward_kernel, block),
        [shape(width, rows, BF16), shape(hidden, rows, BF16), shape(rows, hidden, F32)],
        (*shards, *ups),
        [pltpu.VMEM((rows, width), BF16)],
        flops=2 * rows * width * hidden,
    )


def exchanged(rows, cols):
    return [shape(rows // 2, cols, BF16)] * 4 + [shape(rows // 2, cols, F32)] * 2


def last_far(shards, table, act_turned, far_sum):
    hidden, block = far_sum.shape
    return local_call(
        functools.partial(last_far_kernel, block),
        [shape(2 * SHARD, 3 * block, BF16)] + exchanged(hidden, block)[:2],
        (*shards, table, act_turned, far_sum),
        flops=4 * SHARD * block * hidden,
    )


def last_near(g, act_turned, sum_x, sum_y):
    hidden, block = sum_x.shape
    return local_call(
        functools.partial(last_near_kernel, block),
        exchanged(hidden, block)[2:],
        (g, act_turned, sum_x, sum_y),
        flops=8 * SHARD * block * hidden,
    )


def early_backward(g, downs):
    hidden, block = downs[0].shape
    rows = g.shape[0]
    return local_call(
        functools.partial(early_backward_kernel, block),
        [shape(rows, hidden, F32)],
        (g, *(downs[bits] for bits in SENT)),
        flops=6 * rows * block * hidden,
    )[0]


def most_up(gs, tables, part, slope, x_turned, act_turned, down):
    hidden, block = down.shape
    rows = len(gs) * SHARD
    got = local_call(
        functools.partial(most_up_kernel, block, len(gs)),
        [shape(block, hidden, F32)] * 4 + [shape(hidden, block, F32)],
        (*gs, *tables, part, slope, x_turned, act_turned, down),
        [pltpu.VMEM((rows, block), BF16), pltpu.VMEM((rows, hidden), BF16)],
        flops=12 * rows * block * hidden,
    )
    return got[:4], got[4]


def last_up(shards, table, g, slope, x_turned, act_turned, downs, sums, down_sum):
    hidden, block = downs[0].shape
    rows = 2 * SHARD
    return local_call(
        functools.partial(last_up_kernel, block),
        exchanged(block, hidden) + [shape(block, hidden, F32), shape(hidden, block, F32)],
        (*shards, table, g, slope, x_turned, act_turned, *downs, *sums, down_sum),
        [pltpu.VMEM((rows, block), BF16), pltpu.VMEM((rows, hidden), BF16)],
        flops=18 * rows * block * hidden,
    )


def with_near(own, near_a, near_b):
    return local_call(near_kernel, [shape(*own.shape, F32)], (own, near_a, near_b))[0]


def finish(near_sum, far_a, far_b):
    parts = 4
    return pl.pallas_call(
        functools.partial(finish_kernel, parts),
        out_shape=shape(*near_sum.shape, BF16),
        in_specs=[VMEM] * 3,
        out_specs=pl.BlockSpec(memory_space=pl.ANY),
        scratch_shapes=[pltpu.VMEM(near_sum.shape, BF16), pltpu.SemaphoreType.DMA((parts,))],
        compiler_params=pltpu.CompilerParams(vmem_limit_bytes=GRANT * MIB),
        cost_estimate=pl.CostEstimate(flops=near_sum.size, bytes_accessed=10 * near_sum.size, transcendentals=0),
    )(near_sum, far_a, far_b)


def dense_shards(tokens, grad_out, expert_ids, gate_q, w_up, w_down):
    return dense_body(tokens, grad_out, expert_ids, gate_q, w_up[0], w_down[0])


def dense_body(tokens, grad_out, expert_ids, gate_q, w_up, w_down):
    devices = lax.axis_size("expert")

    def ex(value, perm):
        return lax.ppermute(value, "expert", perm)

    def dp(value, bits):
        return lax.ppermute(value, "dp", xor_perm(4, bits))

    swap = xor_perm(devices, 1)

    def ring(hops):
        return [(i, (i + 2 * hops) % devices) for i in range(devices)]

    up_mid = [(i, i + 2) for i in range(2, devices - 2)]
    down_mid = [(i, i - 2) for i in range(2, devices - 2)]

    ga, gb, tokens_here, up_here, down_here = prepare(grad_out, tokens, w_up, w_down)

    t1 = ex(tokens, ring(1))
    t3 = ex(tokens, ring(-1))
    up_x = dp(w_up, 1)
    down_y = dp(w_down, 2)
    ga1 = ex(ga, ring(1))
    ga3 = ex(ga, ring(-1))
    up_y = dp(w_up, 2)
    down_x = dp(w_down, 1)

    experts = jnp.arange(devices, dtype=jnp.int32)
    named = expert_ids.T[None, :, :] == experts[:, None, None]
    gate_table = jnp.sum(jnp.where(named, gate_q.T[None, :, :], 0), axis=1).astype(F32) * (1.0 / 65536.0)
    c0 = jnp.concatenate([gate_table, ex(gate_table, swap)], axis=1)
    c1 = ex(c0, ring(1))
    c2 = ex(c0, ring(2))
    c3 = ex(c0, ring(3))
    t0b = ex(tokens, swap)
    ga0b = ex(ga, swap)
    gb0b = ex(gb, swap)

    up_d = dp(up_x, 2)
    down_d = dp(down_y, 1)
    t2u = ex(t1, up_mid)
    t2d = ex(t3, down_mid)
    t1b = ex(t1, swap)
    t3b = ex(t3, swap)
    ga2u = ex(ga1, up_mid)
    ga2d = ex(ga3, down_mid)
    ga1b = ex(ga1, swap)
    ga3b = ex(ga3, swap)
    gb1 = ex(gb, ring(1))
    gb3 = ex(gb, ring(-1))
    gb2 = ex(gb, ring(2))
    t2 = merged(t2u, t2d)
    t2b = ex(t2, swap)
    ga2 = merged(ga2u, ga2d)
    ga2b = ex(ga2, swap)
    gb1b = ex(gb1, swap)
    gb3b = ex(gb3, swap)
    gb2b = ex(gb2, swap)

    ups = (up_here, up_x, up_y, up_d)
    downs = (down_here, down_x, down_y, down_d)
    tables = (c0, c1, c3)
    x_tail, x_turned, pre_part = early_forward((tokens_here, t0b, t1, t1b, t3, t3b), ups)
    g_ab, act_ab, slope_ab, *down_sums = most_down((ga, ga0b, ga1, ga1b, ga3, ga3b), tables, x_tail, pre_part, up_y, up_d)
    x_c, act_c, slope_c = last_forward((t2, t2b), ups)
    g_c, *down_far = last_far((ga2, ga2b), c2, act_c, down_sums[0])
    down_parts = (*down_far, *last_near(g_c, act_c, *down_sums[1:]))
    grad_part = early_backward(g_ab, downs)
    up_sums, down_sum = most_up((gb, gb0b, gb1, gb1b, gb3, gb3b), tables, grad_part, slope_ab, x_turned, act_ab, down_here)
    *up_parts, up_own, down_own = last_up((gb2, gb2b), c2, g_c, slope_c, x_c, act_c, downs, up_sums, down_sum)

    def exchange(far_a, far_b, near_a, near_b, side_a, side_b):
        far_a = dp(far_a, 1)
        far_b = dp(far_b, 2)
        near_a = dp(near_a, 1)
        near_b = dp(near_b, 2)
        side_a = (side_a + far_a.astype(F32)).astype(BF16)
        side_b = (side_b + far_b.astype(F32)).astype(BF16)
        return near_a, near_b, dp(side_a, 2), dp(side_b, 1)

    down_got = exchange(*down_parts)
    up_got = exchange(*up_parts)
    down_sum = with_near(down_own, *down_got[:2])
    dw_down = finish(down_sum, *down_got[2:])
    up_sum = with_near(up_own, *up_got[:2])
    dw_up = finish(up_sum, *up_got[2:])
    return dw_up[None], dw_down[None]


def shards(tokens, grad_out, expert_ids, gate_q, w_up, w_down):
    devices = lax.axis_size("expert")
    token_count, top_count = expert_ids.shape
    capacity = max(2, token_count * top_count * 3 // (2 * devices))
    if 2 * capacity >= token_count and devices == 8 and lax.axis_size("dp") == 4 and token_count == SHARD:
        return dense_shards(tokens, grad_out, expert_ids, gate_q, w_up, w_down)
    return sparse_shards(tokens, grad_out, expert_ids, gate_q, w_up, w_down, capacity)


def solution(mesh):
    in_specs = (
        P(("dp", "expert"), None),
        P(("dp", "expert"), None),
        P(("dp", "expert"), None),
        P(("dp", "expert"), None),
        P("expert", "dp", None),
        P("expert", None, "dp"),
    )
    out_specs = (P("expert", "dp", None), P("expert", None, "dp"))
    return jax.shard_map(shards, mesh=mesh, in_specs=in_specs, out_specs=out_specs, check_vma=False)
```

```python
import functools

import jax
import jax.numpy as jnp
from jax import lax
from jax.experimental import pallas as pl
from jax.experimental.pallas import tpu as pltpu
from jax.sharding import PartitionSpec as P


F32 = jnp.float32
BF16 = jnp.bfloat16
FIRST = (((0,), (0,)), ((), ()))
LAST = (((1,), (1,)), ((), ()))


def silu_slope(values):
    sigmoid_part = jax.nn.sigmoid(values)
    return sigmoid_part * (1.0 + values * (1.0 - sigmoid_part))


def summed_up(recv_rows, projected_grad):
    partial_value = lax.dot_general(recv_rows, projected_grad, FIRST, preferred_element_type=F32).astype(BF16)
    pieces = lax.all_to_all(partial_value[None], "dp", split_axis=1, concat_axis=0, tiled=True)
    return jnp.sum(pieces.astype(F32), axis=0, keepdims=True).astype(BF16)


def summed_down(activated, grad_rows):
    partial_value = lax.dot_general(activated, grad_rows, FIRST, preferred_element_type=F32).astype(BF16)
    pieces = lax.all_to_all(partial_value[None], "dp", split_axis=2, concat_axis=0, tiled=True)
    return jnp.sum(pieces.astype(F32), axis=0, keepdims=True).astype(BF16)


def sparse_shards(tokens, grad_out, expert_ids, gate_q, w_up, w_down, capacity):
    devices = lax.axis_size("expert")
    top_count = expert_ids.shape[1]
    model_width = tokens.shape[1]
    slot_expert = expert_ids.reshape(-1)
    onehot_table = (slot_expert[:, None] == jnp.arange(devices, dtype=jnp.int32)[None, :]).astype(jnp.int32)
    earlier = jnp.cumsum(onehot_table, axis=0) - onehot_table
    slot_rank = jnp.sum(earlier * onehot_table, axis=1)
    slot_target = slot_expert * capacity + slot_rank
    gate_values = gate_q.reshape(-1).astype(F32) * (1.0 / 65536.0)
    token_rows = jnp.repeat(tokens, top_count, axis=0)
    slot_grads = (gate_values[:, None] * jnp.repeat(grad_out, top_count, axis=0).astype(F32)).astype(BF16)
    empty_rows = jnp.zeros((devices * capacity, model_width), BF16)
    send_tokens = empty_rows.at[slot_target].set(token_rows).reshape(devices, capacity, model_width)
    grad_slots = empty_rows.at[slot_target].set(slot_grads).reshape(devices, capacity, model_width)
    up_whole = lax.all_gather(w_up, "dp", axis=1, tiled=True)[0]
    down_whole = lax.all_gather(w_down, "dp", axis=2, tiled=True)[0]
    recv_tokens = lax.all_to_all(send_tokens, "expert", split_axis=0, concat_axis=0, tiled=True)
    recv_rows = recv_tokens.reshape(-1, model_width)
    projected = jnp.dot(recv_rows, up_whole, preferred_element_type=F32)
    recv_grads = lax.all_to_all(grad_slots, "expert", split_axis=0, concat_axis=0, tiled=True)
    activated = jax.nn.silu(projected).astype(BF16)
    grad_rows = recv_grads.reshape(-1, model_width)
    act_grad = lax.dot_general(grad_rows, down_whole, LAST, preferred_element_type=F32)
    projected_grad = (act_grad * silu_slope(projected)).astype(BF16)
    return summed_up(recv_rows, projected_grad), summed_down(activated, grad_rows)


def xor_perm(count, bits):
    return [(i, i ^ bits) for i in range(count)]


MIB = 1 << 20


def pick_gate(table_ref, part, expert):
    table = table_ref[:, part * SHARD : (part + 1) * SHARD]
    mine = lax.broadcasted_iota(jnp.int32, table.shape, 0) == expert
    row = jnp.sum(jnp.where(mine, table, 0.0), axis=0, keepdims=True)
    return jnp.transpose(jnp.broadcast_to(row, (SHARD, SHARD)))


SHARD = 128


def scale_rows(gate, rows):
    wide = jnp.concatenate([gate] * (rows.shape[1] // gate.shape[1]), axis=1)
    return (wide * rows.astype(F32)).astype(BF16)


def dot_rows(left, right):
    return jnp.dot(left, right, preferred_element_type=F32)


def dot_last(left, right):
    return lax.dot_general(left, right, LAST, preferred_element_type=F32)


def first_part(rows):
    return rows // 2 + rows // 24 // 32 * 32


def owner_columns(block, bits):
    return pl.ds(pl.multiple_of((lax.axis_index("dp") ^ bits) * block, block), block)


SENT = (3, 1, 2)


def prepare_kernel(block, grad, tokens, up, down, sent, kept, tokens_copy, up_copy, down_copy):
    for place, bits in enumerate(SENT):
        sent[:, place * block : (place + 1) * block] = grad[:, owner_columns(block, bits)]
    kept[...] = grad[:, owner_columns(block, 0)]
    tokens_copy[...] = tokens[...]
    up_copy[...] = up[...]
    down_copy[...] = down[...]


def early_forward_kernel(block, shards, *refs):
    xs, ups = refs[0:shards], refs[shards : shards + 2]
    x_tail, x_turned, part = refs[shards + 2 : shards + 5]
    x = refs[shards + 5]
    for pair in range(shards // 2):
        rows = slice(pair * 2 * SHARD, (pair + 1) * 2 * SHARD)
        for half in range(2):
            for bits in range(4):
                x[half * SHARD : (half + 1) * SHARD, bits * block : (bits + 1) * block] = xs[pair * 2 + half][
                    :, owner_columns(block, bits)
                ]
        part[rows, :] = dot_rows(x[:, :block], ups[0][...]) + dot_rows(x[:, block : 2 * block], ups[1][...])
        x_tail[rows, :] = x[:, 2 * block :]
        x_turned[:, rows] = jnp.transpose(x[...])


def activate(pre):
    sig = jax.nn.sigmoid(pre)
    return (pre * sig).astype(BF16), sig * (1.0 + pre * (1.0 - sig))


def most_down_kernel(block, shards, *refs):
    gs, tables = refs[0:shards], refs[shards : shards + shards // 2]
    x_tail, part, up_y, up_d = refs[shards + shards // 2 : shards + shards // 2 + 4]
    g, act_turned, slope, *sums = refs[shards + shards // 2 + 4 :]
    expert = lax.axis_index("expert")
    for pair in range(shards // 2):
        rows = slice(pair * 2 * SHARD, (pair + 1) * 2 * SHARD)
        for half in range(2):
            own = slice((pair * 2 + half) * SHARD, (pair * 2 + half + 1) * SHARD)
            g[own, :] = scale_rows(pick_gate(tables[pair], half, expert), gs[pair * 2 + half][...])
        pre = part[rows, :] + dot_rows(x_tail[rows, :block], up_y[...]) + dot_rows(x_tail[rows, block:], up_d[...])
        act, slope[rows, :] = activate(pre)
        act_turned[:, rows] = jnp.transpose(act)
    for place in range(3):
        sums[place][...] = dot_rows(act_turned[...], g[:, place * block : (place + 1) * block])


def merge_kernel(upper, lower, out):
    out[...] = upper[...] + lower[...]


def last_forward_kernel(block, *refs):
    shards, ups = refs[0:2], refs[2:6]
    x_turned, act_turned, slope, x = refs[6:]
    for half in range(2):
        for bits in range(4):
            x[half * SHARD : (half + 1) * SHARD, bits * block : (bits + 1) * block] = shards[half][:, owner_columns(block, bits)]
    pre = dot_rows(x[:, :block], ups[0][...])
    for bits in (1, 2, 3):
        pre = pre + dot_rows(x[:, bits * block : (bits + 1) * block], ups[bits][...])
    x_turned[...] = jnp.transpose(x[...])
    act, slope[...] = activate(pre)
    act_turned[...] = jnp.transpose(act)


def last_far_kernel(block, *refs):
    shards, table, act_turned, far_sum = refs[0:2], refs[2], refs[3], refs[4]
    g, far_a, far_b = refs[5:]
    expert = lax.axis_index("expert")
    for half in range(2):
        g[half * SHARD : (half + 1) * SHARD, :] = scale_rows(pick_gate(table, half, expert), shards[half][...])
    middle = first_part(act_turned.shape[0])
    total = dot_rows(act_turned[...], g[:, :block]) + far_sum[...]
    far_a[...] = total[:middle].astype(BF16)
    far_b[...] = total[middle:].astype(BF16)


def last_near_kernel(block, *refs):
    g, act_turned, sum_x, sum_y = refs[:4]
    near_a, near_b, side_a, side_b = refs[4:]
    middle = first_part(act_turned.shape[0])
    total = dot_rows(act_turned[...], g[:, block : 2 * block]) + sum_x[...]
    near_a[...] = total[:middle].astype(BF16)
    side_b[...] = total[middle:]
    total = dot_rows(act_turned[...], g[:, 2 * block :]) + sum_y[...]
    side_a[...] = total[:middle]
    near_b[...] = total[middle:].astype(BF16)


def early_backward_kernel(block, g, *refs):
    downs, part = refs[0:3], refs[3]
    for pair in range(g.shape[0] // (2 * SHARD)):
        rows = slice(pair * 2 * SHARD, (pair + 1) * 2 * SHARD)
        total = dot_last(g[rows, :block], downs[0][...])
        for place in (1, 2):
            total = total + dot_last(g[rows, place * block : (place + 1) * block], downs[place][...])
        part[rows, :] = total


def most_up_kernel(block, shards, *refs):
    gs, tables = refs[0:shards], refs[shards : shards + shards // 2]
    part, slope, x_turned, act_turned, down = refs[shards + shards // 2 : shards + shards // 2 + 5]
    sums, down_own = refs[shards + shards // 2 + 5 : shards + shards // 2 + 9], refs[shards + shards // 2 + 9]
    g, back = refs[shards + shards // 2 + 10 :]
    expert = lax.axis_index("expert")
    for pair in range(shards // 2):
        rows = slice(pair * 2 * SHARD, (pair + 1) * 2 * SHARD)
        for half in range(2):
            own = slice((pair * 2 + half) * SHARD, (pair * 2 + half + 1) * SHARD)
            g[own, :] = scale_rows(pick_gate(tables[pair], half, expert), gs[pair * 2 + half][...])
        back[rows, :] = ((part[rows, :] + dot_last(g[rows, :], down[...])) * slope[rows, :]).astype(BF16)
    for bits in range(4):
        sums[bits][...] = dot_rows(x_turned[bits * block : (bits + 1) * block, :], back[...])
    down_own[...] = dot_rows(act_turned[...], g[...])


def last_up_kernel(block, *refs):
    shards, table, g, slope, x_turned, act_turned = refs[0:2], refs[2], refs[3], refs[4], refs[5], refs[6]
    downs, sums, down_sum = refs[7:11], refs[11:15], refs[15]
    far_a, far_b, near_a, near_b, side_a, side_b, up_own, down_own = refs[16:24]
    kept, back = refs[24:]
    expert = lax.axis_index("expert")
    for half in range(2):
        gate = pick_gate(table, half, expert)
        kept[half * SHARD : (half + 1) * SHARD, :] = scale_rows(gate, shards[half][...])
    grad = dot_last(kept[...], downs[0][...])
    for place, bits in enumerate(SENT):
        grad = grad + dot_last(g[:, place * block : (place + 1) * block], downs[bits][...])
    back[...] = (grad * slope[...]).astype(BF16)
    middle = first_part(block)
    total = dot_rows(x_turned[3 * block :, :], back[...]) + sums[3][...]
    far_a[...] = total[:middle].astype(BF16)
    far_b[...] = total[middle:].astype(BF16)
    total = dot_rows(x_turned[block : 2 * block, :], back[...]) + sums[1][...]
    near_a[...] = total[:middle].astype(BF16)
    side_b[...] = total[middle:]
    total = dot_rows(x_turned[2 * block : 3 * block, :], back[...]) + sums[2][...]
    side_a[...] = total[:middle]
    near_b[...] = total[middle:].astype(BF16)
    up_own[...] = dot_rows(x_turned[:block, :], back[...]) + sums[0][...]
    down_own[...] = dot_rows(act_turned[...], kept[...]) + down_sum[...]


def finish_kernel(near_sum, far_a, far_b, out, stage, sems):
    rows = near_sum.shape[0]
    middle = first_part(rows)
    copies = []
    for far, start, end in ((far_a, 0, middle), (far_b, middle, rows)):
        step = (end - start) // 2
        for i in range(2):
            here = slice(start + i * step, start + (i + 1) * step)
            stage[here, :] = (near_sum[here, :] + far[i * step : (i + 1) * step, :].astype(F32)).astype(BF16)
            place = pl.ds(start + i * step, step)
            copies.append(pltpu.make_async_copy(stage.at[place, :], out.at[place, :], sems.at[len(copies)]))
            copies[-1].start()
    for c in copies:
        c.wait()


def near_kernel(own, near_a, near_b, out):
    middle = first_part(own.shape[0])
    out[:middle, :] = own[:middle, :] + near_a[...].astype(F32)
    out[middle:, :] = own[middle:, :] + near_b[...].astype(F32)


VMEM = pl.BlockSpec(memory_space=pltpu.VMEM)


def local_call(kernel, outs, args, scratch=(), flops=0):
    moved = sum(v.size * v.dtype.itemsize for v in (*args, *outs))
    return pl.pallas_call(
        kernel,
        out_shape=outs,
        in_specs=[VMEM] * len(args),
        out_specs=[VMEM] * len(outs),
        scratch_shapes=list(scratch),
        compiler_params=pltpu.CompilerParams(vmem_limit_bytes=GRANT * MIB),
        cost_estimate=pl.CostEstimate(flops=flops, bytes_accessed=moved, transcendentals=0),
    )(*args)


GRANT = 24


def shape(rows, cols, dtype):
    return jax.ShapeDtypeStruct((rows, cols), dtype)


def prepare(grad, tokens, up, down):
    rows, width = grad.shape
    block = width // 4
    outs = [shape(rows, 3 * block, BF16), shape(rows, block, BF16)] + [shape(*v.shape, BF16) for v in (tokens, up, down)]
    return local_call(functools.partial(prepare_kernel, block), outs, (grad, tokens, up, down))


def early_forward(xs, ups):
    block, hidden = ups[0].shape
    rows, width = len(xs) * SHARD, 4 * block
    return local_call(
        functools.partial(early_forward_kernel, block, len(xs)),
        [shape(rows, 2 * block, BF16), shape(width, rows, BF16), shape(rows, hidden, F32)],
        (*xs, *ups[:2]),
        [pltpu.VMEM((2 * SHARD, width), BF16)],
        flops=4 * rows * block * hidden,
    )


def most_down(gs, tables, x_tail, part, up_y, up_d):
    block, hidden = up_y.shape
    rows = len(gs) * SHARD
    return local_call(
        functools.partial(most_down_kernel, block, len(gs)),
        [shape(rows, 3 * block, BF16), shape(hidden, rows, BF16), shape(rows, hidden, F32)] + [shape(hidden, block, F32)] * 3,
        (*gs, *tables, x_tail, part, up_y, up_d),
        flops=10 * rows * block * hidden,
    )


def merged(upper, lower):
    return local_call(merge_kernel, [shape(*upper.shape, BF16)], (upper, lower))[0]


def last_forward(shards, ups):
    block, hidden = ups[0].shape
    rows, width = 2 * SHARD, 4 * block
    return local_call(
        functools.partial(last_forward_kernel, block),
        [shape(width, rows, BF16), shape(hidden, rows, BF16), shape(rows, hidden, F32)],
        (*shards, *ups),
        [pltpu.VMEM((rows, width), BF16)],
        flops=2 * rows * width * hidden,
    )


def exchanged(rows, cols):
    first = first_part(rows)
    a, b = (shape(first, cols, BF16), shape(rows - first, cols, BF16))
    return [a, b, a, b, shape(first, cols, F32), shape(rows - first, cols, F32)]


def last_far(shards, table, act_turned, far_sum):
    hidden, block = far_sum.shape
    return local_call(
        functools.partial(last_far_kernel, block),
        [shape(2 * SHARD, 3 * block, BF16)] + exchanged(hidden, block)[:2],
        (*shards, table, act_turned, far_sum),
        flops=4 * SHARD * block * hidden,
    )


def last_near(g, act_turned, sum_x, sum_y):
    hidden, block = sum_x.shape
    return local_call(
        functools.partial(last_near_kernel, block),
        exchanged(hidden, block)[2:],
        (g, act_turned, sum_x, sum_y),
        flops=8 * SHARD * block * hidden,
    )


def early_backward(g, downs):
    hidden, block = downs[0].shape
    rows = g.shape[0]
    return local_call(
        functools.partial(early_backward_kernel, block),
        [shape(rows, hidden, F32)],
        (g, *(downs[bits] for bits in SENT)),
        flops=6 * rows * block * hidden,
    )[0]


def most_up(gs, tables, part, slope, x_turned, act_turned, down):
    hidden, block = down.shape
    rows = len(gs) * SHARD
    got = local_call(
        functools.partial(most_up_kernel, block, len(gs)),
        [shape(block, hidden, F32)] * 4 + [shape(hidden, block, F32)],
        (*gs, *tables, part, slope, x_turned, act_turned, down),
        [pltpu.VMEM((rows, block), BF16), pltpu.VMEM((rows, hidden), BF16)],
        flops=12 * rows * block * hidden,
    )
    return got[:4], got[4]


def last_up(shards, table, g, slope, x_turned, act_turned, downs, sums, down_sum):
    hidden, block = downs[0].shape
    rows = 2 * SHARD
    return local_call(
        functools.partial(last_up_kernel, block),
        exchanged(block, hidden) + [shape(block, hidden, F32), shape(hidden, block, F32)],
        (*shards, table, g, slope, x_turned, act_turned, *downs, *sums, down_sum),
        [pltpu.VMEM((rows, block), BF16), pltpu.VMEM((rows, hidden), BF16)],
        flops=18 * rows * block * hidden,
    )


def with_near(own, near_a, near_b):
    return local_call(near_kernel, [shape(*own.shape, F32)], (own, near_a, near_b))[0]


def finish(near_sum, far_a, far_b):
    return pl.pallas_call(
        finish_kernel,
        out_shape=shape(*near_sum.shape, BF16),
        in_specs=[VMEM] * 3,
        out_specs=pl.BlockSpec(memory_space=pl.ANY),
        scratch_shapes=[pltpu.VMEM(near_sum.shape, BF16), pltpu.SemaphoreType.DMA((4,))],
        compiler_params=pltpu.CompilerParams(vmem_limit_bytes=GRANT * MIB),
        cost_estimate=pl.CostEstimate(flops=near_sum.size, bytes_accessed=10 * near_sum.size, transcendentals=0),
    )(near_sum, far_a, far_b)


def dense_shards(tokens, grad_out, expert_ids, gate_q, w_up, w_down):
    return dense_body(tokens, grad_out, expert_ids, gate_q, w_up[0], w_down[0])


def dense_body(tokens, grad_out, expert_ids, gate_q, w_up, w_down):
    devices = lax.axis_size("expert")

    def ex(value, perm):
        return lax.ppermute(value, "expert", perm)

    def dp(value, bits):
        return lax.ppermute(value, "dp", xor_perm(4, bits))

    swap = xor_perm(devices, 1)

    def ring(hops):
        return [(i, (i + 2 * hops) % devices) for i in range(devices)]

    up_mid = [(i, i + 2) for i in range(2, devices - 2)]
    down_mid = [(i, i - 2) for i in range(2, devices - 2)]

    ga, gb, tokens_here, up_here, down_here = prepare(grad_out, tokens, w_up, w_down)

    t1 = ex(tokens, ring(1))
    t3 = ex(tokens, ring(-1))
    up_x = dp(w_up, 1)
    down_y = dp(w_down, 2)
    ga1 = ex(ga, ring(1))
    ga3 = ex(ga, ring(-1))
    up_y = dp(w_up, 2)
    down_x = dp(w_down, 1)

    experts = jnp.arange(devices, dtype=jnp.int32)
    named = expert_ids.T[None, :, :] == experts[:, None, None]
    gate_table = jnp.sum(jnp.where(named, gate_q.T[None, :, :], 0), axis=1).astype(F32) * (1.0 / 65536.0)
    c0 = jnp.concatenate([gate_table, ex(gate_table, swap)], axis=1)
    c1 = ex(c0, ring(1))
    c2 = ex(c0, ring(2))
    c3 = ex(c0, ring(3))
    t0b = ex(tokens, swap)
    ga0b = ex(ga, swap)
    gb0b = ex(gb, swap)

    up_d = dp(up_x, 2)
    down_d = dp(down_y, 1)
    t2u = ex(t1, up_mid)
    t2d = ex(t3, down_mid)
    t1b = ex(t1, swap)
    t3b = ex(t3, swap)
    ga2u = ex(ga1, up_mid)
    ga2d = ex(ga3, down_mid)
    ga1b = ex(ga1, swap)
    ga3b = ex(ga3, swap)
    gb1 = ex(gb, ring(1))
    gb3 = ex(gb, ring(-1))
    gb2 = ex(gb, ring(2))
    t2 = merged(t2u, t2d)
    t2b = ex(t2, swap)
    ga2 = merged(ga2u, ga2d)
    ga2b = ex(ga2, swap)
    gb1b = ex(gb1, swap)
    gb3b = ex(gb3, swap)
    gb2b = ex(gb2, swap)

    ups = (up_here, up_x, up_y, up_d)
    downs = (down_here, down_x, down_y, down_d)
    tables = (c0, c1, c3)
    x_tail, x_turned, pre_part = early_forward((tokens_here, t0b, t1, t1b, t3, t3b), ups)
    g_ab, act_ab, slope_ab, *down_sums = most_down((ga, ga0b, ga1, ga1b, ga3, ga3b), tables, x_tail, pre_part, up_y, up_d)
    x_c, act_c, slope_c = last_forward((t2, t2b), ups)
    g_c, *down_far = last_far((ga2, ga2b), c2, act_c, down_sums[0])
    down_parts = (*down_far, *last_near(g_c, act_c, *down_sums[1:]))
    grad_part = early_backward(g_ab, downs)
    up_sums, down_sum = most_up((gb, gb0b, gb1, gb1b, gb3, gb3b), tables, grad_part, slope_ab, x_turned, act_ab, down_here)
    *up_parts, up_own, down_own = last_up((gb2, gb2b), c2, g_c, slope_c, x_c, act_c, downs, up_sums, down_sum)

    def exchange(far_a, far_b, near_a, near_b, side_a, side_b):
        far_a = dp(far_a, 1)
        far_b = dp(far_b, 2)
        near_a = dp(near_a, 1)
        near_b = dp(near_b, 2)
        side_a = (side_a + far_a.astype(F32)).astype(BF16)
        side_b = (side_b + far_b.astype(F32)).astype(BF16)
        return near_a, near_b, dp(side_a, 2), dp(side_b, 1)

    down_got = exchange(*down_parts)
    up_got = exchange(*up_parts)
    down_sum = with_near(down_own, *down_got[:2])
    dw_down = finish(down_sum, *down_got[2:])
    up_sum = with_near(up_own, *up_got[:2])
    dw_up = finish(up_sum, *up_got[2:])
    return dw_up[None], dw_down[None]


def shards(tokens, grad_out, expert_ids, gate_q, w_up, w_down):
    devices = lax.axis_size("expert")
    token_count, top_count = expert_ids.shape
    capacity = max(2, token_count * top_count * 3 // (2 * devices))
    if 2 * capacity >= token_count and devices == 8 and lax.axis_size("dp") == 4 and token_count == SHARD:
        return dense_shards(tokens, grad_out, expert_ids, gate_q, w_up, w_down)
    return sparse_shards(tokens, grad_out, expert_ids, gate_q, w_up, w_down, capacity)


def solution(mesh):
    in_specs = (
        P(("dp", "expert"), None),
        P(("dp", "expert"), None),
        P(("dp", "expert"), None),
        P(("dp", "expert"), None),
        P("expert", "dp", None),
        P("expert", None, "dp"),
    )
    out_specs = (P("expert", "dp", None), P("expert", None, "dp"))
    return jax.shard_map(shards, mesh=mesh, in_specs=in_specs, out_specs=out_specs, check_vma=False)
```

```python
import functools

import jax
import jax.numpy as jnp
from jax import lax
from jax.experimental import pallas as pl
from jax.experimental.pallas import tpu as pltpu
from jax.sharding import PartitionSpec as P


F32 = jnp.float32
BF16 = jnp.bfloat16
FIRST = (((0,), (0,)), ((), ()))
LAST = (((1,), (1,)), ((), ()))


def silu_slope(values):
    sigmoid_part = jax.nn.sigmoid(values)
    return sigmoid_part * (1.0 + values * (1.0 - sigmoid_part))


def summed_up(recv_rows, projected_grad):
    partial_value = lax.dot_general(recv_rows, projected_grad, FIRST, preferred_element_type=F32).astype(BF16)
    pieces = lax.all_to_all(partial_value[None], "dp", split_axis=1, concat_axis=0, tiled=True)
    return jnp.sum(pieces.astype(F32), axis=0, keepdims=True).astype(BF16)


def summed_down(activated, grad_rows):
    partial_value = lax.dot_general(activated, grad_rows, FIRST, preferred_element_type=F32).astype(BF16)
    pieces = lax.all_to_all(partial_value[None], "dp", split_axis=2, concat_axis=0, tiled=True)
    return jnp.sum(pieces.astype(F32), axis=0, keepdims=True).astype(BF16)


def sparse_shards(tokens, grad_out, expert_ids, gate_q, w_up, w_down, capacity):
    devices = lax.axis_size("expert")
    top_count = expert_ids.shape[1]
    model_width = tokens.shape[1]
    slot_expert = expert_ids.reshape(-1)
    onehot_table = (slot_expert[:, None] == jnp.arange(devices, dtype=jnp.int32)[None, :]).astype(jnp.int32)
    earlier = jnp.cumsum(onehot_table, axis=0) - onehot_table
    slot_rank = jnp.sum(earlier * onehot_table, axis=1)
    slot_target = slot_expert * capacity + slot_rank
    gate_values = gate_q.reshape(-1).astype(F32) * (1.0 / 65536.0)
    token_rows = jnp.repeat(tokens, top_count, axis=0)
    slot_grads = (gate_values[:, None] * jnp.repeat(grad_out, top_count, axis=0).astype(F32)).astype(BF16)
    empty_rows = jnp.zeros((devices * capacity, model_width), BF16)
    send_tokens = empty_rows.at[slot_target].set(token_rows).reshape(devices, capacity, model_width)
    grad_slots = empty_rows.at[slot_target].set(slot_grads).reshape(devices, capacity, model_width)
    up_whole = lax.all_gather(w_up, "dp", axis=1, tiled=True)[0]
    down_whole = lax.all_gather(w_down, "dp", axis=2, tiled=True)[0]
    recv_tokens = lax.all_to_all(send_tokens, "expert", split_axis=0, concat_axis=0, tiled=True)
    recv_rows = recv_tokens.reshape(-1, model_width)
    projected = jnp.dot(recv_rows, up_whole, preferred_element_type=F32)
    recv_grads = lax.all_to_all(grad_slots, "expert", split_axis=0, concat_axis=0, tiled=True)
    activated = jax.nn.silu(projected).astype(BF16)
    grad_rows = recv_grads.reshape(-1, model_width)
    act_grad = lax.dot_general(grad_rows, down_whole, LAST, preferred_element_type=F32)
    projected_grad = (act_grad * silu_slope(projected)).astype(BF16)
    return summed_up(recv_rows, projected_grad), summed_down(activated, grad_rows)


def xor_perm(count, bits):
    return [(i, i ^ bits) for i in range(count)]


MIB = 1 << 20


def pick_gate(table_ref, part, expert):
    table = table_ref[:, part * SHARD : (part + 1) * SHARD]
    mine = lax.broadcasted_iota(jnp.int32, table.shape, 0) == expert
    row = jnp.sum(jnp.where(mine, table, 0.0), axis=0, keepdims=True)
    return jnp.transpose(jnp.broadcast_to(row, (SHARD, SHARD)))


SHARD = 128


def scale_rows(gate, rows):
    wide = jnp.concatenate([gate] * (rows.shape[1] // gate.shape[1]), axis=1)
    return (wide * rows.astype(F32)).astype(BF16)


def dot_rows(left, right):
    return jnp.dot(left, right, preferred_element_type=F32)


def dot_last(left, right):
    return lax.dot_general(left, right, LAST, preferred_element_type=F32)


def first_part(rows):
    return rows // 2 + rows // 24 // 32 * 32


def owner_columns(block, bits):
    return pl.ds(pl.multiple_of((lax.axis_index("dp") ^ bits) * block, block), block)


SENT = (3, 1, 2)


def prepare_kernel(block, grad, tokens, up, down, sent, kept, tokens_copy, up_copy, down_copy):
    for place, bits in enumerate(SENT):
        sent[:, place * block : (place + 1) * block] = grad[:, owner_columns(block, bits)]
    kept[...] = grad[:, owner_columns(block, 0)]
    tokens_copy[...] = tokens[...]
    up_copy[...] = up[...]
    down_copy[...] = down[...]


def early_forward_kernel(block, shards, *refs):
    xs, ups = refs[0:shards], refs[shards : shards + 2]
    x_tail, x_turned, part = refs[shards + 2 : shards + 5]
    x = refs[shards + 5]
    for pair in range(shards // 2):
        rows = slice(pair * 2 * SHARD, (pair + 1) * 2 * SHARD)
        for half in range(2):
            for bits in range(4):
                x[half * SHARD : (half + 1) * SHARD, bits * block : (bits + 1) * block] = xs[pair * 2 + half][
                    :, owner_columns(block, bits)
                ]
        part[rows, :] = dot_rows(x[:, :block], ups[0][...]) + dot_rows(x[:, block : 2 * block], ups[1][...])
        x_tail[rows, :] = x[:, 2 * block :]
        x_turned[:, rows] = jnp.transpose(x[...])


def activate(pre):
    sig = jax.nn.sigmoid(pre)
    return (pre * sig).astype(BF16), sig * (1.0 + pre * (1.0 - sig))


def most_down_kernel(block, shards, *refs):
    gs, tables = refs[0:shards], refs[shards : shards + shards // 2]
    x_tail, part, up_y, up_d = refs[shards + shards // 2 : shards + shards // 2 + 4]
    g, act_turned, slope, *sums = refs[shards + shards // 2 + 4 :]
    expert = lax.axis_index("expert")
    for pair in range(shards // 2):
        rows = slice(pair * 2 * SHARD, (pair + 1) * 2 * SHARD)
        for half in range(2):
            own = slice((pair * 2 + half) * SHARD, (pair * 2 + half + 1) * SHARD)
            g[own, :] = scale_rows(pick_gate(tables[pair], half, expert), gs[pair * 2 + half][...])
        pre = part[rows, :] + dot_rows(x_tail[rows, :block], up_y[...]) + dot_rows(x_tail[rows, block:], up_d[...])
        act, slope[rows, :] = activate(pre)
        act_turned[:, rows] = jnp.transpose(act)
    for place in range(3):
        sums[place][...] = dot_rows(act_turned[...], g[:, place * block : (place + 1) * block])


def merge_kernel(upper, lower, out):
    out[...] = upper[...] + lower[...]


def last_forward_kernel(block, *refs):
    shards, ups = refs[0:2], refs[2:6]
    x_turned, act_turned, slope, x = refs[6:]
    for half in range(2):
        for bits in range(4):
            x[half * SHARD : (half + 1) * SHARD, bits * block : (bits + 1) * block] = shards[half][:, owner_columns(block, bits)]
    pre = dot_rows(x[:, :block], ups[0][...])
    for bits in (1, 2, 3):
        pre = pre + dot_rows(x[:, bits * block : (bits + 1) * block], ups[bits][...])
    x_turned[...] = jnp.transpose(x[...])
    act, slope[...] = activate(pre)
    act_turned[...] = jnp.transpose(act)


def last_far_kernel(block, *refs):
    shards, table, act_turned, far_sum = refs[0:2], refs[2], refs[3], refs[4]
    g, far_a, far_b = refs[5:]
    expert = lax.axis_index("expert")
    for half in range(2):
        g[half * SHARD : (half + 1) * SHARD, :] = scale_rows(pick_gate(table, half, expert), shards[half][:, :block])
    middle = first_part(act_turned.shape[0])
    total = dot_rows(act_turned[...], g[...]) + far_sum[...]
    far_a[...] = total[:middle].astype(BF16)
    far_b[...] = total[middle:].astype(BF16)


def last_near_kernel(block, *refs):
    shards, table, g_far, act_turned, sum_x, sum_y = refs[0:2], refs[2], refs[3], refs[4], refs[5], refs[6]
    g, near_a, near_b, side_a, side_b = refs[7:]
    expert = lax.axis_index("expert")
    g[:, :block] = g_far[...]
    for half in range(2):
        rows = slice(half * SHARD, (half + 1) * SHARD)
        g[rows, block:] = scale_rows(pick_gate(table, half, expert), shards[half][:, block:])
    middle = first_part(act_turned.shape[0])
    total = dot_rows(act_turned[...], g[:, block : 2 * block]) + sum_x[...]
    near_a[...] = total[:middle].astype(BF16)
    side_b[...] = total[middle:]
    total = dot_rows(act_turned[...], g[:, 2 * block :]) + sum_y[...]
    side_a[...] = total[:middle]
    near_b[...] = total[middle:].astype(BF16)


def early_backward_kernel(block, g, *refs):
    downs, part = refs[0:3], refs[3]
    for pair in range(g.shape[0] // (2 * SHARD)):
        rows = slice(pair * 2 * SHARD, (pair + 1) * 2 * SHARD)
        total = dot_last(g[rows, :block], downs[0][...])
        for place in (1, 2):
            total = total + dot_last(g[rows, place * block : (place + 1) * block], downs[place][...])
        part[rows, :] = total


def most_up_kernel(block, shards, *refs):
    gs, tables = refs[0:shards], refs[shards : shards + shards // 2]
    part, slope, x_turned, act_turned, down = refs[shards + shards // 2 : shards + shards // 2 + 5]
    sums, down_own = refs[shards + shards // 2 + 5 : shards + shards // 2 + 9], refs[shards + shards // 2 + 9]
    g, back = refs[shards + shards // 2 + 10 :]
    expert = lax.axis_index("expert")
    for pair in range(shards // 2):
        rows = slice(pair * 2 * SHARD, (pair + 1) * 2 * SHARD)
        for half in range(2):
            own = slice((pair * 2 + half) * SHARD, (pair * 2 + half + 1) * SHARD)
            g[own, :] = scale_rows(pick_gate(tables[pair], half, expert), gs[pair * 2 + half][...])
        back[rows, :] = ((part[rows, :] + dot_last(g[rows, :], down[...])) * slope[rows, :]).astype(BF16)
    for bits in range(4):
        sums[bits][...] = dot_rows(x_turned[bits * block : (bits + 1) * block, :], back[...])
    down_own[...] = dot_rows(act_turned[...], g[...])


def last_up_kernel(block, *refs):
    shards, table, g, slope, x_turned, act_turned = refs[0:2], refs[2], refs[3], refs[4], refs[5], refs[6]
    downs, sums, down_sum = refs[7:11], refs[11:15], refs[15]
    far_a, far_b, near_a, near_b, side_a, side_b, up_own, down_own = refs[16:24]
    kept, back = refs[24:]
    expert = lax.axis_index("expert")
    for half in range(2):
        gate = pick_gate(table, half, expert)
        kept[half * SHARD : (half + 1) * SHARD, :] = scale_rows(gate, shards[half][...])
    grad = dot_last(kept[...], downs[0][...])
    for place, bits in enumerate(SENT):
        grad = grad + dot_last(g[:, place * block : (place + 1) * block], downs[bits][...])
    back[...] = (grad * slope[...]).astype(BF16)
    middle = first_part(block)
    total = dot_rows(x_turned[3 * block :, :], back[...]) + sums[3][...]
    far_a[...] = total[:middle].astype(BF16)
    far_b[...] = total[middle:].astype(BF16)
    total = dot_rows(x_turned[block : 2 * block, :], back[...]) + sums[1][...]
    near_a[...] = total[:middle].astype(BF16)
    side_b[...] = total[middle:]
    total = dot_rows(x_turned[2 * block : 3 * block, :], back[...]) + sums[2][...]
    side_a[...] = total[:middle]
    near_b[...] = total[middle:].astype(BF16)
    up_own[...] = dot_rows(x_turned[:block, :], back[...]) + sums[0][...]
    down_own[...] = dot_rows(act_turned[...], kept[...]) + down_sum[...]


def finish_kernel(near_sum, far_a, far_b, out, stage, sems):
    rows = near_sum.shape[0]
    middle = first_part(rows)
    copies = []
    for far, start, end in ((far_a, 0, middle), (far_b, middle, rows)):
        step = (end - start) // 2
        for i in range(2):
            here = slice(start + i * step, start + (i + 1) * step)
            stage[here, :] = (near_sum[here, :] + far[i * step : (i + 1) * step, :].astype(F32)).astype(BF16)
            place = pl.ds(start + i * step, step)
            copies.append(pltpu.make_async_copy(stage.at[place, :], out.at[place, :], sems.at[len(copies)]))
            copies[-1].start()
    for c in copies:
        c.wait()


def near_kernel(own, near_a, near_b, out):
    middle = first_part(own.shape[0])
    out[:middle, :] = own[:middle, :] + near_a[...].astype(F32)
    out[middle:, :] = own[middle:, :] + near_b[...].astype(F32)


VMEM = pl.BlockSpec(memory_space=pltpu.VMEM)


def local_call(kernel, outs, args, scratch=(), flops=0):
    moved = sum(v.size * v.dtype.itemsize for v in (*args, *outs))
    return pl.pallas_call(
        kernel,
        out_shape=outs,
        in_specs=[VMEM] * len(args),
        out_specs=[VMEM] * len(outs),
        scratch_shapes=list(scratch),
        compiler_params=pltpu.CompilerParams(vmem_limit_bytes=GRANT * MIB),
        cost_estimate=pl.CostEstimate(flops=flops, bytes_accessed=moved, transcendentals=0),
    )(*args)


GRANT = 24


def shape(rows, cols, dtype):
    return jax.ShapeDtypeStruct((rows, cols), dtype)


def prepare(grad, tokens, up, down):
    rows, width = grad.shape
    block = width // 4
    outs = [shape(rows, 3 * block, BF16), shape(rows, block, BF16)] + [shape(*v.shape, BF16) for v in (tokens, up, down)]
    return local_call(functools.partial(prepare_kernel, block), outs, (grad, tokens, up, down))


def early_forward(xs, ups):
    block, hidden = ups[0].shape
    rows, width = len(xs) * SHARD, 4 * block
    return local_call(
        functools.partial(early_forward_kernel, block, len(xs)),
        [shape(rows, 2 * block, BF16), shape(width, rows, BF16), shape(rows, hidden, F32)],
        (*xs, *ups[:2]),
        [pltpu.VMEM((2 * SHARD, width), BF16)],
        flops=4 * rows * block * hidden,
    )


def most_down(gs, tables, x_tail, part, up_y, up_d):
    block, hidden = up_y.shape
    rows = len(gs) * SHARD
    return local_call(
        functools.partial(most_down_kernel, block, len(gs)),
        [shape(rows, 3 * block, BF16), shape(hidden, rows, BF16), shape(rows, hidden, F32)] + [shape(hidden, block, F32)] * 3,
        (*gs, *tables, x_tail, part, up_y, up_d),
        flops=10 * rows * block * hidden,
    )


def merged(upper, lower):
    return local_call(merge_kernel, [shape(*upper.shape, BF16)], (upper, lower))[0]


def last_forward(shards, ups):
    block, hidden = ups[0].shape
    rows, width = 2 * SHARD, 4 * block
    return local_call(
        functools.partial(last_forward_kernel, block),
        [shape(width, rows, BF16), shape(hidden, rows, BF16), shape(rows, hidden, F32)],
        (*shards, *ups),
        [pltpu.VMEM((rows, width), BF16)],
        flops=2 * rows * width * hidden,
    )


def exchanged(rows, cols):
    first = first_part(rows)
    a, b = (shape(first, cols, BF16), shape(rows - first, cols, BF16))
    return [a, b, a, b, shape(first, cols, F32), shape(rows - first, cols, F32)]


def last_far(shards, table, act_turned, far_sum):
    hidden, block = far_sum.shape
    return local_call(
        functools.partial(last_far_kernel, block),
        [shape(2 * SHARD, block, BF16)] + exchanged(hidden, block)[:2],
        (*shards, table, act_turned, far_sum),
        flops=4 * SHARD * block * hidden,
    )


def last_near(shards, table, g_far, act_turned, sum_x, sum_y):
    hidden, block = sum_x.shape
    return local_call(
        functools.partial(last_near_kernel, block),
        [shape(2 * SHARD, 3 * block, BF16)] + exchanged(hidden, block)[2:],
        (*shards, table, g_far, act_turned, sum_x, sum_y),
        flops=8 * SHARD * block * hidden,
    )


def early_backward(g, downs):
    hidden, block = downs[0].shape
    rows = g.shape[0]
    return local_call(
        functools.partial(early_backward_kernel, block),
        [shape(rows, hidden, F32)],
        (g, *(downs[bits] for bits in SENT)),
        flops=6 * rows * block * hidden,
    )[0]


def most_up(gs, tables, part, slope, x_turned, act_turned, down):
    hidden, block = down.shape
    rows = len(gs) * SHARD
    got = local_call(
        functools.partial(most_up_kernel, block, len(gs)),
        [shape(block, hidden, F32)] * 4 + [shape(hidden, block, F32)],
        (*gs, *tables, part, slope, x_turned, act_turned, down),
        [pltpu.VMEM((rows, block), BF16), pltpu.VMEM((rows, hidden), BF16)],
        flops=12 * rows * block * hidden,
    )
    return got[:4], got[4]


def last_up(shards, table, g, slope, x_turned, act_turned, downs, sums, down_sum):
    hidden, block = downs[0].shape
    rows = 2 * SHARD
    return local_call(
        functools.partial(last_up_kernel, block),
        exchanged(block, hidden) + [shape(block, hidden, F32), shape(hidden, block, F32)],
        (*shards, table, g, slope, x_turned, act_turned, *downs, *sums, down_sum),
        [pltpu.VMEM((rows, block), BF16), pltpu.VMEM((rows, hidden), BF16)],
        flops=18 * rows * block * hidden,
    )


def with_near(own, near_a, near_b):
    return local_call(near_kernel, [shape(*own.shape, F32)], (own, near_a, near_b))[0]


def finish(near_sum, far_a, far_b):
    return pl.pallas_call(
        finish_kernel,
        out_shape=shape(*near_sum.shape, BF16),
        in_specs=[VMEM] * 3,
        out_specs=pl.BlockSpec(memory_space=pl.ANY),
        scratch_shapes=[pltpu.VMEM(near_sum.shape, BF16), pltpu.SemaphoreType.DMA((4,))],
        compiler_params=pltpu.CompilerParams(vmem_limit_bytes=GRANT * MIB),
        cost_estimate=pl.CostEstimate(flops=near_sum.size, bytes_accessed=10 * near_sum.size, transcendentals=0),
    )(near_sum, far_a, far_b)


def dense_shards(tokens, grad_out, expert_ids, gate_q, w_up, w_down):
    return dense_body(tokens, grad_out, expert_ids, gate_q, w_up[0], w_down[0])


def dense_body(tokens, grad_out, expert_ids, gate_q, w_up, w_down):
    devices = lax.axis_size("expert")

    def ex(value, perm):
        return lax.ppermute(value, "expert", perm)

    def dp(value, bits):
        return lax.ppermute(value, "dp", xor_perm(4, bits))

    swap = xor_perm(devices, 1)

    def ring(hops):
        return [(i, (i + 2 * hops) % devices) for i in range(devices)]

    up_mid = [(i, i + 2) for i in range(2, devices - 2)]
    down_mid = [(i, i - 2) for i in range(2, devices - 2)]

    ga, gb, tokens_here, up_here, down_here = prepare(grad_out, tokens, w_up, w_down)

    t1 = ex(tokens, ring(1))
    t3 = ex(tokens, ring(-1))
    up_x = dp(w_up, 1)
    down_y = dp(w_down, 2)
    ga1 = ex(ga, ring(1))
    ga3 = ex(ga, ring(-1))
    up_y = dp(w_up, 2)
    down_x = dp(w_down, 1)

    experts = jnp.arange(devices, dtype=jnp.int32)
    named = expert_ids.T[None, :, :] == experts[:, None, None]
    gate_table = jnp.sum(jnp.where(named, gate_q.T[None, :, :], 0), axis=1).astype(F32) * (1.0 / 65536.0)
    c0 = jnp.concatenate([gate_table, ex(gate_table, swap)], axis=1)
    c1 = ex(c0, ring(1))
    c2 = ex(c0, ring(2))
    c3 = ex(c0, ring(3))
    t0b = ex(tokens, swap)
    ga0b = ex(ga, swap)
    gb0b = ex(gb, swap)

    up_d = dp(up_x, 2)
    down_d = dp(down_y, 1)
    t2u = ex(t1, up_mid)
    t2d = ex(t3, down_mid)
    t1b = ex(t1, swap)
    t3b = ex(t3, swap)
    ga2u = ex(ga1, up_mid)
    ga2d = ex(ga3, down_mid)
    ga1b = ex(ga1, swap)
    ga3b = ex(ga3, swap)
    gb1 = ex(gb, ring(1))
    gb3 = ex(gb, ring(-1))
    gb2 = ex(gb, ring(2))
    t2 = merged(t2u, t2d)
    t2b = ex(t2, swap)
    ga2 = merged(ga2u, ga2d)
    ga2b = ex(ga2, swap)
    gb1b = ex(gb1, swap)
    gb3b = ex(gb3, swap)
    gb2b = ex(gb2, swap)

    ups = (up_here, up_x, up_y, up_d)
    downs = (down_here, down_x, down_y, down_d)
    tables = (c0, c1, c3)
    x_tail, x_turned, pre_part = early_forward((tokens_here, t0b, t1, t1b, t3, t3b), ups)
    g_ab, act_ab, slope_ab, *down_sums = most_down((ga, ga0b, ga1, ga1b, ga3, ga3b), tables, x_tail, pre_part, up_y, up_d)
    x_c, act_c, slope_c = last_forward((t2, t2b), ups)
    g_far, *down_far = last_far((ga2, ga2b), c2, act_c, down_sums[0])
    g_c, *down_near = last_near((ga2, ga2b), c2, g_far, act_c, *down_sums[1:])
    down_parts = (*down_far, *down_near)
    grad_part = early_backward(g_ab, downs)
    up_sums, down_sum = most_up((gb, gb0b, gb1, gb1b, gb3, gb3b), tables, grad_part, slope_ab, x_turned, act_ab, down_here)
    *up_parts, up_own, down_own = last_up((gb2, gb2b), c2, g_c, slope_c, x_c, act_c, downs, up_sums, down_sum)

    def exchange(far_a, far_b, near_a, near_b, side_a, side_b):
        far_a = dp(far_a, 1)
        far_b = dp(far_b, 2)
        near_a = dp(near_a, 1)
        near_b = dp(near_b, 2)
        side_a = (side_a + far_a.astype(F32)).astype(BF16)
        side_b = (side_b + far_b.astype(F32)).astype(BF16)
        return near_a, near_b, dp(side_a, 2), dp(side_b, 1)

    down_got = exchange(*down_parts)
    up_got = exchange(*up_parts)
    down_sum = with_near(down_own, *down_got[:2])
    dw_down = finish(down_sum, *down_got[2:])
    up_sum = with_near(up_own, *up_got[:2])
    dw_up = finish(up_sum, *up_got[2:])
    return dw_up[None], dw_down[None]


def shards(tokens, grad_out, expert_ids, gate_q, w_up, w_down):
    devices = lax.axis_size("expert")
    token_count, top_count = expert_ids.shape
    capacity = max(2, token_count * top_count * 3 // (2 * devices))
    if 2 * capacity >= token_count and devices == 8 and lax.axis_size("dp") == 4 and token_count == SHARD:
        return dense_shards(tokens, grad_out, expert_ids, gate_q, w_up, w_down)
    return sparse_shards(tokens, grad_out, expert_ids, gate_q, w_up, w_down, capacity)


def solution(mesh):
    in_specs = (
        P(("dp", "expert"), None),
        P(("dp", "expert"), None),
        P(("dp", "expert"), None),
        P(("dp", "expert"), None),
        P("expert", "dp", None),
        P("expert", None, "dp"),
    )
    out_specs = (P("expert", "dp", None), P("expert", None, "dp"))
    return jax.shard_map(shards, mesh=mesh, in_specs=in_specs, out_specs=out_specs, check_vma=False)
```
